32 devices in a mesh: group: 4 (over x, core), dev: 8 (over z, y).
Axes of the slice: x: 2, y: 2, z: 4, core: 2. Of those that a mesh axis runs over, the one named last changes fastest.
Arguments:
- adjoint_seed: bfloat16 [64, 3, 48, 16, 128], P(('group', 'dev')), may hold values from -6 to 6
- stiffness: float32 [64, 48, 16, 128], P(('group', 'dev')), may hold values from 0.1 to 0.4
- lengths: int32 [64], P(('group', 'dev')), may hold values from 24 to 48, as said below
- conn_lower: int32 [64, 3], P(('group', 'dev')), may hold values from -1 to 7, as said below
- conn_upper: int32 [64, 3], P(('group', 'dev')), may hold values from -1 to 7, as said below
- coord_x: float32 [64, 48], P(('group', 'dev')), may hold values from 0 to 95
- coord_y: float32 [64, 16], P(('group', 'dev')), may hold values from 0 to 63
- coord_z: float32 [64, 128], P(('group', 'dev')), may hold values from 0 to 31
Outputs:
- adjoint_field: float32 [64, 3, 48, 16, 128], P(('group', 'dev'))
- lattice_grad: float32 [96, 6144], P('dev')
The draws below stay inside these ranges and needn't reach their ends.
Inputs may be any that keep to these rules, and one draw needn't show every extreme that they name: `conn_lower`: each row names, within the same cluster of 16 blocks, the device index along dev and the slot of the block whose upper face meets this block's lower face (first entry -1 for a wall, then 0 and 0), and 1 in the third entry where that face is reversed along the second grid dimension. A cluster's links form one chain through all its blocks; each link appears mirrored in conn_upper with the same orientation. `conn_upper`: likewise for the block across the upper face, whose lower face it meets. `lengths`: in every cluster some block has 48 active rows and some 48 // 2.
All inputs are finite; a program needn't handle non-finite values.
Results may differ from the reference program's by a relative error of at most 0.0003.
Values sent between devices are 32-bit elements; how exact they have to be, the bound alone decides.
No kernel may reach another device: no remote copies, remote signals or barrier semaphores. Data moves between devices by JAX's collectives and lax.ppermute only.
A program may use at most 64 MiB of HBM per device.

```python
import math
import jax
import jax.numpy as jnp
from jax import lax

BLK_DEV = 2
CX = 48
CY = 16
CZ = 128
LX = 96
LY = 64
LZ = 32
SWEEPS = 2
GBLOCKS = 16
BLOCKS = 64


def chain_links(key):
    folded = jax.random.fold_in(key, 17)
    clusters = BLOCKS // GBLOCKS
    group_keys = jax.random.split(folded, clusters)

    def one_group(group_key):
        chain_order = jax.random.permutation(jax.random.fold_in(group_key, 1), GBLOCKS).astype(jnp.int32)
        reversals = jax.random.randint(jax.random.fold_in(group_key, 2), (GBLOCKS,), 0, 2).astype(jnp.int32)
        position = jnp.zeros((GBLOCKS,), jnp.int32).at[chain_order].set(jnp.arange(GBLOCKS, dtype=jnp.int32))
        previous = chain_order[jnp.maximum(position - 1, 0)]
        following = chain_order[jnp.minimum(position + 1, GBLOCKS - 1)]
        has_previous = position > 0
        has_following = position < GBLOCKS - 1
        flip_previous = reversals[jnp.maximum(position - 1, 0)]
        flip_following = reversals[position]
        lower_links = jnp.stack([jnp.where(has_previous, previous // BLK_DEV, -1), jnp.where(has_previous, previous % BLK_DEV, 0), jnp.where(has_previous, flip_previous, 0)], axis=1)
        upper_links = jnp.stack([jnp.where(has_following, following // BLK_DEV, -1), jnp.where(has_following, following % BLK_DEV, 0), jnp.where(has_following, flip_following, 0)], axis=1)
        return (lower_links, upper_links)
    lower_links, upper_links = jax.vmap(one_group)(group_keys)
    return (lower_links.reshape(BLOCKS, 3).astype(jnp.int32), upper_links.reshape(BLOCKS, 3).astype(jnp.int32))


def draw_conn_lower(key, part):
    return chain_links(key)[0]


def draw_conn_upper(key, part):
    return chain_links(key)[1]


def draw_lengths(key, part):
    drawn = jax.random.randint(jax.random.fold_in(key, 5), (BLOCKS,), CX // 2, CX + 1).astype(jnp.int32)
    drawn = drawn.at[0::GBLOCKS].set(CX)
    drawn = drawn.at[1::GBLOCKS].set(CX // 2)
    return drawn


def levels(key, extent, cuts, low, high):
    gain = 1.0
    for dim, shards_of in cuts:
        draws = jax.random.uniform(jax.random.fold_in(jax.random.fold_in(key, 6), dim), (shards_of,), jnp.float32, low / len(cuts), high / len(cuts))
        gain = gain * jnp.repeat(jnp.exp(draws), extent[dim] // shards_of).reshape((-1,) + (1,) * (len(extent) - 1 - dim))
    return gain


def bell_draw(rng, dims, spread, bound, cuts=(), held_as=jnp.bfloat16):
    values = jax.random.normal(rng, dims, jnp.float32) * spread
    if len(cuts) > 0:
        values = levels(rng, dims, cuts, -0.22, 0.18) * values
    return jnp.clip(values, min=-bound, max=bound).astype(held_as)


def setup_inputs(seed: int = 0) -> dict:
    splits = jax.random.split(jax.random.key(seed), 9)
    return {
        "adjoint_seed": bell_draw(splits[0], (BLOCKS, 3, CX, CY, CZ), 1.0, 6.0, ((0, 32),)),
        "stiffness": jnp.clip(jnp.exp(math.log(0.4) - 1.3862944 * jax.random.uniform(splits[1], (BLOCKS, CX, CY, CZ), jnp.float32) ** levels(splits[1], (BLOCKS, CX, CY, CZ), ((0, 32),), -0.2, 0.2)), 0.1, 0.4),
        "lengths": draw_lengths(jax.random.fold_in(splits[8], 71), 0),
        "conn_lower": draw_conn_lower(jax.random.fold_in(splits[8], 71), 0),
        "conn_upper": draw_conn_upper(jax.random.fold_in(splits[8], 71), 0),
        "coord_x": jnp.clip(95.0 * jax.random.uniform(splits[5], (BLOCKS, CX), jnp.float32) ** levels(splits[5], (BLOCKS, CX), ((0, 32),), -0.2, 0.2), 0.0, 95.0),
        "coord_y": jnp.clip(63.0 * jax.random.uniform(splits[6], (BLOCKS, CY), jnp.float32) ** levels(splits[6], (BLOCKS, CY), ((0, 32),), -0.2, 0.2), 0.0, 63.0),
        "coord_z": jnp.clip(31.0 * jax.random.uniform(splits[7], (BLOCKS, CZ), jnp.float32) ** levels(splits[7], (BLOCKS, CZ), ((0, 32),), -0.2, 0.2), 0.0, 31.0),
    }


TAPS = [(shift_x, shift_y, shift_z, 1.0 / (shift_x * shift_x + shift_y * shift_y + shift_z * shift_z)) for shift_x in (-1, 0, 1) for shift_y in (-1, 0, 1) for shift_z in (-1, 0, 1) if (shift_x, shift_y, shift_z) != (0, 0, 0)]
DOMINANCE = 1.25

def stencil(padded, count_x, count_y, count_z):
    running = None
    for shift_x, shift_y, shift_z, factor in TAPS:
        window = padded[:, 1 + shift_x:1 + shift_x + count_x, 1 + shift_y:1 + shift_y + count_y, 1 + shift_z:1 + shift_z + count_z]
        running = factor * window if running is None else running + factor * window
    return running

def extend(values, lower_halo, upper_halo, length):
    zero_row = jnp.zeros_like(lower_halo)[:, None]
    joined = jnp.concatenate([lower_halo[:, None], values, zero_row], axis=1)
    joined = lax.dynamic_update_slice(joined, upper_halo[:, None], (jnp.int32(0), (length + 1).astype(jnp.int32), jnp.int32(0), jnp.int32(0)))
    return jnp.pad(joined, ((0, 0), (0, 0), (1, 1), (1, 1)))

def end_faces(values, lengths):
    lower_face = values[:, :, 0]
    upper_face = jax.vmap(lambda block_values, length: lax.dynamic_index_in_dim(block_values, (length - 1).astype(jnp.int32), axis=1, keepdims=False))(values, lengths)
    return jnp.stack([lower_face, upper_face], axis=1)

def partner_tiles(face_tiles, links, side, group_base, slots):
    partner = (group_base + jnp.maximum(links[:, 0], 0) * slots + links[:, 1]).astype(jnp.int32)
    chosen = face_tiles[partner, side]
    mirrored = chosen[..., ::-1, :]
    turned = jnp.where((links[:, 2] == 1)[:, None, None, None], mirrored, chosen)
    return jnp.where((links[:, 0] >= 0)[:, None, None, None], turned, jnp.zeros_like(turned))

def reference(adjoint_seed, stiffness, lengths, conn_lower, conn_upper, coord_x, coord_y, coord_z):
    active = (jnp.arange(CX, dtype=jnp.int32)[None, :] < lengths[:, None]).astype(jnp.float32)[:, :, None, None]
    stiff_masked = stiffness * active
    group_base = jnp.arange(BLOCKS, dtype=jnp.int32) // GBLOCKS * GBLOCKS

    def halos(values):
        face_tiles = end_faces(values, lengths)
        lower_halo = partner_tiles(face_tiles, conn_lower, 1, group_base, BLK_DEV)
        upper_halo = partner_tiles(face_tiles, conn_upper, 0, group_base, BLK_DEV)
        return (lower_halo, upper_halo)
    stiff_lower, stiff_upper = halos(stiff_masked[:, None])

    def diagonal_one(operands):
        stiff_block, lower_halo, upper_halo, length = operands
        near = stencil(extend(stiff_block[None], lower_halo, upper_halo, length), CX, CY, CZ)[0]
        return DOMINANCE * stiff_block * near
    diagonal = lax.map(diagonal_one, (stiff_masked, stiff_lower, stiff_upper, lengths))
    safe = jnp.where(active > 0, diagonal, jnp.ones_like(diagonal))
    source = adjoint_seed.astype(jnp.float32) * active[:, None]
    adjoint = source / safe[:, None]
    for sweep_index in range(SWEEPS):
        weighted = stiff_masked[:, None] * adjoint
        lower_halo, upper_halo = halos(weighted)

        def sweep_one(operands):
            values, low_tile, high_tile, length, stiff_block, source_block, safe_block = operands
            near = stencil(extend(values, low_tile, high_tile, length), CX, CY, CZ)
            return (source_block + stiff_block[None] * near) / safe_block[None]
        adjoint = lax.map(sweep_one, (weighted, lower_halo, upper_halo, lengths, stiff_masked, source, safe))

    def hat(coords, points):
        grid_points = jnp.arange(points, dtype=jnp.float32)[:, None]
        return jnp.maximum(0.0, 1.0 - jnp.abs(grid_points - coords[None, :]))

    def lattice_step(carry, operands):
        values, along_x, along_y, along_z = operands
        hat_x = hat(along_x, LX)
        hat_y = hat(along_y, LY)
        hat_z = hat(along_z, LZ)
        first = jnp.einsum('cxyz,nz->cxyn', values, hat_z, precision=lax.Precision.HIGHEST)
        second = jnp.einsum('cxyn,my->xcmn', first, hat_y, precision=lax.Precision.HIGHEST)
        second = second.reshape(CX, 3 * LY * LZ)
        return (carry + jnp.dot(hat_x, second, precision=lax.Precision.HIGHEST, preferred_element_type=jnp.float32), None)
    start = jnp.zeros((LX, 3 * LY * LZ), jnp.float32)
    lattice, unused = lax.scan(lattice_step, start, (adjoint, coord_x, coord_y, coord_z))
    scale = math.sqrt(LX * LY * LZ / (BLOCKS * CX * CY * CZ))
    return (adjoint, lattice * scale)
```

```python
import functools
import math

import jax
import jax.numpy as jnp
from jax import lax
from jax.experimental import pallas as pl
from jax.experimental.pallas import tpu as pltpu
from jax.sharding import PartitionSpec as P

LX = 96
LY = 64
LZ = 32
DOMINANCE = 1.25
PLANES = 8
STEP = 4

F32 = jnp.float32
BF16 = jnp.bfloat16
SMEM = pl.BlockSpec(memory_space=pltpu.SMEM)
VMEM = pl.BlockSpec(memory_space=pltpu.VMEM)


def params():
    return pltpu.CompilerParams(vmem_limit_bytes=60 * 1024 * 1024)


def neighbours(v, axis):
    extent = v.shape[axis]
    place = lax.broadcasted_iota(jnp.int32, v.shape, axis)
    up = jnp.where(place == 0, 0.0, pltpu.roll(v, 1, axis))
    down = jnp.where(place == extent - 1, 0.0, pltpu.roll(v, extent - 1, axis))
    return up + down


def plane_parts(v):
    along_z = neighbours(v, v.ndim - 1)
    first = v + 0.5 * along_z
    second = 0.5 * v + (1.0 / 3.0) * along_z
    beside = first + neighbours(second, v.ndim - 2)
    own = along_z + neighbours(first, v.ndim - 2)
    return beside, own


def split(v):
    high = v.astype(BF16)
    return high, (v - high.astype(F32)).astype(BF16)


def dot3(a, b, contract_b=0):
    numbers = (((1,), (contract_b,)), ((), ()))
    mul = lambda p, q: lax.dot_general(p, q, numbers, preferred_element_type=F32)
    return mul(a[0], b[0]) + (mul(a[0], b[1]) + mul(a[1], b[0]))


def pack_kernel(devs, len_ref, low_ref, up_ref, seed_ref, stiff_ref, out_ref, packet):
    slots, _, cy, cz = stiff_ref.shape
    rows = PLANES * cy
    chunk = rows // devs
    for s in range(slots):
        length = len_ref[s]
        for side in range(2):
            at = [k if side == 0 else length - 1 - k for k in range(3)]
            stiff = [stiff_ref[s, i] for i in at]
            parts = [plane_parts(v) for v in stiff]
            inner = parts[0][1] + parts[1][0]
            next_near = parts[1][1] + parts[0][0] + parts[2][0]
            scale = 1.0 / (DOMINANCE * next_near)
            planes = [stiff[0], inner]
            planes += [seed_ref[s, c, at[0]].astype(F32) for c in range(3)]
            for c in range(3):
                planes.append(plane_parts(seed_ref[s, c, at[1]].astype(F32) * scale)[0])
            for k, plane in enumerate(planes):
                packet[2 * s + side, k * cy : (k + 1) * cy] = plane
    wanted = []
    for s in range(slots):
        for side, ref in ((0, low_ref), (1, up_ref)):
            number = jnp.maximum(ref[s, 0], 0) * (2 * slots) + ref[s, 1] * 2 + (1 - side)
            wanted.append(number.astype(F32))
    row = lax.broadcasted_iota(jnp.int32, (8, cz), 0)
    note = jnp.zeros((8, cz), F32)
    for f, number in enumerate(wanted):
        note = jnp.where(row == f, number, note)
    for j in range(devs):
        for f in range(2 * slots):
            out_ref[j, f * chunk : (f + 1) * chunk] = packet[f, j * chunk : (j + 1) * chunk]
        out_ref[j, 2 * slots * chunk :] = note


def route_kernel(in_ref, out_ref):
    devs, rows, _ = out_ref.shape
    faces = 4
    chunk = rows // faces
    for e in range(devs):
        for f in range(faces):
            cell = in_ref[e, rows + f : rows + f + 1, 0:1]
            number = cell[0, 0].astype(jnp.int32)
            source = number // faces
            start = (number % faces) * chunk
            if chunk % 8 == 0:
                start = pl.multiple_of(start, 8)
            out_ref[e, f * chunk : (f + 1) * chunk] = in_ref[source, pl.ds(start, chunk)]


def main_kernel(
    per,
    dest_ref,
    len_ref,
    low_ref,
    up_ref,
    seed_ref,
    stiff_ref,
    halo_ref,
    cx_ref,
    cy_ref,
    cz_ref,
    out_ref,
    keep_ref,
    send_ref,
    pack,
    s_ext,
    w_ext,
    v_ext,
    inv_ref,
    fac_ref,
    zdone,
    xdone,
):
    slots, nx, ny, nz = stiff_ref.shape
    devs = halo_ref.shape[0]
    chunk = halo_ref.shape[1] // (2 * slots)
    zero_plane = jnp.zeros((ny, nz), F32)

    for s in range(slots):
        for side, ref in ((0, low_ref), (1, up_ref)):
            f = 2 * s + side
            wall = ref[s, 0] < 0
            turned = ref[s, 2] == 1

            def place(reverse, f=f):
                for k in range(PLANES):
                    for r in range(ny):
                        at = k * ny + r
                        to = ny - 1 - r if reverse else r
                        j, o = at // chunk, at % chunk
                        pack[f, k, to : to + 1] = halo_ref[j, f * chunk + o : f * chunk + o + 1]

            @pl.when(wall)
            def _(f=f):
                for k in range(PLANES):
                    pack[f, k] = zero_plane

            @pl.when(jnp.logical_and(jnp.logical_not(wall), turned))
            def _(place=place):
                place(True)

            @pl.when(jnp.logical_and(jnp.logical_not(wall), jnp.logical_not(turned)))
            def _(place=place):
                place(False)

    def sweep(get, finish):
        before, _ = plane_parts(get(0, 1))
        here, own = plane_parts(get(1, 1))

        def body(step, carry):
            before, here, own = carry
            i = step * STEP
            beside, mine = plane_parts(get(i + 2, STEP))
            all_beside = jnp.concatenate([before, here, beside], axis=0)
            all_own = jnp.concatenate([own, mine], axis=0)
            near = all_own[:STEP] + all_beside[:STEP] + all_beside[2:]
            finish(i, near)
            return all_beside[STEP : STEP + 1], all_beside[STEP + 1 :], all_own[STEP:]

        lax.fori_loop(0, nx // STEP, body, (before, here, own))

    for b in range(slots):
        length = len_ref[b]
        lower, upper = 2 * b, 2 * b + 1

        def fill(step, _, b=b, length=length):
            i = step * STEP
            at = i + lax.broadcasted_iota(jnp.int32, (STEP, ny, nz), 0)
            s_ext[pl.ds(i + 1, STEP)] = jnp.where(at < length, stiff_ref[b, pl.ds(i, STEP)], 0.0)
            return 0

        lax.fori_loop(0, nx // STEP, fill, 0)
        s_ext[nx + 1] = zero_plane
        s_ext[0] = pack[lower, 0]
        s_ext[length + 1] = pack[upper, 0]

        def first(i, near, b=b, length=length):
            at = i + lax.broadcasted_iota(jnp.int32, (STEP, ny, nz), 0)
            active = at < length
            stiff = jnp.where(active, stiff_ref[b, pl.ds(i, STEP)], 0.0)
            safe = jnp.where(active, DOMINANCE * stiff * near, 1.0)
            inv = jnp.where(active, 1.0 / safe, 0.0)
            fac = stiff * inv
            inv_ref[pl.ds(i, STEP)] = inv
            fac_ref[pl.ds(i, STEP)] = fac
            for c in range(3):
                w_ext[c, pl.ds(i + 1, STEP)] = seed_ref[b, c, pl.ds(i, STEP)].astype(F32) * fac

        sweep(lambda i, n: s_ext[pl.ds(i, n)], first)

        ends = ((lower, 1, 0), (upper, length, length + 1))
        for f, mine, there in ends:
            near = pack[f, 1] + plane_parts(stiff_ref[b, mine - 1])[0]
            fac = 1.0 / (DOMINANCE * near)
            for c in range(3):
                weighted = pack[f, 2 + c] * fac
                beside, own = plane_parts(weighted)
                total = own + pack[f, 5 + c] + plane_parts(w_ext[c, mine])[0]
                v_ext[c, there] = (pack[f, 2 + c] + pack[f, 0] * total) * fac
                pack[f, 5 + c] = weighted
        for c in range(3):
            w_ext[c, nx + 1] = zero_plane
        for f, mine, there in ends:
            for c in range(3):
                w_ext[c, there] = pack[f, 5 + c]
        keep_ends = [[v_ext[c, there] for c in range(3)] for f, mine, there in ends]

        for c in range(3):

            def second(i, near, b=b, c=c):
                seed = seed_ref[b, c, pl.ds(i, STEP)].astype(F32)
                stiff = stiff_ref[b, pl.ds(i, STEP)]
                v_ext[c, pl.ds(i + 1, STEP)] = (seed + stiff * near) * fac_ref[pl.ds(i, STEP)]

            sweep(lambda i, n, c=c: w_ext[c, pl.ds(i, n)], second)
            v_ext[c, nx + 1] = zero_plane
            v_ext[c, 0] = keep_ends[0][c]
            v_ext[c, length + 1] = keep_ends[1][c]

            def third(i, near, b=b, c=c):
                seed = seed_ref[b, c, pl.ds(i, STEP)].astype(F32)
                stiff = stiff_ref[b, pl.ds(i, STEP)]
                out_ref[b, c, pl.ds(i, STEP)] = (seed + stiff * near) * inv_ref[pl.ds(i, STEP)]

            sweep(lambda i, n, c=c: v_ext[c, pl.ds(i, n)], third)

    group = 16
    row = lax.broadcasted_iota(jnp.int32, (128, 3 * nz), 0)
    lane = lax.broadcasted_iota(jnp.int32, (128, 3 * nz), 1)
    same = (row // LZ) == (lane // nz)
    point = (row % LZ).astype(F32)
    for b in range(slots):
        cz = cz_ref[b : b + 1, :]
        hat_z = jnp.maximum(0.0, 1.0 - jnp.abs(point - jnp.concatenate([cz, cz, cz], axis=1)))
        hat_z = split(jnp.where(same, hat_z, 0.0))
        for x in range(0, nx, group):
            rows = [out_ref[b, c, x : x + group].reshape(group * ny, nz) for c in range(3)]
            done = dot3(split(jnp.concatenate(rows, axis=1)), hat_z, 1)
            zdone[pl.ds((b * nx + x) * ny, group * ny)] = done
        line = lax.broadcasted_iota(jnp.int32, (LX, nx), 0).astype(F32)
        hat_x = split(jnp.maximum(0.0, 1.0 - jnp.abs(line - cx_ref[b : b + 1, :])))
        for y in range(ny):
            part = zdone[pl.ds(b * nx * ny + y, nx, stride=ny), :]
            xdone[pl.ds(b * ny + y, LX, stride=slots * ny), :] = dot3(hat_x, split(part))

    depth = per * slots * ny
    row = lax.broadcasted_iota(jnp.int32, (LY * per, depth), 0).astype(F32)
    lane = lax.broadcasted_iota(jnp.int32, (LY * per, depth), 1).astype(F32)
    which = jnp.floor((row + 0.5) * (1.0 / per))
    inside = row - which * per
    owner = jnp.floor((lane + 0.5) * (1.0 / (slots * ny)))
    hat_y = jnp.maximum(0.0, 1.0 - jnp.abs(which - cy_ref[...]))
    hat_y = split(jnp.where(inside == owner, hat_y, 0.0))
    third_rows = LY // 4 * per
    pieces = keep_ref.shape[3]
    tail = lax.broadcasted_iota(jnp.int32, (third_rows, 128), 1) >= 3 * LZ

    def close(number, _):
        start = number * depth
        if depth % 8 == 0:
            start = pl.multiple_of(start, 8)
        done = dot3(hat_y, split(xdone[pl.ds(start, depth), :]))
        last = done[3 * third_rows :]
        dense = []
        for q in range(3):
            moved = pltpu.roll(last, 3 * LZ - q * LZ, 1)
            dense.append(jnp.where(tail, moved, done[q * third_rows : (q + 1) * third_rows]))
        dense = jnp.concatenate(dense, axis=0)
        size = 3 * third_rows // 8
        d, t = number // pieces, number % pieces
        for core in range(2):

            @pl.when(dest_ref[0] == core)
            def _(core=core):
                for g in range(8):
                    ref = keep_ref if g // 4 == core else send_ref
                    ref[d, g // 2 % 2, g % 2, t] = dense[g * size : (g + 1) * size]

        return 0

    lax.fori_loop(0, LX // per, close, 0)


def core_kernel(dest_ref, keep_ref, got_ref, keep_y, send_y, keep_x, send_x):
    y, x = dest_ref[2], dest_ref[1]
    keep_y[...] = keep_ref[:, y, 0] + got_ref[:, y, 0]
    send_y[...] = keep_ref[:, 1 - y, 0] + got_ref[:, 1 - y, 0]
    keep_x[...] = keep_ref[:, :, 1, x] + got_ref[:, :, 1, x]
    send_x[...] = keep_ref[:, :, 1, 1 - x] + got_ref[:, :, 1, 1 - x]


def plane_kernel(dest_ref, keep_y, got_y, keep_x, got_x, keep_0, send_0, keep_1, send_1):
    y, x = dest_ref[2], dest_ref[1]
    keep_0[...] = keep_y[:, x] + got_y[:, x]
    send_0[...] = keep_y[:, 1 - x] + got_y[:, 1 - x]
    keep_1[...] = keep_x[:, y] + got_x[:, y]
    send_1[...] = keep_x[:, 1 - y] + got_x[:, 1 - y]


def line_kernel(dest_ref, keep_0, got_0, keep_1, got_1, *outs):
    z = dest_ref[3]
    count = len(outs)
    for k, out in enumerate(outs):
        at = lax.rem(z + k, count)
        out[0] = keep_0[at] + got_0[at]
        out[1] = keep_1[at] + got_1[at]


def sum_kernel(scale, *refs):
    total = refs[0][...]
    for ref in refs[1:-1]:
        total = total + ref[...]
    refs[-1][...] = total * scale


def unpack_kernel(per, dest_ref, own, got_c, got_x, got_xc, out_ref, pieces):
    core, x = dest_ref[0], dest_ref[1]
    pieces[core, x] = own[...]
    pieces[1 - core, x] = got_c[...]
    pieces[core, 1 - x] = got_x[...]
    pieces[1 - core, 1 - x] = got_xc[...]
    count = own.shape[1]
    quarter = LY // 4
    size = 3 * quarter // 8
    lane = lax.broadcasted_iota(jnp.int32, (per, 128), 1) // LZ
    for t in range(count):

        def strip(r):
            g, at = r // size, r % size
            return pieces[g // 4, g % 2, g // 2 % 2, t, at * per : (at + 1) * per]

        for c in range(3):
            for m4 in range(LY // 4):
                tile = None
                for k in range(4):
                    m = 4 * m4 + k
                    if m < 3 * quarter:
                        value, lies = strip(m), c
                    else:
                        value, lies = strip(c * quarter + m - 3 * quarter), 3
                    shift = ((k - lies) * LZ) % 128
                    value = pltpu.roll(value, shift, 1) if shift else value
                    tile = value if tile is None else jnp.where(lane == k, value, tile)
                at = c * LY * LZ + m4 * 128
                out_ref[t * per : (t + 1) * per, at : at + 128] = tile


def on_device(groups, devs, seed, stiff, lengths, low, up, coord_x, coord_y, coord_z):
    slots, nx, ny, nz = stiff.shape
    faces = 2 * slots
    chunk = PLANES * ny // devs
    rows = faces * chunk
    mine = LX // devs
    per = 4 if mine % 4 == 0 else mine
    pieces = mine // per
    size = 3 * LY // 4 // 8 * per
    group_at = lax.axis_index("group")
    dev_at = lax.axis_index("dev")
    fast = groups == 4 and devs % 2 == 0 and size % 8 == 0
    if fast:
        dest = jnp.stack([group_at % 2, group_at // 2, dev_at % 2, dev_at // 2]).astype(jnp.int32)
    else:
        dest = jnp.zeros((4,), jnp.int32)
    shape = lambda *dims: jax.ShapeDtypeStruct(dims, F32)

    packed = pl.pallas_call(
        functools.partial(pack_kernel, devs),
        out_shape=shape(devs, rows + 8, nz),
        in_specs=[SMEM, SMEM, SMEM, VMEM, VMEM],
        out_specs=VMEM,
        scratch_shapes=[pltpu.VMEM((faces, PLANES * ny, nz), F32)],
        compiler_params=params(),
        name="pack",
    )(lengths, low, up, seed, stiff)
    spread = lax.all_to_all(packed, "dev", 0, 0)
    routed = pl.pallas_call(
        route_kernel,
        out_shape=shape(devs, rows, nz),
        in_specs=[VMEM],
        out_specs=VMEM,
        compiler_params=params(),
        name="route",
    )(spread)
    halos = lax.all_to_all(routed, "dev", 0, 0)

    ext = pltpu.VMEM((nx + 2, ny, nz), F32)
    ext3 = pltpu.VMEM((3, nx + 2, ny, nz), F32)
    plain = pltpu.VMEM((nx, ny, nz), F32)
    half = shape(devs, 2, 2, pieces, size, 128)
    adjoint, keep, send = pl.pallas_call(
        functools.partial(main_kernel, per),
        out_shape=(shape(slots, 3, nx, ny, nz), half, half),
        in_specs=[SMEM] * 4 + [VMEM] * 6,
        out_specs=(VMEM,) * 3,
        scratch_shapes=[
            pltpu.VMEM((faces, PLANES, ny, nz), F32),
            ext,
            ext3,
            ext3,
            plain,
            plain,
            pltpu.VMEM((slots * nx * ny, 128), F32),
            pltpu.VMEM((LX * slots * ny, 128), F32),
        ],
        compiler_params=params(),
        name="main",
    )(
        dest,
        lengths,
        low,
        up,
        seed,
        stiff,
        halos,
        coord_x,
        jnp.tile(coord_y.reshape(1, slots * ny), (1, per)),
        coord_z,
    )

    scale = math.sqrt(LX * LY * LZ / (groups * devs * slots * nx * ny * nz))

    def small(kernel, outs, args, scratch=()):
        return pl.pallas_call(
            kernel,
            out_shape=outs,
            in_specs=[SMEM if a is dest else VMEM for a in args],
            out_specs=jax.tree.map(lambda _: VMEM, outs),
            scratch_shapes=scratch,
            compiler_params=params(),
        )(*args)

    piece = (2, pieces, size, 128)
    if fast:
        lines = devs // 2
        body = pieces * size

        def move(value, to):
            links = []
            for g in range(groups):
                for d in range(devs):
                    c2, x2, y2, z2 = to(g % 2, g // 2, d % 2, d // 2)
                    links.append((g * devs + d, (x2 * 2 + c2) * devs + z2 * 2 + y2))
            return lax.ppermute(value, ("group", "dev"), links)

        flip_c = lambda c, x, y, z: (1 - c, x, y, z)
        flip_x = lambda c, x, y, z: (c, 1 - x, y, z)
        flip_y = lambda c, x, y, z: (c, x, 1 - y, z)
        flip_xc = lambda c, x, y, z: (1 - c, 1 - x, y, z)
        got = move(send, flip_c)
        view = (lines, 2, 2, 2, body, 128)
        part = shape(lines, 2, body, 128)
        keep_y, send_y, keep_x, send_x = small(
            core_kernel, (part,) * 4, (dest, keep.reshape(view), got.reshape(view))
        )
        got_y, got_x = move(send_y, flip_y), move(send_x, flip_x)
        part = shape(lines, body, 128)
        keep_0, send_0, keep_1, send_1 = small(
            plane_kernel, (part,) * 4, (dest, keep_y, got_y, keep_x, got_x)
        )
        got_0, got_1 = move(send_0, flip_x), move(send_1, flip_y)
        part = shape(2, body, 128)
        sums = small(line_kernel, (part,) * lines, (dest, keep_0, got_0, keep_1, got_1))
        terms = [sums[0]]
        for k in range(1, lines):
            terms.append(move(sums[k], lambda c, x, y, z, k=k: (c, x, y, (z + k) % lines)))
        own = small(functools.partial(sum_kernel, scale), part, tuple(terms))
        others = [move(own, to) for to in (flip_c, flip_x, flip_xc)]
        quarters = [v.reshape(piece) for v in (own, *others)]
    else:
        whole = jnp.stack([keep, send], axis=1).reshape(devs, -1, 128)
        owned = lax.psum_scatter(whole, "dev", scatter_dimension=0, tiled=True)
        owned = lax.psum(owned, "group") * scale
        owned = owned.reshape(2, 2, 2, pieces, size, 128)
        quarters = [owned[c, :, x] for x in range(2) for c in range(2)]
    lattice = small(
        functools.partial(unpack_kernel, per),
        shape(mine, 3 * LY * LZ),
        (dest, *quarters),
        [pltpu.VMEM((2, 2, *piece), F32)],
    )
    return adjoint, lattice


def solution(mesh):
    both = ("group", "dev")
    in_specs = (
        P(both, None, None, None, None),
        P(both, None, None, None),
        P(both),
        P(both, None),
        P(both, None),
        P(both, None),
        P(both, None),
        P(both, None),
    )
    out_specs = (P(both, None, None, None, None), P("dev", None))
    body = functools.partial(on_device, mesh.shape["group"], mesh.shape["dev"])
    return jax.shard_map(
        body, mesh=mesh, in_specs=in_specs, out_specs=out_specs, check_vma=False
    )
```

```python
import functools
import math

import jax
import jax.numpy as jnp
from jax import lax
from jax.experimental import pallas as pl
from jax.experimental.pallas import tpu as pltpu
from jax.sharding import PartitionSpec as P

LX = 96
LY = 64
LZ = 32
DOMINANCE = 1.25
PLANES = 8
STEP = 4
ENDS = 3
EDGES = 20

F32 = jnp.float32
BF16 = jnp.bfloat16
SMEM = pl.BlockSpec(memory_space=pltpu.SMEM)
VMEM = pl.BlockSpec(memory_space=pltpu.VMEM)
ANY = pl.BlockSpec(memory_space=pl.ANY)


def params(mib):
    return pltpu.CompilerParams(vmem_limit_bytes=mib * 1024 * 1024)


def neighbours(v, axis):
    extent = v.shape[axis]
    place = lax.broadcasted_iota(jnp.int32, v.shape, axis)
    up = jnp.where(place == 0, 0.0, pltpu.roll(v, 1, axis))
    down = jnp.where(place == extent - 1, 0.0, pltpu.roll(v, extent - 1, axis))
    return up + down


def plane_parts(v):
    along_z = neighbours(v, v.ndim - 1)
    first = v + 0.5 * along_z
    second = 0.5 * v + (1.0 / 3.0) * along_z
    beside = first + neighbours(second, v.ndim - 2)
    own = along_z + neighbours(first, v.ndim - 2)
    return beside, own


def padded_stencil(ref, lead, i, count):
    rows = ref.shape[-2] - 16
    planes = pl.ds(i, count + 2)
    v = ref[(*lead, planes, slice(8, 8 + rows))]
    t = ref[(*lead, planes, slice(7, 7 + rows))] + ref[(*lead, planes, slice(9, 9 + rows))]
    t_beside = t[:-2] + t[2:]
    near = t[1:-1] + (v[:-2] + v[2:])
    mixed = v[1:-1] + 0.5 * near + (1.0 / 3.0) * t_beside
    return v[1:-1], near + 0.5 * t_beside + neighbours(mixed, mixed.ndim - 1)


def split(v):
    high = v.astype(BF16)
    return high, (v - high.astype(F32)).astype(BF16)


def thrice(v, axis, data):
    high, low = split(v)
    parts = [high, low, high] if data else [high, high, low]
    return jnp.concatenate(parts, axis=axis)


def dot(a, b, contract_b=0):
    numbers = (((1,), (contract_b,)), ((), ()))
    return lax.dot_general(a, b, numbers, preferred_element_type=F32)


def pack_kernel(devs, len_ref, low_ref, up_ref, seed_ref, stiff_ref, out_ref, packet):
    slots, _, cy, cz = stiff_ref.shape
    rows = PLANES * cy
    chunk = rows // devs
    for s in range(slots):
        length = len_ref[s]
        for side in range(2):
            at = [k if side == 0 else length - 1 - k for k in range(3)]
            stiff = [stiff_ref[s, i] for i in at]
            parts = [plane_parts(v) for v in stiff]
            inner = parts[0][1] + parts[1][0]
            next_near = parts[1][1] + parts[0][0] + parts[2][0]
            scale = 1.0 / (DOMINANCE * next_near)
            planes = [stiff[0], inner]
            planes += [seed_ref[s, c, at[0]].astype(F32) for c in range(3)]
            for c in range(3):
                planes.append(plane_parts(seed_ref[s, c, at[1]].astype(F32) * scale)[0])
            for k, plane in enumerate(planes):
                packet[2 * s + side, k * cy : (k + 1) * cy] = plane
    wanted = []
    for s in range(slots):
        for side, ref in ((0, low_ref), (1, up_ref)):
            number = jnp.maximum(ref[s, 0], 0) * (2 * slots) + ref[s, 1] * 2 + (1 - side)
            wanted.append(number.astype(F32))
    row = lax.broadcasted_iota(jnp.int32, (8, cz), 0)
    note = jnp.zeros((8, cz), F32)
    for f, number in enumerate(wanted):
        note = jnp.where(row == f, number, note)
    for j in range(devs):
        for f in range(2 * slots):
            out_ref[j, f * chunk : (f + 1) * chunk] = packet[f, j * chunk : (j + 1) * chunk]
        out_ref[j, 2 * slots * chunk :] = note


def route_kernel(in_ref, out_ref):
    devs, rows, _ = out_ref.shape
    faces = 4
    chunk = rows // faces
    for e in range(devs):
        for f in range(faces):
            cell = in_ref[e, rows + f : rows + f + 1, 0:1]
            number = cell[0, 0].astype(jnp.int32)
            source = number // faces
            start = (number % faces) * chunk
            if chunk % 8 == 0:
                start = pl.multiple_of(start, 8)
            out_ref[e, f * chunk : (f + 1) * chunk] = in_ref[source, pl.ds(start, chunk)]


def inner_kernel(len_ref, seed_ref, stiff_ref, out_ref, edge_ref, s_ext, w_ext, v_ext, fac_ref, mul_ref):
    slots, nx, ny, nz = stiff_ref.shape
    last = 8 + ny
    zeros = jnp.zeros((nx + 2, 8, nz), F32)
    for ref, lead in ((s_ext, ()), *((r, (c,)) for r in (w_ext, v_ext) for c in range(3))):
        ref[(*lead, slice(None), slice(0, 8))] = zeros
        ref[(*lead, slice(None), slice(last, last + 8))] = zeros
        for i in (0, nx + 1):
            ref[(*lead, i, slice(8, last))] = jnp.zeros((ny, nz), F32)

    def loop(body):
        def step(k, _):
            body(k * STEP)
            return 0

        lax.fori_loop(0, nx // STEP, step, 0)

    for b in range(slots):
        length = len_ref[b]

        def active_at(i, length=length):
            return i + lax.broadcasted_iota(jnp.int32, (STEP, ny, nz), 0) < length

        def fill(i, b=b, active_at=active_at):
            s_ext[pl.ds(i + 1, STEP), 8:last] = jnp.where(
                active_at(i), stiff_ref[b, pl.ds(i, STEP)], 0.0
            )

        loop(fill)

        def first(i, b=b, active_at=active_at):
            stiff, near = padded_stencil(s_ext, (), i, STEP)
            active = active_at(i)
            safe = jnp.where(active, DOMINANCE * stiff * near, 1.0)
            inv = jnp.where(active, 1.0 / safe, 0.0)
            fac = stiff * inv
            fac_ref[pl.ds(i, STEP)] = fac
            mul_ref[pl.ds(i, STEP)] = stiff * fac
            for c in range(3):
                seed = seed_ref[b, c, pl.ds(i, STEP)].astype(F32)
                w_ext[c, pl.ds(i + 1, STEP), 8:last] = seed * fac
                out_ref[b, c, pl.ds(i, STEP)] = seed * inv

        loop(first)

        for c in range(3):
            for side in range(2):
                f = 2 * b + side
                for k, at in ((11 + c, 1), (14 + c, 2)):
                    row = at if side == 0 else length - 1 - at
                    edge_ref[f, k] = out_ref[b, c, row]

        for c in range(3):

            def second(i, c=c):
                here, near = padded_stencil(w_ext, (c,), i, STEP)
                v_ext[c, pl.ds(i + 1, STEP), 8:last] = here + mul_ref[pl.ds(i, STEP)] * near

            loop(second)

            def third(i, b=b, c=c):
                _, near = padded_stencil(v_ext, (c,), i, STEP)
                out_ref[b, c, pl.ds(i, STEP)] += fac_ref[pl.ds(i, STEP)] * near

            loop(third)

        for side in range(2):
            f = 2 * b + side
            at = [k if side == 0 else length - 1 - k for k in range(4)]
            stiff = [stiff_ref[b, at[k]] for k in range(2)]
            edge_ref[f, 0] = stiff[0]
            edge_ref[f, 1] = plane_parts(stiff[0])[1] + plane_parts(stiff[1])[0]
            mul_1, fac_1, fac_2 = mul_ref[at[1]], fac_ref[at[1]], fac_ref[at[2]]
            edge_ref[f, 17], edge_ref[f, 18], edge_ref[f, 19] = mul_1, fac_1, fac_2
            for c in range(3):
                edge_ref[f, 2 + c] = seed_ref[b, c, at[0]].astype(F32)
                w_1, w_2 = w_ext[c, at[1] + 1, 8:last], w_ext[c, at[2] + 1, 8:last]
                v_2, v_3 = v_ext[c, at[2] + 1, 8:last], v_ext[c, at[3] + 1, 8:last]
                beside, own = plane_parts(w_1)
                edge_ref[f, 5 + c] = beside
                edge_ref[f, 8 + c] = w_1 + mul_1 * (own + plane_parts(w_2)[0])
                beside, own = plane_parts(v_2)
                edge_ref[f, 11 + c] += fac_1 * beside
                edge_ref[f, 14 + c] += fac_2 * (own + plane_parts(v_3)[0])


def hat_along_z(coord, nz):
    row = lax.broadcasted_iota(jnp.int32, (128, 3 * nz), 0)
    lane = lax.broadcasted_iota(jnp.int32, (128, 3 * nz), 1)
    point = (row % LZ).astype(F32)
    hat = jnp.maximum(0.0, 1.0 - jnp.abs(point - jnp.concatenate([coord] * 3, axis=1)))
    return thrice(jnp.where((row // LZ) == (lane // nz), hat, 0.0), 1, False)


def lattice_kernel(len_ref, adj_ref, cx_ref, cz_ref, out_ref, zdone):
    slots, _, nx, ny, nz = adj_ref.shape
    group = 16
    for b in range(slots):
        hat_z = hat_along_z(cz_ref[b : b + 1, :], nz)
        for x in range(0, nx, group):
            rows = [adj_ref[b, c, x : x + group].reshape(group * ny, nz) for c in range(3)]
            done = dot(thrice(jnp.concatenate(rows, axis=1), 1, True), hat_z, 1)
            zdone[pl.ds((b * nx + x) * ny, group * ny)] = done
        line = lax.broadcasted_iota(jnp.int32, (LX, 3 * nx), 0).astype(F32)
        lane = lax.broadcasted_iota(jnp.int32, (LX, 3 * nx), 1)
        x = lane % nx
        hat = jnp.maximum(0.0, 1.0 - jnp.abs(line - cx_ref[b : b + 1, :]))
        hat = jnp.where(jnp.logical_and(x >= ENDS, x < len_ref[b] - ENDS), hat, 0.0)
        high, low = split(hat)
        hat_x = jnp.where(lane < 2 * nx, high.astype(F32), low.astype(F32)).astype(BF16)
        for y in range(0, ny, 2):
            part = [zdone[pl.ds(b * nx * ny + y + k, nx, stride=ny), :] for k in range(2)]
            done = dot(hat_x, thrice(jnp.concatenate(part, axis=1), 0, True))
            for k in range(2):
                at = pl.ds(b * ny + y + k, LX, stride=slots * ny)
                out_ref[at, :] = done[:, 128 * k : 128 * (k + 1)]


def outer_kernel(
    per,
    dest_ref,
    len_ref,
    low_ref,
    up_ref,
    cx_ref,
    halo_ref,
    edge_ref,
    part_ref,
    cy_ref,
    cz_ref,
    adj_in,
    adj_out,
    keep_ref,
    send_ref,
    pack,
    ends,
    zdone,
    xdone,
    sems,
):
    del adj_in
    faces, _, ny, nz = edge_ref.shape
    slots = faces // 2
    chunk = halo_ref.shape[1] // faces
    zero_plane = jnp.zeros((ny, nz), F32)

    for s in range(slots):
        for side, ref in ((0, low_ref), (1, up_ref)):
            f = 2 * s + side
            wall = ref[s, 0] < 0
            turned = ref[s, 2] == 1

            def place(reverse, f=f):
                for k in range(PLANES):
                    for r in range(ny):
                        at = k * ny + r
                        to = ny - 1 - r if reverse else r
                        j, o = at // chunk, at % chunk
                        pack[f, k, to : to + 1] = halo_ref[j, f * chunk + o : f * chunk + o + 1]

            @pl.when(wall)
            def _(f=f):
                for k in range(PLANES):
                    pack[f, k] = zero_plane

            @pl.when(jnp.logical_and(jnp.logical_not(wall), turned))
            def _(place=place):
                place(True)

            @pl.when(jnp.logical_and(jnp.logical_not(wall), jnp.logical_not(turned)))
            def _(place=place):
                place(False)

    copies = []
    for f in range(faces):
        b, side = f // 2, f % 2
        stiff, inside = edge_ref[f, 0], edge_ref[f, 1]
        beside = plane_parts(stiff)[0]
        there = 1.0 / (DOMINANCE * (pack[f, 1] + beside))
        inv = 1.0 / (DOMINANCE * stiff * (inside + plane_parts(pack[f, 0])[0]))
        fac = stiff * inv
        mul_1, fac_1, fac_2 = edge_ref[f, 17], edge_ref[f, 18], edge_ref[f, 19]
        for c in range(3):
            seed = edge_ref[f, 2 + c]
            w_n = pack[f, 2 + c] * there
            w_0 = seed * fac
            beside_n, own_n = plane_parts(w_n)
            beside_0, own_0 = plane_parts(w_0)
            v_n = w_n + pack[f, 0] * there * (own_n + pack[f, 5 + c] + beside_0)
            v_0 = w_0 + stiff * fac * (own_0 + edge_ref[f, 5 + c] + beside_n)
            v_1 = edge_ref[f, 8 + c] + mul_1 * beside_0
            beside_n = plane_parts(v_n)[0]
            beside_0, own_0 = plane_parts(v_0)
            beside_1, own_1 = plane_parts(v_1)
            rows = [
                seed * inv + fac * (own_0 + beside_1 + beside_n),
                edge_ref[f, 11 + c] + fac_1 * (own_1 + beside_0),
                edge_ref[f, 14 + c] + fac_2 * beside_1,
            ]
            for k, row in enumerate(rows):
                ends[b, c, k if side == 0 else 2 * ENDS - 1 - k] = row
            start = 0 if side == 0 else len_ref[b] - ENDS
            copy = pltpu.make_async_copy(
                ends.at[b, c, pl.ds(side * ENDS, ENDS)],
                adj_out.at[b, c, pl.ds(start, ENDS)],
                sems.at[f, c],
            )
            copy.start()
            copies.append(copy)

    eight = 8
    line = lax.broadcasted_iota(jnp.int32, (LX, 4 * eight), 0).astype(F32)
    lane = lax.broadcasted_iota(jnp.int32, (LX, 4 * eight), 1)
    for b in range(slots):
        hat_z = hat_along_z(cz_ref[b : b + 1, :], nz)
        rows = [ends[b, c].reshape(2 * ENDS * ny, nz) for c in range(3)]
        done = dot(thrice(jnp.concatenate(rows, axis=1), 1, True), hat_z, 1)
        zdone[0 : 2 * ENDS * ny] = done
        zdone[2 * ENDS * ny : eight * ny] = jnp.zeros(((eight - 2 * ENDS) * ny, 128), F32)
        coord = jnp.full((LX, 4 * eight), -4.0, F32)
        for k in range(2 * ENDS):
            at = k if k < ENDS else len_ref[b] - 2 * ENDS + k
            coord = jnp.where(lane % eight == k, cx_ref[b, at], coord)
        hat = jnp.maximum(0.0, 1.0 - jnp.abs(line - coord))
        high, low = split(hat)
        hat_x = jnp.where(lane < 2 * eight, high.astype(F32), low.astype(F32)).astype(BF16)
        for y in range(0, ny, 2):
            part = [zdone[pl.ds(y + k, eight, stride=ny), :] for k in range(2)]
            high, low = split(jnp.concatenate(part, axis=1))
            high, low = high.astype(F32), low.astype(F32)
            stack = jnp.concatenate([high, low, high, jnp.zeros_like(high)], axis=0)
            done = dot(hat_x, stack.astype(BF16))
            for k in range(2):
                at = pl.ds(b * ny + y + k, LX, stride=slots * ny)
                xdone[at, :] = done[:, 128 * k : 128 * (k + 1)]

    depth = per * slots * ny
    row = lax.broadcasted_iota(jnp.int32, (LY * per, depth), 0).astype(F32)
    lane = lax.broadcasted_iota(jnp.int32, (LY * per, depth), 1).astype(F32)
    which = jnp.floor((row + 0.5) * (1.0 / per))
    inside = row - which * per
    owner = jnp.floor((lane + 0.5) * (1.0 / (slots * ny)))
    hat_y = jnp.maximum(0.0, 1.0 - jnp.abs(which - cy_ref[...]))
    hat_y = thrice(jnp.where(inside == owner, hat_y, 0.0), 1, False)
    third_rows = LY // 4 * per
    pieces = keep_ref.shape[3]
    size = 3 * third_rows // 8
    tail = lax.broadcasted_iota(jnp.int32, (third_rows, 128), 1) >= 3 * LZ

    def close(pair, _):
        terms = []
        for k in range(2):
            start = (2 * pair + k) * depth
            if depth % 8 == 0:
                start = pl.multiple_of(start, 8)
            terms.append(part_ref[pl.ds(start, depth), :] + xdone[pl.ds(start, depth), :])
        both = dot(hat_y, thrice(jnp.concatenate(terms, axis=1), 0, True))
        for k in range(2):
            done = both[:, 128 * k : 128 * (k + 1)]
            tops = done[3 * third_rows :]
            dense = []
            for q in range(3):
                moved = pltpu.roll(tops, 3 * LZ - q * LZ, 1)
                dense.append(jnp.where(tail, moved, done[q * third_rows : (q + 1) * third_rows]))
            dense = jnp.concatenate(dense, axis=0)
            number = 2 * pair + k
            d, t = number // pieces, number % pieces
            for core in range(2):

                @pl.when(dest_ref[0] == core)
                def _(core=core, dense=dense, d=d, t=t):
                    for g in range(8):
                        ref = keep_ref if g // 4 == core else send_ref
                        ref[d, g // 2 % 2, g % 2, t] = dense[g * size : (g + 1) * size]

        return 0

    lax.fori_loop(0, LX // per // 2, close, 0)
    for copy in copies:
        copy.wait()


def core_kernel(dest_ref, keep_ref, got_ref, keep_y, send_y, keep_x, send_x):
    y, x = dest_ref[2], dest_ref[1]
    keep_y[...] = keep_ref[:, y, 0] + got_ref[:, y, 0]
    send_y[...] = keep_ref[:, 1 - y, 0] + got_ref[:, 1 - y, 0]
    keep_x[...] = keep_ref[:, :, 1, x] + got_ref[:, :, 1, x]
    send_x[...] = keep_ref[:, :, 1, 1 - x] + got_ref[:, :, 1, 1 - x]


def plane_kernel(dest_ref, keep_y, got_y, keep_x, got_x, keep_0, send_0, keep_1, send_1):
    y, x = dest_ref[2], dest_ref[1]
    keep_0[...] = keep_y[:, x] + got_y[:, x]
    send_0[...] = keep_y[:, 1 - x] + got_y[:, 1 - x]
    keep_1[...] = keep_x[:, y] + got_x[:, y]
    send_1[...] = keep_x[:, 1 - y] + got_x[:, 1 - y]


def line_kernel(dest_ref, keep_0, got_0, keep_1, got_1, *outs):
    z = dest_ref[3]
    count = len(outs)
    for k, out in enumerate(outs):
        at = lax.rem(z + k, count)
        out[0] = keep_0[at] + got_0[at]
        out[1] = keep_1[at] + got_1[at]


def sum_kernel(scale, *refs):
    total = refs[0][...]
    for ref in refs[1:-1]:
        total = total + ref[...]
    refs[-1][...] = total * scale


def unpack_kernel(per, dest_ref, own, got_c, got_x, got_xc, out_ref, pieces):
    core, x = dest_ref[0], dest_ref[1]
    pieces[core, x] = own[...]
    pieces[1 - core, x] = got_c[...]
    pieces[core, 1 - x] = got_x[...]
    pieces[1 - core, 1 - x] = got_xc[...]
    count = own.shape[1]
    quarter = LY // 4
    size = 3 * quarter // 8
    lane = lax.broadcasted_iota(jnp.int32, (per, 128), 1) // LZ
    for t in range(count):

        def strip(r):
            g, at = r // size, r % size
            return pieces[g // 4, g % 2, g // 2 % 2, t, at * per : (at + 1) * per]

        for c in range(3):
            for m4 in range(LY // 4):
                tile = None
                for k in range(4):
                    m = 4 * m4 + k
                    if m < 3 * quarter:
                        value, lies = strip(m), c
                    else:
                        value, lies = strip(c * quarter + m - 3 * quarter), 3
                    shift = ((k - lies) * LZ) % 128
                    value = pltpu.roll(value, shift, 1) if shift else value
                    tile = value if tile is None else jnp.where(lane == k, value, tile)
                at = c * LY * LZ + m4 * 128
                out_ref[t * per : (t + 1) * per, at : at + 128] = tile


def on_device(groups, devs, seed, stiff, lengths, low, up, coord_x, coord_y, coord_z):
    slots, nx, ny, nz = stiff.shape
    faces = 2 * slots
    chunk = PLANES * ny // devs
    rows = faces * chunk
    mine = LX // devs
    per = 4 if mine % 4 == 0 else mine
    pieces = mine // per
    size = 3 * LY // 4 // 8 * per
    group_at = lax.axis_index("group")
    dev_at = lax.axis_index("dev")
    fast = groups == 4 and devs % 2 == 0 and size % 8 == 0
    if fast:
        dest = jnp.stack([group_at % 2, group_at // 2, dev_at % 2, dev_at // 2]).astype(jnp.int32)
    else:
        dest = jnp.zeros((4,), jnp.int32)
    shape = lambda *dims: jax.ShapeDtypeStruct(dims, F32)

    packed = pl.pallas_call(
        functools.partial(pack_kernel, devs),
        out_shape=shape(devs, rows + 8, nz),
        in_specs=[SMEM, SMEM, SMEM, VMEM, VMEM],
        out_specs=VMEM,
        scratch_shapes=[pltpu.VMEM((faces, PLANES * ny, nz), F32)],
        compiler_params=params(8),
        name="pack",
    )(lengths, low, up, seed, stiff)
    spread = lax.all_to_all(packed, "dev", 0, 0)
    ext = (nx + 2, ny + 16, nz)
    plain = pltpu.VMEM((nx, ny, nz), F32)
    early, edges = pl.pallas_call(
        inner_kernel,
        out_shape=(shape(slots, 3, nx, ny, nz), shape(faces, EDGES, ny, nz)),
        in_specs=[SMEM, VMEM, VMEM],
        out_specs=(VMEM, VMEM),
        scratch_shapes=[
            pltpu.VMEM(ext, F32),
            pltpu.VMEM((3, *ext), F32),
            pltpu.VMEM((3, *ext), F32),
            plain,
            plain,
        ],
        compiler_params=params(24),
        cost_estimate=pl.CostEstimate(flops=4 * 10**8, bytes_accessed=2 * 10**7, transcendentals=0),
        name="inner",
    )(lengths, seed, stiff)
    routed = pl.pallas_call(
        route_kernel,
        out_shape=shape(devs, rows, nz),
        in_specs=[VMEM],
        out_specs=VMEM,
        compiler_params=params(4),
        name="route",
    )(spread)
    early, routed = lax.optimization_barrier((early, routed))
    halos = lax.all_to_all(routed, "dev", 0, 0)
    inside = pl.pallas_call(
        lattice_kernel,
        out_shape=shape(LX * slots * ny, 128),
        in_specs=[SMEM, VMEM, VMEM, VMEM],
        out_specs=VMEM,
        scratch_shapes=[pltpu.VMEM((slots * nx * ny, 128), F32)],
        compiler_params=params(16),
        cost_estimate=pl.CostEstimate(flops=2 * 10**9, bytes_accessed=2 * 10**7, transcendentals=0),
        name="lattice",
    )(lengths, early, jnp.tile(coord_x, (1, 3)), coord_z)

    half = shape(devs, 2, 2, pieces, size, 128)
    adjoint, keep, send = pl.pallas_call(
        functools.partial(outer_kernel, per),
        out_shape=(shape(slots, 3, nx, ny, nz), half, half),
        in_specs=[SMEM] * 5 + [VMEM] * 5 + [ANY],
        out_specs=(ANY, VMEM, VMEM),
        scratch_shapes=[
            pltpu.VMEM((faces, PLANES, ny, nz), F32),
            pltpu.VMEM((slots, 3, 2 * ENDS, ny, nz), F32),
            pltpu.VMEM((8 * ny, 128), F32),
            pltpu.VMEM((LX * slots * ny, 128), F32),
            pltpu.SemaphoreType.DMA((faces, 3)),
        ],
        input_output_aliases={10: 0},
        compiler_params=params(16),
        name="outer",
    )(
        dest,
        lengths,
        low,
        up,
        coord_x,
        halos,
        edges,
        inside,
        jnp.tile(coord_y.reshape(1, slots * ny), (1, per)),
        coord_z,
        early,
    )

    scale = math.sqrt(LX * LY * LZ / (groups * devs * slots * nx * ny * nz))

    def small(kernel, outs, args, scratch=()):
        return pl.pallas_call(
            kernel,
            out_shape=outs,
            in_specs=[SMEM if a is dest else VMEM for a in args],
            out_specs=jax.tree.map(lambda _: VMEM, outs),
            scratch_shapes=scratch,
            compiler_params=params(8),
        )(*args)

    piece = (2, pieces, size, 128)
    if fast:
        lines = devs // 2
        body = pieces * size

        def move(value, to):
            links = []
            for g in range(groups):
                for d in range(devs):
                    c2, x2, y2, z2 = to(g % 2, g // 2, d % 2, d // 2)
                    links.append((g * devs + d, (x2 * 2 + c2) * devs + z2 * 2 + y2))
            return lax.ppermute(value, ("group", "dev"), links)

        flip_c = lambda c, x, y, z: (1 - c, x, y, z)
        flip_x = lambda c, x, y, z: (c, 1 - x, y, z)
        flip_y = lambda c, x, y, z: (c, x, 1 - y, z)
        flip_xc = lambda c, x, y, z: (1 - c, 1 - x, y, z)
        got = move(send, flip_c)
        view = (lines, 2, 2, 2, body, 128)
        part = shape(lines, 2, body, 128)
        keep_y, send_y, keep_x, send_x = small(
            core_kernel, (part,) * 4, (dest, keep.reshape(view), got.reshape(view))
        )
        got_y, got_x = move(send_y, flip_y), move(send_x, flip_x)
        part = shape(lines, body, 128)
        keep_0, send_0, keep_1, send_1 = small(
            plane_kernel, (part,) * 4, (dest, keep_y, got_y, keep_x, got_x)
        )
        got_0, got_1 = move(send_0, flip_x), move(send_1, flip_y)
        part = shape(2, body, 128)
        sums = small(line_kernel, (part,) * lines, (dest, keep_0, got_0, keep_1, got_1))
        terms = [sums[0]]
        for k in range(1, lines):
            terms.append(move(sums[k], lambda c, x, y, z, k=k: (c, x, y, (z + k) % lines)))
        own = small(functools.partial(sum_kernel, scale), part, tuple(terms))
        others = [move(own, to) for to in (flip_c, flip_x, flip_xc)]
        quarters = [v.reshape(piece) for v in (own, *others)]
    else:
        whole = jnp.stack([keep, send], axis=1).reshape(devs, -1, 128)
        owned = lax.psum_scatter(whole, "dev", scatter_dimension=0, tiled=True)
        owned = lax.psum(owned, "group") * scale
        owned = owned.reshape(2, 2, 2, pieces, size, 128)
        quarters = [owned[c, :, x] for x in range(2) for c in range(2)]
    lattice = small(
        functools.partial(unpack_kernel, per),
        shape(mine, 3 * LY * LZ),
        (dest, *quarters),
        [pltpu.VMEM((2, 2, *piece), F32)],
    )
    return adjoint, lattice


def solution(mesh):
    both = ("group", "dev")
    in_specs = (
        P(both, None, None, None, None),
        P(both, None, None, None),
        P(both),
        P(both, None),
        P(both, None),
        P(both, None),
        P(both, None),
        P(both, None),
    )
    out_specs = (P(both, None, None, None, None), P("dev", None))
    body = functools.partial(on_device, mesh.shape["group"], mesh.shape["dev"])
    return jax.shard_map(
        body, mesh=mesh, in_specs=in_specs, out_specs=out_specs, check_vma=False
    )
```

```python
import functools
import math

import jax
import jax.numpy as jnp
from jax import lax
from jax.experimental import pallas as pl
from jax.experimental.pallas import tpu as pltpu
from jax.sharding import PartitionSpec as P

LX = 96
LY = 64
LZ = 32
DOMINANCE = 1.25
PLANES = 8
STEP = 4
ENDS = 3
EDGES = 20

F32 = jnp.float32
BF16 = jnp.bfloat16
SMEM = pl.BlockSpec(memory_space=pltpu.SMEM)
VMEM = pl.BlockSpec(memory_space=pltpu.VMEM)
ANY = pl.BlockSpec(memory_space=pl.ANY)
HBM = pl.BlockSpec(memory_space=pltpu.HBM)


def params(mib):
    return pltpu.CompilerParams(vmem_limit_bytes=mib * 1024 * 1024)


def neighbours(v, axis):
    extent = v.shape[axis]
    place = lax.broadcasted_iota(jnp.int32, v.shape, axis)
    up = jnp.where(place == 0, 0.0, pltpu.roll(v, 1, axis))
    down = jnp.where(place == extent - 1, 0.0, pltpu.roll(v, extent - 1, axis))
    return up + down


def plane_parts(v):
    along_z = neighbours(v, v.ndim - 1)
    first = v + 0.5 * along_z
    second = 0.5 * v + (1.0 / 3.0) * along_z
    beside = first + neighbours(second, v.ndim - 2)
    own = along_z + neighbours(first, v.ndim - 2)
    return beside, own


def padded_stencil(ref, lead, i, count):
    rows = ref.shape[-2] - 16
    planes = pl.ds(i, count + 2)
    v = ref[(*lead, planes, slice(8, 8 + rows))]
    t = ref[(*lead, planes, slice(7, 7 + rows))] + ref[(*lead, planes, slice(9, 9 + rows))]
    t_beside = t[:-2] + t[2:]
    near = t[1:-1] + (v[:-2] + v[2:])
    mixed = v[1:-1] + 0.5 * near + (1.0 / 3.0) * t_beside
    return v[1:-1], near + 0.5 * t_beside + neighbours(mixed, mixed.ndim - 1)


def split(v):
    high = v.astype(BF16)
    return high, (v - high.astype(F32)).astype(BF16)


def thrice(v, axis, data):
    high, low = split(v)
    parts = [high, low, high] if data else [high, high, low]
    return jnp.concatenate(parts, axis=axis)


def dot(a, b, contract_b=0):
    numbers = (((1,), (contract_b,)), ((), ()))
    return lax.dot_general(a, b, numbers, preferred_element_type=F32)


def pack_kernel(devs, slots, nx, ny, nz, len_in, low_in, up_in, seed_in, stiff_in, out_ref, *scratch):
    len_ref, low_ref, up_ref, seed_ref, stiff_ref, packet, sems = scratch
    rows = PLANES * ny
    chunk = rows // devs
    small = []
    for k, (src, dst) in enumerate(((len_in, len_ref), (low_in, low_ref), (up_in, up_ref))):
        small.append(pltpu.make_async_copy(src, dst, sems.at[0, k]))
        small[k].start()
    copies = {}

    def fetch(s, side):
        f = 2 * s + side
        start = [0, 0] if side == 0 else [len_ref[s] - 3, len_ref[s] - 2]
        copies[f] = (
            pltpu.make_async_copy(stiff_in.at[s, pl.ds(start[0], 3)], stiff_ref.at[f], sems.at[1, f]),
            pltpu.make_async_copy(seed_in.at[s, :, pl.ds(start[1], 2)], seed_ref.at[f], sems.at[2, f]),
        )
        for copy in copies[f]:
            copy.start()

    for s in range(slots):
        fetch(s, 0)
    small[0].wait()
    for s in range(slots):
        fetch(s, 1)
    small[1].wait()
    small[2].wait()
    wanted = []
    for s in range(slots):
        for side, ref in ((0, low_ref), (1, up_ref)):
            number = jnp.maximum(ref[s, 0], 0) * (2 * slots) + ref[s, 1] * 2 + (1 - side)
            wanted.append(number.astype(F32))
    row = lax.broadcasted_iota(jnp.int32, (8, nz), 0)
    note = jnp.zeros((8, nz), F32)
    for f, number in enumerate(wanted):
        note = jnp.where(row == f, number, note)
    for f in (0, 2, 1, 3):
        side = f % 2
        for copy in copies[f]:
            copy.wait()
        stiff = [stiff_ref[f, k if side == 0 else 2 - k] for k in range(3)]
        parts = [plane_parts(v) for v in stiff]
        inner = parts[0][1] + parts[1][0]
        next_near = parts[1][1] + parts[0][0] + parts[2][0]
        scale = 1.0 / (DOMINANCE * next_near)
        planes = [stiff[0], inner]
        planes += [seed_ref[f, c, side].astype(F32) for c in range(3)]
        for c in range(3):
            planes.append(plane_parts(seed_ref[f, c, 1 - side].astype(F32) * scale)[0])
        for k, plane in enumerate(planes):
            packet[f, k * ny : (k + 1) * ny] = plane
    for j in range(devs):
        for f in range(2 * slots):
            out_ref[j, f * chunk : (f + 1) * chunk] = packet[f, j * chunk : (j + 1) * chunk]
        out_ref[j, 2 * slots * chunk :] = note


def route_kernel(in_ref, out_ref):
    devs, rows, _ = out_ref.shape
    faces = 4
    chunk = rows // faces
    for e in range(devs):
        for f in range(faces):
            cell = in_ref[e, rows + f : rows + f + 1, 0:1]
            number = cell[0, 0].astype(jnp.int32)
            source = number // faces
            start = (number % faces) * chunk
            if chunk % 8 == 0:
                start = pl.multiple_of(start, 8)
            out_ref[e, f * chunk : (f + 1) * chunk] = in_ref[source, pl.ds(start, chunk)]


def hat_along_z(coord, nz):
    row = lax.broadcasted_iota(jnp.int32, (128, 3 * nz), 0)
    lane = lax.broadcasted_iota(jnp.int32, (128, 3 * nz), 1)
    point = (row % LZ).astype(F32)
    hat = jnp.maximum(0.0, 1.0 - jnp.abs(point - jnp.concatenate([coord] * 3, axis=1)))
    return thrice(jnp.where((row // LZ) == (lane // nz), hat, 0.0), 1, False)


def block_kernel(b, len_ref, seed_in, stiff_in, cx_ref, cz_ref, *refs):
    adj_out, edge_ref, part_ref, s_ext, w_ext, v_ext, fac_ref, mul_ref, adj, seeds, zdone, sems = refs[-12:]
    nx, ny, nz = fac_ref.shape
    last = 8 + ny
    length = len_ref[b]
    loads = (
        pltpu.make_async_copy(
            stiff_in.at[b], s_ext.at[pl.ds(1, nx), pl.ds(8, ny)], sems.at[0]
        ),
        pltpu.make_async_copy(seed_in.at[b], seeds, sems.at[1]),
    )
    for copy in loads:
        copy.start()
    zeros = jnp.zeros((nx + 2, 8, nz), F32)
    plane = jnp.zeros((ny, nz), F32)
    for ref, lead in ((s_ext, ()), *((r, (c,)) for r in (w_ext, v_ext) for c in range(3))):
        ref[(*lead, slice(None), slice(0, 8))] = zeros
        ref[(*lead, slice(None), slice(last, last + 8))] = zeros
        for i in (0, nx + 1):
            ref[(*lead, i, slice(8, last))] = plane
    hat_z = hat_along_z(cz_ref[b : b + 1, :], nz)
    line = lax.broadcasted_iota(jnp.int32, (LX, 3 * nx), 0).astype(F32)
    lane = lax.broadcasted_iota(jnp.int32, (LX, 3 * nx), 1)
    x = lane % nx
    coord = jnp.concatenate([cx_ref[b : b + 1, :]] * 3, axis=1)
    hat = jnp.maximum(0.0, 1.0 - jnp.abs(line - coord))
    hat = jnp.where(jnp.logical_and(x >= ENDS, x < length - ENDS), hat, 0.0)
    high, low = split(hat)
    hat_x = jnp.where(lane < 2 * nx, high.astype(F32), low.astype(F32)).astype(BF16)
    for copy in loads:
        copy.wait()

    def clear(i, _):
        s_ext[i + 1, 8:last] = plane
        return 0

    lax.fori_loop(length, nx, clear, 0)

    def loop(body):
        def step(k, _):
            body(k * STEP)
            return 0

        lax.fori_loop(0, nx // STEP, step, 0)

    def first(i):
        stiff, near = padded_stencil(s_ext, (), i, STEP)
        active = i + lax.broadcasted_iota(jnp.int32, (STEP, ny, nz), 0) < length
        safe = jnp.where(active, DOMINANCE * stiff * near, 1.0)
        inv = jnp.where(active, 1.0 / safe, 0.0)
        fac = stiff * inv
        fac_ref[pl.ds(i, STEP)] = fac
        mul_ref[pl.ds(i, STEP)] = stiff * fac
        for c in range(3):
            seed = seeds[c, pl.ds(i, STEP)].astype(F32)
            w_ext[c, pl.ds(i + 1, STEP), 8:last] = seed * fac
            adj[c, pl.ds(i, STEP)] = seed * inv

    loop(first)

    at = [[k if side == 0 else length - 1 - k for k in range(4)] for side in range(2)]
    for f in range(2):
        for c in range(3):
            edge_ref[f, 11 + c] = adj[c, at[f][1]]
            edge_ref[f, 14 + c] = adj[c, at[f][2]]

    def second(i):
        mul = mul_ref[pl.ds(i, STEP)]
        for c in range(3):
            here, near = padded_stencil(w_ext, (c,), i, STEP)
            v_ext[c, pl.ds(i + 1, STEP), 8:last] = here + mul * near

    loop(second)

    def third(i):
        fac = fac_ref[pl.ds(i, STEP)]
        for c in range(3):
            _, near = padded_stencil(v_ext, (c,), i, STEP)
            adj[c, pl.ds(i, STEP)] += fac * near

    loop(third)
    store = pltpu.make_async_copy(adj, adj_out.at[b], sems.at[2])
    store.start()

    def parts(ref, *lead):
        v = ref[(*lead, slice(8, last))]
        t = ref[(*lead, slice(7, last - 1))] + ref[(*lead, slice(9, last + 1))]
        own = t + neighbours(v + 0.5 * t, 1)
        return v + 0.5 * t + neighbours(0.5 * v + (1.0 / 3.0) * t, 1), own

    for f in range(2):
        edge_ref[f, 0] = s_ext[at[f][0] + 1, 8:last]
        edge_ref[f, 1] = parts(s_ext, at[f][0] + 1)[1] + parts(s_ext, at[f][1] + 1)[0]
        mul_1, fac_1, fac_2 = mul_ref[at[f][1]], fac_ref[at[f][1]], fac_ref[at[f][2]]
        edge_ref[f, 17], edge_ref[f, 18], edge_ref[f, 19] = mul_1, fac_1, fac_2
        for c in range(3):
            edge_ref[f, 2 + c] = seeds[c, at[f][0]].astype(F32)
            beside, own = parts(w_ext, c, at[f][1] + 1)
            edge_ref[f, 5 + c] = beside
            own = own + parts(w_ext, c, at[f][2] + 1)[0]
            edge_ref[f, 8 + c] = w_ext[c, at[f][1] + 1, 8:last] + mul_1 * own
            beside, own = parts(v_ext, c, at[f][2] + 1)
            edge_ref[f, 11 + c] += fac_1 * beside
            edge_ref[f, 14 + c] += fac_2 * (own + parts(v_ext, c, at[f][3] + 1)[0])

    group = 16
    pitch = ny + 1
    for x in range(0, nx, group):
        rows = [adj[c, x : x + group].reshape(group * ny, nz) for c in range(3)]
        done = dot(thrice(jnp.concatenate(rows, axis=1), 1, True), hat_z, 1)
        for k in range(group):
            zdone[(x + k) * pitch : (x + k) * pitch + ny] = done[k * ny : (k + 1) * ny]
    for y in range(0, ny, 2):
        part = [zdone[pl.ds(y + k, nx, stride=pitch), :] for k in range(2)]
        done = dot(hat_x, thrice(jnp.concatenate(part, axis=1), 0, True))
        for k in range(2):
            part_ref[pl.ds(y + k, LX, stride=pitch), :] = done[:, 128 * k : 128 * (k + 1)]
    store.wait()


def outer_kernel(
    per,
    dest_ref,
    len_ref,
    low_ref,
    up_ref,
    cx_ref,
    halo_ref,
    edge_0,
    edge_1,
    part_0,
    part_1,
    cy_ref,
    cz_ref,
    adj_in,
    adj_out,
    keep_ref,
    send_ref,
    pack,
    ends,
    zdone,
    xdone,
    sems,
):
    del adj_in
    slots = 2
    faces = 2 * slots
    _, _, ny, nz = edge_0.shape
    pitch = ny + 1
    chunk = halo_ref.shape[1] // faces
    zero_plane = jnp.zeros((ny, nz), F32)

    for s in range(slots):
        for side, ref in ((0, low_ref), (1, up_ref)):
            f = 2 * s + side
            wall = ref[s, 0] < 0
            turned = ref[s, 2] == 1

            def place(reverse, f=f):
                for k in range(PLANES):
                    for r in range(ny):
                        at = k * ny + r
                        to = ny - 1 - r if reverse else r
                        j, o = at // chunk, at % chunk
                        pack[f, k, to : to + 1] = halo_ref[j, f * chunk + o : f * chunk + o + 1]

            @pl.when(wall)
            def _(f=f):
                for k in range(PLANES):
                    pack[f, k] = zero_plane

            @pl.when(jnp.logical_and(jnp.logical_not(wall), turned))
            def _(place=place):
                place(True)

            @pl.when(jnp.logical_and(jnp.logical_not(wall), jnp.logical_not(turned)))
            def _(place=place):
                place(False)

    copies = []
    for f in range(faces):
        b, side = f // 2, f % 2
        edge = (edge_0, edge_1)[b].at[side]
        stiff, inside = edge[0], edge[1]
        beside = plane_parts(stiff)[0]
        there = 1.0 / (DOMINANCE * (pack[f, 1] + beside))
        inv = 1.0 / (DOMINANCE * stiff * (inside + plane_parts(pack[f, 0])[0]))
        fac = stiff * inv
        mul_1, fac_1, fac_2 = edge[17], edge[18], edge[19]
        for c in range(3):
            seed = edge[2 + c]
            w_n = pack[f, 2 + c] * there
            w_0 = seed * fac
            beside_n, own_n = plane_parts(w_n)
            beside_0, own_0 = plane_parts(w_0)
            v_n = w_n + pack[f, 0] * there * (own_n + pack[f, 5 + c] + beside_0)
            v_0 = w_0 + stiff * fac * (own_0 + edge[5 + c] + beside_n)
            v_1 = edge[8 + c] + mul_1 * beside_0
            beside_n = plane_parts(v_n)[0]
            beside_0, own_0 = plane_parts(v_0)
            beside_1, own_1 = plane_parts(v_1)
            rows = [
                seed * inv + fac * (own_0 + beside_1 + beside_n),
                edge[11 + c] + fac_1 * (own_1 + beside_0),
                edge[14 + c] + fac_2 * beside_1,
            ]
            for k, row in enumerate(rows):
                ends[b, c, k if side == 0 else 2 * ENDS - 1 - k] = row
            start = 0 if side == 0 else len_ref[b] - ENDS
            copy = pltpu.make_async_copy(
                ends.at[b, c, pl.ds(side * ENDS, ENDS)],
                adj_out.at[b, c, pl.ds(start, ENDS)],
                sems.at[f, c],
            )
            copy.start()
            copies.append(copy)

    eight = 8
    line = lax.broadcasted_iota(jnp.int32, (LX, 4 * eight), 0).astype(F32)
    lane = lax.broadcasted_iota(jnp.int32, (LX, 4 * eight), 1)
    for b in range(slots):
        hat_z = hat_along_z(cz_ref[b : b + 1, :], nz)
        rows = [ends[b, c].reshape(2 * ENDS * ny, nz) for c in range(3)]
        done = dot(thrice(jnp.concatenate(rows, axis=1), 1, True), hat_z, 1)
        for k in range(eight):
            rows = done[k * ny : (k + 1) * ny] if k < 2 * ENDS else jnp.zeros((ny, 128), F32)
            zdone[k * pitch : k * pitch + ny] = rows
        coord = jnp.full((LX, 4 * eight), -4.0, F32)
        for k in range(2 * ENDS):
            at = k if k < ENDS else len_ref[b] - 2 * ENDS + k
            coord = jnp.where(lane % eight == k, cx_ref[b, at], coord)
        hat = jnp.maximum(0.0, 1.0 - jnp.abs(line - coord))
        high, low = split(hat)
        hat_x = jnp.where(lane < 2 * eight, high.astype(F32), low.astype(F32)).astype(BF16)
        for y in range(0, ny, 2):
            part = [zdone[pl.ds(y + k, eight, stride=pitch), :] for k in range(2)]
            high, low = split(jnp.concatenate(part, axis=1))
            high, low = high.astype(F32), low.astype(F32)
            stack = jnp.concatenate([high, low, high, jnp.zeros_like(high)], axis=0)
            done = dot(hat_x, stack.astype(BF16))
            for k in range(2):
                xdone[b, pl.ds(y + k, LX, stride=pitch), :] = done[:, 128 * k : 128 * (k + 1)]

    depth = per * slots * ny
    row = lax.broadcasted_iota(jnp.int32, (LY * per, depth), 0).astype(F32)
    lane = lax.broadcasted_iota(jnp.int32, (LY * per, depth), 1).astype(F32)
    which = jnp.floor((row + 0.5) * (1.0 / per))
    inside = row - which * per
    owner = jnp.floor((lane + 0.5) * (1.0 / (slots * ny)))
    coord = jnp.concatenate([cy_ref[b : b + 1, :] for b in range(slots)] * per, axis=1)
    hat_y = jnp.maximum(0.0, 1.0 - jnp.abs(which - coord))
    hat_y = thrice(jnp.where(inside == owner, hat_y, 0.0), 1, False)
    third_rows = LY // 4 * per
    pieces = keep_ref.shape[3]
    size = 3 * third_rows // 8
    tail = lax.broadcasted_iota(jnp.int32, (third_rows, 128), 1) >= 3 * LZ
    even = dest_ref[0] == 0
    for pair in range(LX // per // 2):
        terms = []
        for number in (2 * pair, 2 * pair + 1):
            rows = []
            for line in range(number * per, (number + 1) * per):
                at = slice(line * pitch, line * pitch + ny)
                rows += [part_0[at] + xdone[0, at], part_1[at] + xdone[1, at]]
            terms.append(jnp.concatenate(rows, axis=0))
        both = dot(hat_y, thrice(jnp.concatenate(terms, axis=1), 0, True))
        for k in range(2):
            done = both[:, 128 * k : 128 * (k + 1)]
            tops = done[3 * third_rows :]
            dense = []
            for q in range(3):
                moved = pltpu.roll(tops, 3 * LZ - q * LZ, 1)
                dense.append(jnp.where(tail, moved, done[q * third_rows : (q + 1) * third_rows]))
            dense = jnp.concatenate(dense, axis=0)
            number = 2 * pair + k
            d, t = number // pieces, number % pieces
            for g in range(4):
                first = dense[g * size : (g + 1) * size]
                second = dense[(g + 4) * size : (g + 5) * size]
                keep_ref[d, g // 2, g % 2, t] = jnp.where(even, first, second)
                send_ref[d, g // 2, g % 2, t] = jnp.where(even, second, first)
    for copy in copies:
        copy.wait()


def core_kernel(dest_ref, keep_ref, got_ref, keep_y, send_y, keep_x, send_x):
    y, x = dest_ref[2], dest_ref[1]
    keep_y[...] = keep_ref[:, y, 0] + got_ref[:, y, 0]
    send_y[...] = keep_ref[:, 1 - y, 0] + got_ref[:, 1 - y, 0]
    keep_x[...] = keep_ref[:, :, 1, x] + got_ref[:, :, 1, x]
    send_x[...] = keep_ref[:, :, 1, 1 - x] + got_ref[:, :, 1, 1 - x]


def plane_kernel(dest_ref, keep_y, got_y, keep_x, got_x, keep_0, send_0, keep_1, send_1):
    y, x = dest_ref[2], dest_ref[1]
    keep_0[...] = keep_y[:, x] + got_y[:, x]
    send_0[...] = keep_y[:, 1 - x] + got_y[:, 1 - x]
    keep_1[...] = keep_x[:, y] + got_x[:, y]
    send_1[...] = keep_x[:, 1 - y] + got_x[:, 1 - y]


def line_kernel(dest_ref, keep_0, got_0, keep_1, got_1, *outs):
    z = dest_ref[3]
    count = len(outs)
    for k, out in enumerate(outs):
        at = lax.rem(z + k, count)
        out[0] = keep_0[at] + got_0[at]
        out[1] = keep_1[at] + got_1[at]


def sum_kernel(scale, *refs):
    total = refs[0][...]
    for ref in refs[1:-1]:
        total = total + ref[...]
    refs[-1][...] = total * scale


def unpack_kernel(per, dest_ref, own, got_c, got_x, got_xc, out_ref, pieces):
    core, x = dest_ref[0], dest_ref[1]
    pieces[core, x] = own[...]
    pieces[1 - core, x] = got_c[...]
    pieces[core, 1 - x] = got_x[...]
    pieces[1 - core, 1 - x] = got_xc[...]
    count = own.shape[1]
    quarter = LY // 4
    size = 3 * quarter // 8
    lane = lax.broadcasted_iota(jnp.int32, (per, 128), 1) // LZ
    for t in range(count):

        def strip(r):
            g, at = r // size, r % size
            return pieces[g // 4, g % 2, g // 2 % 2, t, at * per : (at + 1) * per]

        for c in range(3):
            for m4 in range(LY // 4):
                tile = None
                for k in range(4):
                    m = 4 * m4 + k
                    if m < 3 * quarter:
                        value, lies = strip(m), c
                    else:
                        value, lies = strip(c * quarter + m - 3 * quarter), 3
                    shift = ((k - lies) * LZ) % 128
                    value = pltpu.roll(value, shift, 1) if shift else value
                    tile = value if tile is None else jnp.where(lane == k, value, tile)
                at = c * LY * LZ + m4 * 128
                out_ref[t * per : (t + 1) * per, at : at + 128] = tile


def on_device(groups, devs, seed, stiff, lengths, low, up, coord_x, coord_y, coord_z):
    slots, nx, ny, nz = stiff.shape
    faces = 2 * slots
    chunk = PLANES * ny // devs
    rows = faces * chunk
    mine = LX // devs
    per = 4 if mine % 4 == 0 else mine
    pieces = mine // per
    size = 3 * LY // 4 // 8 * per
    group_at = lax.axis_index("group")
    dev_at = lax.axis_index("dev")
    fast = groups == 4 and devs % 2 == 0 and size % 8 == 0
    if fast:
        dest = jnp.stack([group_at % 2, group_at // 2, dev_at % 2, dev_at // 2]).astype(jnp.int32)
    else:
        dest = jnp.zeros((4,), jnp.int32)
    shape = lambda *dims: jax.ShapeDtypeStruct(dims, F32)

    packed = pl.pallas_call(
        functools.partial(pack_kernel, devs, slots, nx, ny, nz),
        out_shape=shape(devs, rows + 8, nz),
        in_specs=[HBM] * 5,
        out_specs=VMEM,
        scratch_shapes=[
            pltpu.SMEM((slots,), jnp.int32),
            pltpu.SMEM((slots, 3), jnp.int32),
            pltpu.SMEM((slots, 3), jnp.int32),
            pltpu.VMEM((faces, 3, 2, ny, nz), seed.dtype),
            pltpu.VMEM((faces, 3, ny, nz), F32),
            pltpu.VMEM((faces, PLANES * ny, nz), F32),
            pltpu.SemaphoreType.DMA((3, faces)),
        ],
        compiler_params=params(4),
        name="pack",
    )(lengths, low, up, seed, stiff)
    spread = lax.all_to_all(packed, "dev", 0, 0)
    ext = (nx + 2, ny + 16, nz)
    plain = pltpu.VMEM((nx, ny, nz), F32)

    def one_block(b, adjoint):
        given = () if adjoint is None else (adjoint,)
        return pl.pallas_call(
            functools.partial(block_kernel, b),
            out_shape=(
                shape(slots, 3, nx, ny, nz),
                shape(2, EDGES, ny, nz),
                shape(LX * (ny + 1), 128),
            ),
            in_specs=[SMEM, ANY, ANY, VMEM, VMEM] + [HBM] * len(given),
            out_specs=(HBM, VMEM, VMEM),
            scratch_shapes=[
                pltpu.VMEM(ext, F32),
                pltpu.VMEM((3, *ext), F32),
                pltpu.VMEM((3, *ext), F32),
                plain,
                plain,
                pltpu.VMEM((3, nx, ny, nz), F32),
                pltpu.VMEM((3, nx, ny, nz), seed.dtype),
                pltpu.VMEM((nx * (ny + 1), 128), F32),
                pltpu.SemaphoreType.DMA((3,)),
            ],
            input_output_aliases={5: 0} if given else {},
            compiler_params=params(16),
            cost_estimate=pl.CostEstimate(
                flops=3 * 10**9, bytes_accessed=10**7, transcendentals=0
            ),
            name=f"block_{b}",
        )(lengths, seed, stiff, coord_x, coord_z, *given)

    early, edge_0, part_0 = one_block(0, None)
    routed = pl.pallas_call(
        route_kernel,
        out_shape=shape(devs, rows, nz),
        in_specs=[VMEM],
        out_specs=VMEM,
        compiler_params=params(4),
        name="route",
    )(spread)
    early, routed = lax.optimization_barrier((early, routed))
    halos = lax.all_to_all(routed, "dev", 0, 0)
    early, edge_1, part_1 = one_block(1, early)

    half = shape(devs, 2, 2, pieces, size, 128)
    adjoint, keep, send = pl.pallas_call(
        functools.partial(outer_kernel, per),
        out_shape=(shape(slots, 3, nx, ny, nz), half, half),
        in_specs=[SMEM] * 5 + [VMEM] * 7 + [HBM],
        out_specs=(HBM, VMEM, VMEM),
        scratch_shapes=[
            pltpu.VMEM((faces, PLANES, ny, nz), F32),
            pltpu.VMEM((slots, 3, 2 * ENDS, ny, nz), F32),
            pltpu.VMEM((8 * (ny + 1), 128), F32),
            pltpu.VMEM((slots, LX * (ny + 1), 128), F32),
            pltpu.SemaphoreType.DMA((faces, 3)),
        ],
        input_output_aliases={12: 0},
        compiler_params=params(16),
        name="outer",
    )(
        dest,
        lengths,
        low,
        up,
        coord_x,
        halos,
        edge_0,
        edge_1,
        part_0,
        part_1,
        coord_y,
        coord_z,
        early,
    )

    scale = math.sqrt(LX * LY * LZ / (groups * devs * slots * nx * ny * nz))

    def small(kernel, outs, args, scratch=()):
        return pl.pallas_call(
            kernel,
            out_shape=outs,
            in_specs=[SMEM if a is dest else VMEM for a in args],
            out_specs=jax.tree.map(lambda _: VMEM, outs),
            scratch_shapes=scratch,
            compiler_params=params(8),
        )(*args)

    piece = (2, pieces, size, 128)
    if fast:
        lines = devs // 2
        body = pieces * size

        def move(value, to):
            links = []
            for g in range(groups):
                for d in range(devs):
                    c2, x2, y2, z2 = to(g % 2, g // 2, d % 2, d // 2)
                    links.append((g * devs + d, (x2 * 2 + c2) * devs + z2 * 2 + y2))
            return lax.ppermute(value, ("group", "dev"), links)

        flip_c = lambda c, x, y, z: (1 - c, x, y, z)
        flip_x = lambda c, x, y, z: (c, 1 - x, y, z)
        flip_y = lambda c, x, y, z: (c, x, 1 - y, z)
        flip_xc = lambda c, x, y, z: (1 - c, 1 - x, y, z)
        got = move(send, flip_c)
        view = (lines, 2, 2, 2, body, 128)
        part = shape(lines, 2, body, 128)
        keep_y, send_y, keep_x, send_x = small(
            core_kernel, (part,) * 4, (dest, keep.reshape(view), got.reshape(view))
        )
        got_y, got_x = move(send_y, flip_y), move(send_x, flip_x)
        part = shape(lines, body, 128)
        keep_0, send_0, keep_1, send_1 = small(
            plane_kernel, (part,) * 4, (dest, keep_y, got_y, keep_x, got_x)
        )
        got_0, got_1 = move(send_0, flip_x), move(send_1, flip_y)
        part = shape(2, body, 128)
        sums = small(line_kernel, (part,) * lines, (dest, keep_0, got_0, keep_1, got_1))
        terms = [sums[0]]
        for k in range(1, lines):
            terms.append(move(sums[k], lambda c, x, y, z, k=k: (c, x, y, (z + k) % lines)))
        own = small(functools.partial(sum_kernel, scale), part, tuple(terms))
        others = [move(own, to) for to in (flip_c, flip_x, flip_xc)]
        quarters = [v.reshape(piece) for v in (own, *others)]
    else:
        whole = jnp.stack([keep, send], axis=1).reshape(devs, -1, 128)
        owned = lax.psum_scatter(whole, "dev", scatter_dimension=0, tiled=True)
        owned = lax.psum(owned, "group") * scale
        owned = owned.reshape(2, 2, 2, pieces, size, 128)
        quarters = [owned[c, :, x] for x in range(2) for c in range(2)]
    lattice = small(
        functools.partial(unpack_kernel, per),
        shape(mine, 3 * LY * LZ),
        (dest, *quarters),
        [pltpu.VMEM((2, 2, *piece), F32)],
    )
    return adjoint, lattice


def solution(mesh):
    both = ("group", "dev")
    in_specs = (
        P(both, None, None, None, None),
        P(both, None, None, None),
        P(both),
        P(both, None),
        P(both, None),
        P(both, None),
        P(both, None),
        P(both, None),
    )
    out_specs = (P(both, None, None, None, None), P("dev", None))
    body = functools.partial(on_device, mesh.shape["group"], mesh.shape["dev"])
    return jax.shard_map(
        body, mesh=mesh, in_specs=in_specs, out_specs=out_specs, check_vma=False
    )
```

```python
import functools
import math

import jax
import jax.numpy as jnp
from jax import lax
from jax.experimental import pallas as pl
from jax.experimental.pallas import tpu as pltpu
from jax.sharding import PartitionSpec as P

LX = 96
LY = 64
LZ = 32
DOMINANCE = 1.25
PLANES = 8
STEP = 24
ENDS = 3
EDGES = 20

F32 = jnp.float32
BF16 = jnp.bfloat16
SMEM = pl.BlockSpec(memory_space=pltpu.SMEM)
VMEM = pl.BlockSpec(memory_space=pltpu.VMEM)
ANY = pl.BlockSpec(memory_space=pl.ANY)
HBM = pl.BlockSpec(memory_space=pltpu.HBM)


def params(mib):
    return pltpu.CompilerParams(vmem_limit_bytes=mib * 1024 * 1024)


def neighbours(v, axis):
    extent = v.shape[axis]
    place = lax.broadcasted_iota(jnp.int32, v.shape, axis)
    up = jnp.where(place == 0, 0.0, pltpu.roll(v, 1, axis))
    down = jnp.where(place == extent - 1, 0.0, pltpu.roll(v, extent - 1, axis))
    return up + down


def plane_parts(v):
    along_z = neighbours(v, v.ndim - 1)
    first = v + 0.5 * along_z
    second = 0.5 * v + (1.0 / 3.0) * along_z
    beside = first + neighbours(second, v.ndim - 2)
    own = along_z + neighbours(first, v.ndim - 2)
    return beside, own


def padded_stencil(ref, lead, i, count):
    rows = ref.shape[-2] - 16
    planes = pl.ds(i, count + 2)
    v = ref[(*lead, planes, slice(8, 8 + rows))]
    t = ref[(*lead, planes, slice(7, 7 + rows))] + ref[(*lead, planes, slice(9, 9 + rows))]
    t_beside = t[:-2] + t[2:]
    near = t[1:-1] + (v[:-2] + v[2:])
    mixed = v[1:-1] + 0.5 * near + (1.0 / 3.0) * t_beside
    return v[1:-1], near + 0.5 * t_beside + neighbours(mixed, mixed.ndim - 1)


def split(v):
    high = v.astype(BF16)
    return high, (v - high.astype(F32)).astype(BF16)


def thrice(v, axis, data):
    high, low = split(v)
    parts = [high, low, high] if data else [high, high, low]
    return jnp.concatenate(parts, axis=axis)


def dot(a, b, contract_b=0):
    numbers = (((1,), (contract_b,)), ((), ()))
    return lax.dot_general(a, b, numbers, preferred_element_type=F32)


def pack_kernel(devs, slots, nx, ny, nz, len_in, low_in, up_in, seed_in, stiff_in, out_ref, *scratch):
    len_ref, low_ref, up_ref, seed_ref, stiff_ref, packet, sems = scratch
    rows = PLANES * ny
    chunk = rows // devs
    small = []
    for k, (src, dst) in enumerate(((len_in, len_ref), (low_in, low_ref), (up_in, up_ref))):
        small.append(pltpu.make_async_copy(src, dst, sems.at[0, k]))
        small[k].start()
    copies = {}

    def fetch(s, side):
        f = 2 * s + side
        start = [0, 0] if side == 0 else [len_ref[s] - 3, len_ref[s] - 2]
        copies[f] = (
            pltpu.make_async_copy(stiff_in.at[s, pl.ds(start[0], 3)], stiff_ref.at[f], sems.at[1, f]),
            pltpu.make_async_copy(seed_in.at[s, :, pl.ds(start[1], 2)], seed_ref.at[f], sems.at[2, f]),
        )
        for copy in copies[f]:
            copy.start()

    for s in range(slots):
        fetch(s, 0)
    small[0].wait()
    for s in range(slots):
        fetch(s, 1)
    small[1].wait()
    small[2].wait()
    wanted = []
    for s in range(slots):
        for side, ref in ((0, low_ref), (1, up_ref)):
            number = jnp.maximum(ref[s, 0], 0) * (2 * slots) + ref[s, 1] * 2 + (1 - side)
            wanted.append(number.astype(F32))
    row = lax.broadcasted_iota(jnp.int32, (8, nz), 0)
    note = jnp.zeros((8, nz), F32)
    for f, number in enumerate(wanted):
        note = jnp.where(row == f, number, note)
    for f in (0, 2, 1, 3):
        side = f % 2
        for copy in copies[f]:
            copy.wait()
        stiff = [stiff_ref[f, k if side == 0 else 2 - k] for k in range(3)]
        parts = [plane_parts(v) for v in stiff]
        inner = parts[0][1] + parts[1][0]
        next_near = parts[1][1] + parts[0][0] + parts[2][0]
        scale = 1.0 / (DOMINANCE * next_near)
        planes = [stiff[0], inner]
        planes += [seed_ref[f, c, side].astype(F32) for c in range(3)]
        for c in range(3):
            planes.append(plane_parts(seed_ref[f, c, 1 - side].astype(F32) * scale)[0])
        for k, plane in enumerate(planes):
            packet[f, k * ny : (k + 1) * ny] = plane
    for j in range(devs):
        for f in range(2 * slots):
            out_ref[j, f * chunk : (f + 1) * chunk] = packet[f, j * chunk : (j + 1) * chunk]
        out_ref[j, 2 * slots * chunk :] = note


def route_kernel(in_ref, out_ref):
    devs, rows, _ = out_ref.shape
    faces = 4
    chunk = rows // faces
    for e in range(devs):
        for f in range(faces):
            cell = in_ref[e, rows + f : rows + f + 1, 0:1]
            number = cell[0, 0].astype(jnp.int32)
            source = number // faces
            start = (number % faces) * chunk
            if chunk % 8 == 0:
                start = pl.multiple_of(start, 8)
            out_ref[e, f * chunk : (f + 1) * chunk] = in_ref[source, pl.ds(start, chunk)]


def hat_along_z(coord, nz):
    row = lax.broadcasted_iota(jnp.int32, (128, 3 * nz), 0)
    lane = lax.broadcasted_iota(jnp.int32, (128, 3 * nz), 1)
    point = (row % LZ).astype(F32)
    hat = jnp.maximum(0.0, 1.0 - jnp.abs(point - jnp.concatenate([coord] * 3, axis=1)))
    return thrice(jnp.where((row // LZ) == (lane // nz), hat, 0.0), 1, False)


class Planes:
    def __init__(self, ref, start, ny):
        self.ref, self.start, self.ny = ref, start, ny

    def rows(self, key):
        return pl.ds(self.start + (key[0] * EDGES + key[1]) * self.ny, self.ny)

    def __getitem__(self, key):
        return self.ref[self.rows(key)]

    def __setitem__(self, key, value):
        self.ref[self.rows(key)] = value


def block_kernel(b, len_ref, seed_in, stiff_in, cx_ref, cz_ref, *refs):
    s_ext, w_ext, v_ext, fac_ref, mul_ref, adj, seeds, zdone, sems = refs[-9:]
    adj_out, part_ref, *passed = refs[:3] if b == 0 else refs[1:3]
    nx, ny, nz = fac_ref.shape
    edge_ref = Planes(part_ref, LX * (ny + 1), ny)
    last = 8 + ny
    length = len_ref[b]
    loads = (
        pltpu.make_async_copy(
            stiff_in.at[0] if b == 0 else stiff_in, s_ext.at[pl.ds(1, nx), pl.ds(8, ny)], sems.at[0]
        ),
        pltpu.make_async_copy(seed_in.at[b], seeds, sems.at[1]),
    )
    for copy in loads:
        copy.start()
    if b == 0:
        ahead = pltpu.make_async_copy(stiff_in.at[1], passed[0], sems.at[3])
        ahead.start()
    zeros = jnp.zeros((nx + 2, 8, nz), F32)
    plane = jnp.zeros((ny, nz), F32)
    for ref, lead in ((s_ext, ()), *((r, (c,)) for r in (w_ext, v_ext) for c in range(3))):
        ref[(*lead, slice(None), slice(0, 8))] = zeros
        ref[(*lead, slice(None), slice(last, last + 8))] = zeros
        for i in (0, nx + 1):
            ref[(*lead, i, slice(8, last))] = plane
    hat_z = hat_along_z(cz_ref[b : b + 1, :], nz)
    line = lax.broadcasted_iota(jnp.int32, (LX, 3 * nx), 0).astype(F32)
    lane = lax.broadcasted_iota(jnp.int32, (LX, 3 * nx), 1)
    x = lane % nx
    coord = jnp.concatenate([cx_ref[b : b + 1, :]] * 3, axis=1)
    hat = jnp.maximum(0.0, 1.0 - jnp.abs(line - coord))
    hat = jnp.where(jnp.logical_and(x >= ENDS, x < length - ENDS), hat, 0.0)
    high, low = split(hat)
    hat_x = jnp.where(lane < 2 * nx, high.astype(F32), low.astype(F32)).astype(BF16)
    for copy in loads:
        copy.wait()

    def clear(i, _):
        s_ext[i + 1, 8:last] = plane
        return 0

    lax.fori_loop(length, nx, clear, 0)

    def loop(body):
        def step(k, _):
            body(k * STEP)
            return 0

        lax.fori_loop(0, nx // STEP, step, 0)

    def first(i):
        stiff, near = padded_stencil(s_ext, (), i, STEP)
        active = i + lax.broadcasted_iota(jnp.int32, (STEP, ny, nz), 0) < length
        safe = jnp.where(active, DOMINANCE * stiff * near, 1.0)
        inv = jnp.where(active, 1.0 / safe, 0.0)
        fac = stiff * inv
        fac_ref[pl.ds(i, STEP)] = fac
        mul_ref[pl.ds(i, STEP)] = stiff * fac
        for c in range(3):
            seed = seeds[c, pl.ds(i, STEP)].astype(F32)
            w_ext[c, pl.ds(i + 1, STEP), 8:last] = seed * fac
            adj[c, pl.ds(i, STEP)] = seed * inv

    loop(first)

    at = [[k if side == 0 else length - 1 - k for k in range(4)] for side in range(2)]
    for f in range(2):
        for c in range(3):
            edge_ref[f, 11 + c] = adj[c, at[f][1]]
            edge_ref[f, 14 + c] = adj[c, at[f][2]]

    def second(i):
        mul = mul_ref[pl.ds(i, STEP)]
        for c in range(3):
            here, near = padded_stencil(w_ext, (c,), i, STEP)
            v_ext[c, pl.ds(i + 1, STEP), 8:last] = here + mul * near

    loop(second)

    def third(i):
        fac = fac_ref[pl.ds(i, STEP)]
        for c in range(3):
            _, near = padded_stencil(v_ext, (c,), i, STEP)
            adj[c, pl.ds(i, STEP)] += fac * near

    loop(third)
    store = pltpu.make_async_copy(adj, adj_out.at[b], sems.at[2])
    store.start()

    def parts(ref, *lead):
        v = ref[(*lead, slice(8, last))]
        t = ref[(*lead, slice(7, last - 1))] + ref[(*lead, slice(9, last + 1))]
        own = t + neighbours(v + 0.5 * t, 1)
        return v + 0.5 * t + neighbours(0.5 * v + (1.0 / 3.0) * t, 1), own

    for f in range(2):
        edge_ref[f, 0] = s_ext[at[f][0] + 1, 8:last]
        edge_ref[f, 1] = parts(s_ext, at[f][0] + 1)[1] + parts(s_ext, at[f][1] + 1)[0]
        mul_1, fac_1, fac_2 = mul_ref[at[f][1]], fac_ref[at[f][1]], fac_ref[at[f][2]]
        edge_ref[f, 17], edge_ref[f, 18], edge_ref[f, 19] = mul_1, fac_1, fac_2
        for c in range(3):
            edge_ref[f, 2 + c] = seeds[c, at[f][0]].astype(F32)
            beside, own = parts(w_ext, c, at[f][1] + 1)
            edge_ref[f, 5 + c] = beside
            own = own + parts(w_ext, c, at[f][2] + 1)[0]
            edge_ref[f, 8 + c] = w_ext[c, at[f][1] + 1, 8:last] + mul_1 * own
            beside, own = parts(v_ext, c, at[f][2] + 1)
            edge_ref[f, 11 + c] += fac_1 * beside
            edge_ref[f, 14 + c] += fac_2 * (own + parts(v_ext, c, at[f][3] + 1)[0])

    group = 16
    pitch = ny + 1
    for x in range(0, nx, group):
        rows = [adj[c, x : x + group].reshape(group * ny, nz) for c in range(3)]
        done = dot(thrice(jnp.concatenate(rows, axis=1), 1, True), hat_z, 1)
        for k in range(group):
            zdone[(x + k) * pitch : (x + k) * pitch + ny] = done[k * ny : (k + 1) * ny]
    for y in range(0, ny, 2):
        part = [zdone[pl.ds(y + k, nx, stride=pitch), :] for k in range(2)]
        done = dot(hat_x, thrice(jnp.concatenate(part, axis=1), 0, True))
        for k in range(2):
            part_ref[pl.ds(y + k, LX, stride=pitch), :] = done[:, 128 * k : 128 * (k + 1)]
    store.wait()
    if b == 0:
        ahead.wait()


def outer_kernel(
    per,
    dest_ref,
    len_ref,
    low_ref,
    up_ref,
    cx_ref,
    halo_ref,
    part_0,
    part_1,
    cy_ref,
    cz_ref,
    adj_in,
    adj_out,
    keep_ref,
    send_ref,
    pack,
    ends,
    zdone,
    xdone,
    sems,
):
    del adj_in
    slots = 2
    faces = 2 * slots
    _, _, _, ny, nz = ends.shape
    pitch = ny + 1
    chunk = halo_ref.shape[1] // faces
    zero_plane = jnp.zeros((ny, nz), F32)

    for s in range(slots):
        for side, ref in ((0, low_ref), (1, up_ref)):
            f = 2 * s + side
            wall = ref[s, 0] < 0
            turned = ref[s, 2] == 1

            def place(reverse, f=f):
                for k in range(PLANES):
                    for r in range(ny):
                        at = k * ny + r
                        to = ny - 1 - r if reverse else r
                        j, o = at // chunk, at % chunk
                        pack[f, k, to : to + 1] = halo_ref[j, f * chunk + o : f * chunk + o + 1]

            @pl.when(wall)
            def _(f=f):
                for k in range(PLANES):
                    pack[f, k] = zero_plane

            @pl.when(jnp.logical_and(jnp.logical_not(wall), turned))
            def _(place=place):
                place(True)

            @pl.when(jnp.logical_and(jnp.logical_not(wall), jnp.logical_not(turned)))
            def _(place=place):
                place(False)

    copies = []
    for f in range(faces):
        b, side = f // 2, f % 2
        edge = Planes((part_0, part_1)[b], LX * pitch, ny)
        stiff, inside = edge[side, 0], edge[side, 1]
        beside = plane_parts(stiff)[0]
        there = 1.0 / (DOMINANCE * (pack[f, 1] + beside))
        inv = 1.0 / (DOMINANCE * stiff * (inside + plane_parts(pack[f, 0])[0]))
        fac = stiff * inv
        mul_1, fac_1, fac_2 = edge[side, 17], edge[side, 18], edge[side, 19]
        for c in range(3):
            seed = edge[side, 2 + c]
            w_n = pack[f, 2 + c] * there
            w_0 = seed * fac
            beside_n, own_n = plane_parts(w_n)
            beside_0, own_0 = plane_parts(w_0)
            v_n = w_n + pack[f, 0] * there * (own_n + pack[f, 5 + c] + beside_0)
            v_0 = w_0 + stiff * fac * (own_0 + edge[side, 5 + c] + beside_n)
            v_1 = edge[side, 8 + c] + mul_1 * beside_0
            beside_n = plane_parts(v_n)[0]
            beside_0, own_0 = plane_parts(v_0)
            beside_1, own_1 = plane_parts(v_1)
            rows = [
                seed * inv + fac * (own_0 + beside_1 + beside_n),
                edge[side, 11 + c] + fac_1 * (own_1 + beside_0),
                edge[side, 14 + c] + fac_2 * beside_1,
            ]
            for k, row in enumerate(rows):
                ends[b, c, k if side == 0 else 2 * ENDS - 1 - k] = row
            start = 0 if side == 0 else len_ref[b] - ENDS
            copy = pltpu.make_async_copy(
                ends.at[b, c, pl.ds(side * ENDS, ENDS)],
                adj_out.at[b, c, pl.ds(start, ENDS)],
                sems.at[f, c],
            )
            copy.start()
            copies.append(copy)

    eight = 8
    line = lax.broadcasted_iota(jnp.int32, (LX, 4 * eight), 0).astype(F32)
    lane = lax.broadcasted_iota(jnp.int32, (LX, 4 * eight), 1)
    for b in range(slots):
        hat_z = hat_along_z(cz_ref[b : b + 1, :], nz)
        rows = [ends[b, c].reshape(2 * ENDS * ny, nz) for c in range(3)]
        done = dot(thrice(jnp.concatenate(rows, axis=1), 1, True), hat_z, 1)
        for k in range(eight):
            rows = done[k * ny : (k + 1) * ny] if k < 2 * ENDS else jnp.zeros((ny, 128), F32)
            zdone[k * pitch : k * pitch + ny] = rows
        coord = jnp.full((LX, 4 * eight), -4.0, F32)
        for k in range(2 * ENDS):
            at = k if k < ENDS else len_ref[b] - 2 * ENDS + k
            coord = jnp.where(lane % eight == k, cx_ref[b, at], coord)
        hat = jnp.maximum(0.0, 1.0 - jnp.abs(line - coord))
        high, low = split(hat)
        hat_x = jnp.where(lane < 2 * eight, high.astype(F32), low.astype(F32)).astype(BF16)
        for y in range(0, ny, 2):
            part = [zdone[pl.ds(y + k, eight, stride=pitch), :] for k in range(2)]
            high, low = split(jnp.concatenate(part, axis=1))
            high, low = high.astype(F32), low.astype(F32)
            stack = jnp.concatenate([high, low, high, jnp.zeros_like(high)], axis=0)
            done = dot(hat_x, stack.astype(BF16))
            for k in range(2):
                xdone[b, pl.ds(y + k, LX, stride=pitch), :] = done[:, 128 * k : 128 * (k + 1)]

    depth = per * slots * ny
    row = lax.broadcasted_iota(jnp.int32, (LY * per, depth), 0).astype(F32)
    lane = lax.broadcasted_iota(jnp.int32, (LY * per, depth), 1).astype(F32)
    which = jnp.floor((row + 0.5) * (1.0 / per))
    inside = row - which * per
    owner = jnp.floor((lane + 0.5) * (1.0 / (slots * ny)))
    coord = jnp.concatenate([cy_ref[b : b + 1, :] for b in range(slots)] * per, axis=1)
    hat_y = jnp.maximum(0.0, 1.0 - jnp.abs(which - coord))
    hat_y = thrice(jnp.where(inside == owner, hat_y, 0.0), 1, False)
    third_rows = LY // 4 * per
    pieces = keep_ref.shape[3]
    size = 3 * third_rows // 8
    tail = lax.broadcasted_iota(jnp.int32, (third_rows, 128), 1) >= 3 * LZ
    even = dest_ref[0] == 0
    for pair in range(LX // per // 2):
        terms = []
        for number in (2 * pair, 2 * pair + 1):
            rows = []
            for line in range(number * per, (number + 1) * per):
                at = slice(line * pitch, line * pitch + ny)
                rows += [part_0[at] + xdone[0, at], part_1[at] + xdone[1, at]]
            terms.append(jnp.concatenate(rows, axis=0))
        both = dot(hat_y, thrice(jnp.concatenate(terms, axis=1), 0, True))
        for k in range(2):
            done = both[:, 128 * k : 128 * (k + 1)]
            tops = done[3 * third_rows :]
            dense = []
            for q in range(3):
                moved = pltpu.roll(tops, 3 * LZ - q * LZ, 1)
                dense.append(jnp.where(tail, moved, done[q * third_rows : (q + 1) * third_rows]))
            dense = jnp.concatenate(dense, axis=0)
            number = 2 * pair + k
            d, t = number // pieces, number % pieces
            for g in range(4):
                first = dense[g * size : (g + 1) * size]
                second = dense[(g + 4) * size : (g + 5) * size]
                keep_ref[d, g // 2, g % 2, t] = jnp.where(even, first, second)
                send_ref[d, g // 2, g % 2, t] = jnp.where(even, second, first)
    for copy in copies:
        copy.wait()


def core_kernel(dest_ref, keep_ref, got_ref, keep_y, send_y, keep_x, send_x):
    y, x = dest_ref[2], dest_ref[1]
    keep_y[...] = keep_ref[:, y, 0] + got_ref[:, y, 0]
    send_y[...] = keep_ref[:, 1 - y, 0] + got_ref[:, 1 - y, 0]
    keep_x[...] = keep_ref[:, :, 1, x] + got_ref[:, :, 1, x]
    send_x[...] = keep_ref[:, :, 1, 1 - x] + got_ref[:, :, 1, 1 - x]


def plane_kernel(dest_ref, keep_y, got_y, keep_x, got_x, keep_0, send_0, keep_1, send_1):
    y, x = dest_ref[2], dest_ref[1]
    keep_0[...] = keep_y[:, x] + got_y[:, x]
    send_0[...] = keep_y[:, 1 - x] + got_y[:, 1 - x]
    keep_1[...] = keep_x[:, y] + got_x[:, y]
    send_1[...] = keep_x[:, 1 - y] + got_x[:, 1 - y]


def line_kernel(dest_ref, keep_0, got_0, keep_1, got_1, *outs):
    z = dest_ref[3]
    count = len(outs)
    for k, out in enumerate(outs):
        at = lax.rem(z + k, count)
        out[0] = keep_0[at] + got_0[at]
        out[1] = keep_1[at] + got_1[at]


def sum_kernel(scale, *refs):
    total = refs[0][...]
    for ref in refs[1:-1]:
        total = total + ref[...]
    refs[-1][...] = total * scale


def unpack_kernel(per, dest_ref, own, got_c, got_x, got_xc, out_ref, pieces):
    core, x = dest_ref[0], dest_ref[1]
    pieces[core, x] = own[...]
    pieces[1 - core, x] = got_c[...]
    pieces[core, 1 - x] = got_x[...]
    pieces[1 - core, 1 - x] = got_xc[...]
    count = own.shape[1]
    quarter = LY // 4
    size = 3 * quarter // 8
    lane = lax.broadcasted_iota(jnp.int32, (per, 128), 1) // LZ
    for t in range(count):

        def strip(r):
            g, at = r // size, r % size
            return pieces[g // 4, g % 2, g // 2 % 2, t, at * per : (at + 1) * per]

        for c in range(3):
            for m4 in range(LY // 4):
                tile = None
                for k in range(4):
                    m = 4 * m4 + k
                    if m < 3 * quarter:
                        value, lies = strip(m), c
                    else:
                        value, lies = strip(c * quarter + m - 3 * quarter), 3
                    shift = ((k - lies) * LZ) % 128
                    value = pltpu.roll(value, shift, 1) if shift else value
                    tile = value if tile is None else jnp.where(lane == k, value, tile)
                at = c * LY * LZ + m4 * 128
                out_ref[t * per : (t + 1) * per, at : at + 128] = tile


def on_device(groups, devs, seed, stiff, lengths, low, up, coord_x, coord_y, coord_z):
    slots, nx, ny, nz = stiff.shape
    faces = 2 * slots
    chunk = PLANES * ny // devs
    rows = faces * chunk
    mine = LX // devs
    per = 4 if mine % 4 == 0 else mine
    pieces = mine // per
    size = 3 * LY // 4 // 8 * per
    group_at = lax.axis_index("group")
    dev_at = lax.axis_index("dev")
    fast = groups == 4 and devs % 2 == 0 and size % 8 == 0
    if fast:
        dest = jnp.stack([group_at % 2, group_at // 2, dev_at % 2, dev_at // 2]).astype(jnp.int32)
    else:
        dest = jnp.zeros((4,), jnp.int32)
    shape = lambda *dims: jax.ShapeDtypeStruct(dims, F32)

    packed = pl.pallas_call(
        functools.partial(pack_kernel, devs, slots, nx, ny, nz),
        out_shape=shape(devs, rows + 8, nz),
        in_specs=[HBM] * 5,
        out_specs=VMEM,
        scratch_shapes=[
            pltpu.SMEM((slots,), jnp.int32),
            pltpu.SMEM((slots, 3), jnp.int32),
            pltpu.SMEM((slots, 3), jnp.int32),
            pltpu.VMEM((faces, 3, 2, ny, nz), seed.dtype),
            pltpu.VMEM((faces, 3, ny, nz), F32),
            pltpu.VMEM((faces, PLANES * ny, nz), F32),
            pltpu.SemaphoreType.DMA((3, faces)),
        ],
        compiler_params=params(60),
        name="pack",
    )(lengths, low, up, seed, stiff)
    spread = lax.all_to_all(packed, "dev", 0, 0)
    ext = (nx + 2, ny + 16, nz)
    plain = pltpu.VMEM((nx, ny, nz), F32)

    def one_block(b, stiff, *given):
        return pl.pallas_call(
            functools.partial(block_kernel, b),
            out_shape=(
                shape(slots, 3, nx, ny, nz),
                shape(LX * (ny + 1) + 2 * EDGES * ny, 128),
                *([shape(nx, ny, nz)] if b == 0 else []),
            ),
            in_specs=[SMEM, ANY, ANY, VMEM, VMEM] + [HBM] * len(given),
            out_specs=(HBM, VMEM, VMEM) if b == 0 else (HBM, VMEM),
            scratch_shapes=[
                pltpu.VMEM(ext, F32),
                pltpu.VMEM((3, *ext), F32),
                pltpu.VMEM((3, *ext), F32),
                plain,
                plain,
                pltpu.VMEM((3, nx, ny, nz), F32),
                pltpu.VMEM((3, nx, ny, nz), seed.dtype),
                pltpu.VMEM((nx * (ny + 1), 128), F32),
                pltpu.SemaphoreType.DMA((4,)),
            ],
            input_output_aliases={5: 0} if given else {},
            compiler_params=params(12),
            cost_estimate=pl.CostEstimate(
                flops=3 * 10**9, bytes_accessed=10**7, transcendentals=0
            ),
            name=f"block_{b}",
        )(lengths, seed, stiff, coord_x, coord_z, *given)

    early, part_0, stiff_1 = one_block(0, stiff)
    routed = pl.pallas_call(
        route_kernel,
        out_shape=shape(devs, rows, nz),
        in_specs=[VMEM],
        out_specs=VMEM,
        compiler_params=params(4),
        name="route",
    )(spread)
    early, routed = lax.optimization_barrier((early, routed))
    halos = lax.all_to_all(routed, "dev", 0, 0)
    early, part_1 = one_block(1, stiff_1, early)

    half = shape(devs, 2, 2, pieces, size, 128)
    adjoint, keep, send = pl.pallas_call(
        functools.partial(outer_kernel, per),
        out_shape=(shape(slots, 3, nx, ny, nz), half, half),
        in_specs=[SMEM] * 5 + [VMEM] * 5 + [HBM],
        out_specs=(HBM, VMEM, VMEM),
        scratch_shapes=[
            pltpu.VMEM((faces, PLANES, ny, nz), F32),
            pltpu.VMEM((slots, 3, 2 * ENDS, ny, nz), F32),
            pltpu.VMEM((8 * (ny + 1), 128), F32),
            pltpu.VMEM((slots, LX * (ny + 1), 128), F32),
            pltpu.SemaphoreType.DMA((faces, 3)),
        ],
        input_output_aliases={10: 0},
        compiler_params=params(12),
        name="outer",
    )(
        dest,
        lengths,
        low,
        up,
        coord_x,
        halos,
        part_0,
        part_1,
        coord_y,
        coord_z,
        early,
    )

    scale = math.sqrt(LX * LY * LZ / (groups * devs * slots * nx * ny * nz))

    def small(kernel, outs, args, scratch=()):
        return pl.pallas_call(
            kernel,
            out_shape=outs,
            in_specs=[SMEM if a is dest else VMEM for a in args],
            out_specs=jax.tree.map(lambda _: VMEM, outs),
            scratch_shapes=scratch,
            compiler_params=params(8),
        )(*args)

    piece = (2, pieces, size, 128)
    if fast:
        lines = devs // 2
        body = pieces * size

        def move(value, to):
            links = []
            for g in range(groups):
                for d in range(devs):
                    c2, x2, y2, z2 = to(g % 2, g // 2, d % 2, d // 2)
                    links.append((g * devs + d, (x2 * 2 + c2) * devs + z2 * 2 + y2))
            return lax.ppermute(value, ("group", "dev"), links)

        flip_c = lambda c, x, y, z: (1 - c, x, y, z)
        flip_x = lambda c, x, y, z: (c, 1 - x, y, z)
        flip_y = lambda c, x, y, z: (c, x, 1 - y, z)
        flip_xc = lambda c, x, y, z: (1 - c, 1 - x, y, z)
        got = move(send, flip_c)
        view = (lines, 2, 2, 2, body, 128)
        part = shape(lines, 2, body, 128)
        keep_y, send_y, keep_x, send_x = small(
            core_kernel, (part,) * 4, (dest, keep.reshape(view), got.reshape(view))
        )
        got_y, got_x = move(send_y, flip_y), move(send_x, flip_x)
        part = shape(lines, body, 128)
        keep_0, send_0, keep_1, send_1 = small(
            plane_kernel, (part,) * 4, (dest, keep_y, got_y, keep_x, got_x)
        )
        got_0, got_1 = move(send_0, flip_x), move(send_1, flip_y)
        part = shape(2, body, 128)
        sums = small(line_kernel, (part,) * lines, (dest, keep_0, got_0, keep_1, got_1))
        terms = [sums[0]]
        for k in range(1, lines):
            terms.append(move(sums[k], lambda c, x, y, z, k=k: (c, x, y, (z + k) % lines)))
        own = small(functools.partial(sum_kernel, scale), part, tuple(terms))
        others = [move(own, to) for to in (flip_c, flip_x, flip_xc)]
        quarters = [v.reshape(piece) for v in (own, *others)]
    else:
        whole = jnp.stack([keep, send], axis=1).reshape(devs, -1, 128)
        owned = lax.psum_scatter(whole, "dev", scatter_dimension=0, tiled=True)
        owned = lax.psum(owned, "group") * scale
        owned = owned.reshape(2, 2, 2, pieces, size, 128)
        quarters = [owned[c, :, x] for x in range(2) for c in range(2)]
    lattice = small(
        functools.partial(unpack_kernel, per),
        shape(mine, 3 * LY * LZ),
        (dest, *quarters),
        [pltpu.VMEM((2, 2, *piece), F32)],
    )
    return adjoint, lattice


def solution(mesh):
    both = ("group", "dev")
    in_specs = (
        P(both, None, None, None, None),
        P(both, None, None, None),
        P(both),
        P(both, None),
        P(both, None),
        P(both, None),
        P(both, None),
        P(both, None),
    )
    out_specs = (P(both, None, None, None, None), P("dev", None))
    body = functools.partial(on_device, mesh.shape["group"], mesh.shape["dev"])
    return jax.shard_map(
        body, mesh=mesh, in_specs=in_specs, out_specs=out_specs, check_vma=False
    )
```

```python
import functools
import math

import jax
import jax.numpy as jnp
from jax import lax
from jax.experimental import pallas as pl
from jax.experimental.pallas import tpu as pltpu
from jax.sharding import PartitionSpec as P

LX = 96
LY = 64
LZ = 32
DOMINANCE = 1.25
PLANES = 8
STEP = 24
ENDS = 3
EDGES = 20

F32 = jnp.float32
BF16 = jnp.bfloat16
SMEM = pl.BlockSpec(memory_space=pltpu.SMEM)
VMEM = pl.BlockSpec(memory_space=pltpu.VMEM)
ANY = pl.BlockSpec(memory_space=pl.ANY)
HBM = pl.BlockSpec(memory_space=pltpu.HBM)


def place_of(fast):
    if not fast:
        return (jnp.int32(0),) * 4
    group, dev = lax.axis_index("group"), lax.axis_index("dev")
    halve = lambda v: lax.shift_right_logical(v, 1)
    return group & 1, halve(group), dev & 1, halve(dev)


def params(mib):
    return pltpu.CompilerParams(vmem_limit_bytes=mib * 1024 * 1024)


def neighbours(v, axis):
    extent = v.shape[axis]
    place = lax.broadcasted_iota(jnp.int32, v.shape, axis)
    up = jnp.where(place == 0, 0.0, pltpu.roll(v, 1, axis))
    down = jnp.where(place == extent - 1, 0.0, pltpu.roll(v, extent - 1, axis))
    return up + down


def plane_parts(v):
    along_z = neighbours(v, v.ndim - 1)
    first = v + 0.5 * along_z
    second = 0.5 * v + (1.0 / 3.0) * along_z
    beside = first + neighbours(second, v.ndim - 2)
    own = along_z + neighbours(first, v.ndim - 2)
    return beside, own


def padded_stencil(ref, lead, i, count):
    rows = ref.shape[-2] - 16
    planes = pl.ds(i, count + 2)
    v = ref[(*lead, planes, slice(8, 8 + rows))]
    t = ref[(*lead, planes, slice(7, 7 + rows))] + ref[(*lead, planes, slice(9, 9 + rows))]
    t_beside = t[:-2] + t[2:]
    near = t[1:-1] + (v[:-2] + v[2:])
    mixed = v[1:-1] + 0.5 * near + (1.0 / 3.0) * t_beside
    return v[1:-1], near + 0.5 * t_beside + neighbours(mixed, mixed.ndim - 1)


def split(v):
    high = v.astype(BF16)
    return high, (v - high.astype(F32)).astype(BF16)


def thrice(v, axis, data):
    high, low = split(v)
    parts = [high, low, high] if data else [high, high, low]
    return jnp.concatenate(parts, axis=axis)


def dot(a, b, contract_b=0):
    numbers = (((1,), (contract_b,)), ((), ()))
    return lax.dot_general(a, b, numbers, preferred_element_type=F32)


def pack_kernel(devs, slots, nx, ny, nz, len_in, low_in, up_in, seed_in, stiff_in, out_ref, *scratch):
    len_ref, low_ref, up_ref, seed_ref, stiff_ref, packet, sems = scratch
    rows = PLANES * ny
    chunk = rows // devs
    small = []
    for k, (src, dst) in enumerate(((len_in, len_ref), (low_in, low_ref), (up_in, up_ref))):
        small.append(pltpu.make_async_copy(src, dst, sems.at[0, k]))
        small[k].start()
    copies = {}

    def fetch(s, side):
        f = 2 * s + side
        start = [0, 0] if side == 0 else [len_ref[s] - 3, len_ref[s] - 2]
        copies[f] = (
            pltpu.make_async_copy(stiff_in.at[s, pl.ds(start[0], 3)], stiff_ref.at[f], sems.at[1, f]),
            pltpu.make_async_copy(seed_in.at[s, :, pl.ds(start[1], 2)], seed_ref.at[f], sems.at[2, f]),
        )
        for copy in copies[f]:
            copy.start()

    for s in range(slots):
        fetch(s, 0)
    small[0].wait()
    for s in range(slots):
        fetch(s, 1)
    small[1].wait()
    small[2].wait()
    wanted = []
    for s in range(slots):
        for side, ref in ((0, low_ref), (1, up_ref)):
            number = jnp.maximum(ref[s, 0], 0) * (2 * slots) + ref[s, 1] * 2 + (1 - side)
            wanted.append(number.astype(F32))
    row = lax.broadcasted_iota(jnp.int32, (8, nz), 0)
    note = jnp.zeros((8, nz), F32)
    for f, number in enumerate(wanted):
        note = jnp.where(row == f, number, note)
    for f in (0, 2, 1, 3):
        side = f % 2
        for copy in copies[f]:
            copy.wait()
        stiff = [stiff_ref[f, k if side == 0 else 2 - k] for k in range(3)]
        parts = [plane_parts(v) for v in stiff]
        inner = parts[0][1] + parts[1][0]
        next_near = parts[1][1] + parts[0][0] + parts[2][0]
        scale = 1.0 / (DOMINANCE * next_near)
        planes = [stiff[0], inner]
        planes += [seed_ref[f, c, side].astype(F32) for c in range(3)]
        for c in range(3):
            planes.append(plane_parts(seed_ref[f, c, 1 - side].astype(F32) * scale)[0])
        for k, plane in enumerate(planes):
            packet[f, k * ny : (k + 1) * ny] = plane
    for j in range(devs):
        for f in range(2 * slots):
            out_ref[j, f * chunk : (f + 1) * chunk] = packet[f, j * chunk : (j + 1) * chunk]
        out_ref[j, 2 * slots * chunk :] = note


def route_kernel(in_ref, out_ref):
    devs, rows, _ = out_ref.shape
    faces = 4
    chunk = rows // faces
    for e in range(devs):
        for f in range(faces):
            cell = in_ref[e, rows + f : rows + f + 1, 0:1]
            number = cell[0, 0].astype(jnp.int32)
            source = lax.shift_right_logical(number, 2)
            start = (number & 3) * chunk
            if chunk % 8 == 0:
                start = pl.multiple_of(start, 8)
            out_ref[e, f * chunk : (f + 1) * chunk] = in_ref[source, pl.ds(start, chunk)]


def hat_along_z(coord, nz):
    row = lax.broadcasted_iota(jnp.int32, (128, 3 * nz), 0)
    lane = lax.broadcasted_iota(jnp.int32, (128, 3 * nz), 1)
    point = (row % LZ).astype(F32)
    hat = jnp.maximum(0.0, 1.0 - jnp.abs(point - jnp.concatenate([coord] * 3, axis=1)))
    return thrice(jnp.where((row // LZ) == (lane // nz), hat, 0.0), 1, False)


class Planes:
    def __init__(self, ref, start, ny):
        self.ref, self.start, self.ny = ref, start, ny

    def rows(self, key):
        return pl.ds(self.start + (key[0] * EDGES + key[1]) * self.ny, self.ny)

    def __getitem__(self, key):
        return self.ref[self.rows(key)]

    def __setitem__(self, key, value):
        self.ref[self.rows(key)] = value


def block_kernel(b, len_ref, seed_in, stiff_in, cx_ref, cz_ref, *refs):
    s_ext, w_ext, v_ext, fac_ref, mul_ref, adj, seeds, zdone, sems = refs[-9:]
    adj_out, part_ref, *passed = refs[:3] if b == 0 else refs[1:3]
    nx, ny, nz = fac_ref.shape
    edge_ref = Planes(part_ref, LX * (ny + 1), ny)
    last = 8 + ny
    length = len_ref[b]
    loads = (
        pltpu.make_async_copy(
            stiff_in.at[0] if b == 0 else stiff_in, s_ext.at[pl.ds(1, nx), pl.ds(8, ny)], sems.at[0]
        ),
        pltpu.make_async_copy(seed_in.at[b], seeds, sems.at[1]),
    )
    for copy in loads:
        copy.start()
    if b == 0:
        ahead = pltpu.make_async_copy(stiff_in.at[1], passed[0], sems.at[3])
        ahead.start()
    zeros = jnp.zeros((nx + 2, 8, nz), F32)
    plane = jnp.zeros((ny, nz), F32)
    for ref, lead in ((s_ext, ()), *((r, (c,)) for r in (w_ext, v_ext) for c in range(3))):
        ref[(*lead, slice(None), slice(0, 8))] = zeros
        ref[(*lead, slice(None), slice(last, last + 8))] = zeros
        for i in (0, nx + 1):
            ref[(*lead, i, slice(8, last))] = plane
    hat_z = hat_along_z(cz_ref[b : b + 1, :], nz)
    line = lax.broadcasted_iota(jnp.int32, (LX, 3 * nx), 0).astype(F32)
    lane = lax.broadcasted_iota(jnp.int32, (LX, 3 * nx), 1)
    x = lane % nx
    coord = jnp.concatenate([cx_ref[b : b + 1, :]] * 3, axis=1)
    hat = jnp.maximum(0.0, 1.0 - jnp.abs(line - coord))
    hat = jnp.where(jnp.logical_and(x >= ENDS, x < length - ENDS), hat, 0.0)
    high, low = split(hat)
    hat_x = jnp.where(lane < 2 * nx, high.astype(F32), low.astype(F32)).astype(BF16)
    for copy in loads:
        copy.wait()

    def clear(i, _):
        s_ext[i + 1, 8:last] = plane
        return 0

    lax.fori_loop(length, nx, clear, 0)

    def loop(body):
        def step(k, _):
            body(k * STEP)
            return 0

        lax.fori_loop(0, nx // STEP, step, 0)

    def first(i):
        stiff, near = padded_stencil(s_ext, (), i, STEP)
        active = i + lax.broadcasted_iota(jnp.int32, (STEP, ny, nz), 0) < length
        safe = jnp.where(active, DOMINANCE * stiff * near, 1.0)
        inv = jnp.where(active, 1.0 / safe, 0.0)
        fac = stiff * inv
        fac_ref[pl.ds(i, STEP)] = fac
        mul_ref[pl.ds(i, STEP)] = stiff * fac
        for c in range(3):
            seed = seeds[c, pl.ds(i, STEP)].astype(F32)
            w_ext[c, pl.ds(i + 1, STEP), 8:last] = seed * fac
            adj[c, pl.ds(i, STEP)] = seed * inv

    loop(first)

    at = [[k if side == 0 else length - 1 - k for k in range(4)] for side in range(2)]
    for f in range(2):
        for c in range(3):
            edge_ref[f, 11 + c] = adj[c, at[f][1]]
            edge_ref[f, 14 + c] = adj[c, at[f][2]]

    def second(i):
        mul = mul_ref[pl.ds(i, STEP)]
        for c in range(3):
            here, near = padded_stencil(w_ext, (c,), i, STEP)
            v_ext[c, pl.ds(i + 1, STEP), 8:last] = here + mul * near

    loop(second)

    def third(i):
        fac = fac_ref[pl.ds(i, STEP)]
        for c in range(3):
            _, near = padded_stencil(v_ext, (c,), i, STEP)
            adj[c, pl.ds(i, STEP)] += fac * near

    loop(third)
    store = pltpu.make_async_copy(adj, adj_out.at[b], sems.at[2])
    store.start()

    def parts(ref, *lead):
        v = ref[(*lead, slice(8, last))]
        t = ref[(*lead, slice(7, last - 1))] + ref[(*lead, slice(9, last + 1))]
        own = t + neighbours(v + 0.5 * t, 1)
        return v + 0.5 * t + neighbours(0.5 * v + (1.0 / 3.0) * t, 1), own

    for f in range(2):
        edge_ref[f, 0] = s_ext[at[f][0] + 1, 8:last]
        edge_ref[f, 1] = parts(s_ext, at[f][0] + 1)[1] + parts(s_ext, at[f][1] + 1)[0]
        mul_1, fac_1, fac_2 = mul_ref[at[f][1]], fac_ref[at[f][1]], fac_ref[at[f][2]]
        edge_ref[f, 17], edge_ref[f, 18], edge_ref[f, 19] = mul_1, fac_1, fac_2
        for c in range(3):
            edge_ref[f, 2 + c] = seeds[c, at[f][0]].astype(F32)
            beside, own = parts(w_ext, c, at[f][1] + 1)
            edge_ref[f, 5 + c] = beside
            own = own + parts(w_ext, c, at[f][2] + 1)[0]
            edge_ref[f, 8 + c] = w_ext[c, at[f][1] + 1, 8:last] + mul_1 * own
            beside, own = parts(v_ext, c, at[f][2] + 1)
            edge_ref[f, 11 + c] += fac_1 * beside
            edge_ref[f, 14 + c] += fac_2 * (own + parts(v_ext, c, at[f][3] + 1)[0])

    group = 16
    pitch = ny + 1
    for x in range(0, nx, group):
        rows = [adj[c, x : x + group].reshape(group * ny, nz) for c in range(3)]
        done = dot(thrice(jnp.concatenate(rows, axis=1), 1, True), hat_z, 1)
        for k in range(group):
            zdone[(x + k) * pitch : (x + k) * pitch + ny] = done[k * ny : (k + 1) * ny]
    for y in range(0, ny, 2):
        part = [zdone[pl.ds(y + k, nx, stride=pitch), :] for k in range(2)]
        done = dot(hat_x, thrice(jnp.concatenate(part, axis=1), 0, True))
        for k in range(2):
            part_ref[pl.ds(y + k, LX, stride=pitch), :] = done[:, 128 * k : 128 * (k + 1)]
    store.wait()
    if b == 0:
        ahead.wait()


def outer_kernel(
    fast,
    per,
    len_ref,
    low_ref,
    up_ref,
    cx_ref,
    halo_ref,
    part_0,
    part_1,
    cy_ref,
    cz_ref,
    adj_in,
    adj_out,
    keep_ref,
    send_ref,
    pack,
    ends,
    zdone,
    xdone,
    sems,
):
    del adj_in
    slots = 2
    faces = 2 * slots
    _, _, _, ny, nz = ends.shape
    pitch = ny + 1
    chunk = halo_ref.shape[1] // faces
    zero_plane = jnp.zeros((ny, nz), F32)

    for s in range(slots):
        for side, ref in ((0, low_ref), (1, up_ref)):
            f = 2 * s + side
            wall = ref[s, 0] < 0
            turned = ref[s, 2] == 1

            def place(reverse, f=f):
                for k in range(PLANES):
                    for r in range(ny):
                        at = k * ny + r
                        to = ny - 1 - r if reverse else r
                        j, o = at // chunk, at % chunk
                        pack[f, k, to : to + 1] = halo_ref[j, f * chunk + o : f * chunk + o + 1]

            @pl.when(wall)
            def _(f=f):
                for k in range(PLANES):
                    pack[f, k] = zero_plane

            @pl.when(jnp.logical_and(jnp.logical_not(wall), turned))
            def _(place=place):
                place(True)

            @pl.when(jnp.logical_and(jnp.logical_not(wall), jnp.logical_not(turned)))
            def _(place=place):
                place(False)

    copies = []
    for f in range(faces):
        b, side = f // 2, f % 2
        edge = Planes((part_0, part_1)[b], LX * pitch, ny)
        stiff, inside = edge[side, 0], edge[side, 1]
        beside = plane_parts(stiff)[0]
        there = 1.0 / (DOMINANCE * (pack[f, 1] + beside))
        inv = 1.0 / (DOMINANCE * stiff * (inside + plane_parts(pack[f, 0])[0]))
        fac = stiff * inv
        mul_1, fac_1, fac_2 = edge[side, 17], edge[side, 18], edge[side, 19]
        for c in range(3):
            seed = edge[side, 2 + c]
            w_n = pack[f, 2 + c] * there
            w_0 = seed * fac
            beside_n, own_n = plane_parts(w_n)
            beside_0, own_0 = plane_parts(w_0)
            v_n = w_n + pack[f, 0] * there * (own_n + pack[f, 5 + c] + beside_0)
            v_0 = w_0 + stiff * fac * (own_0 + edge[side, 5 + c] + beside_n)
            v_1 = edge[side, 8 + c] + mul_1 * beside_0
            beside_n = plane_parts(v_n)[0]
            beside_0, own_0 = plane_parts(v_0)
            beside_1, own_1 = plane_parts(v_1)
            rows = [
                seed * inv + fac * (own_0 + beside_1 + beside_n),
                edge[side, 11 + c] + fac_1 * (own_1 + beside_0),
                edge[side, 14 + c] + fac_2 * beside_1,
            ]
            for k, row in enumerate(rows):
                ends[b, c, k if side == 0 else 2 * ENDS - 1 - k] = row
            start = 0 if side == 0 else len_ref[b] - ENDS
            copy = pltpu.make_async_copy(
                ends.at[b, c, pl.ds(side * ENDS, ENDS)],
                adj_out.at[b, c, pl.ds(start, ENDS)],
                sems.at[f, c],
            )
            copy.start()
            copies.append(copy)

    eight = 8
    line = lax.broadcasted_iota(jnp.int32, (LX, 4 * eight), 0).astype(F32)
    lane = lax.broadcasted_iota(jnp.int32, (LX, 4 * eight), 1)
    for b in range(slots):
        hat_z = hat_along_z(cz_ref[b : b + 1, :], nz)
        rows = [ends[b, c].reshape(2 * ENDS * ny, nz) for c in range(3)]
        done = dot(thrice(jnp.concatenate(rows, axis=1), 1, True), hat_z, 1)
        for k in range(eight):
            rows = done[k * ny : (k + 1) * ny] if k < 2 * ENDS else jnp.zeros((ny, 128), F32)
            zdone[k * pitch : k * pitch + ny] = rows
        coord = jnp.full((LX, 4 * eight), -4.0, F32)
        for k in range(2 * ENDS):
            at = k if k < ENDS else len_ref[b] - 2 * ENDS + k
            coord = jnp.where(lane % eight == k, cx_ref[b, at], coord)
        hat = jnp.maximum(0.0, 1.0 - jnp.abs(line - coord))
        high, low = split(hat)
        hat_x = jnp.where(lane < 2 * eight, high.astype(F32), low.astype(F32)).astype(BF16)
        for y in range(0, ny, 2):
            part = [zdone[pl.ds(y + k, eight, stride=pitch), :] for k in range(2)]
            high, low = split(jnp.concatenate(part, axis=1))
            high, low = high.astype(F32), low.astype(F32)
            stack = jnp.concatenate([high, low, high, jnp.zeros_like(high)], axis=0)
            done = dot(hat_x, stack.astype(BF16))
            for k in range(2):
                xdone[b, pl.ds(y + k, LX, stride=pitch), :] = done[:, 128 * k : 128 * (k + 1)]

    depth = per * slots * ny
    row = lax.broadcasted_iota(jnp.int32, (LY * per, depth), 0).astype(F32)
    lane = lax.broadcasted_iota(jnp.int32, (LY * per, depth), 1).astype(F32)
    which = jnp.floor((row + 0.5) * (1.0 / per))
    inside = row - which * per
    owner = jnp.floor((lane + 0.5) * (1.0 / (slots * ny)))
    coord = jnp.concatenate([cy_ref[b : b + 1, :] for b in range(slots)] * per, axis=1)
    hat_y = jnp.maximum(0.0, 1.0 - jnp.abs(which - coord))
    hat_y = thrice(jnp.where(inside == owner, hat_y, 0.0), 1, False)
    third_rows = LY // 4 * per
    pieces = keep_ref.shape[3]
    size = 3 * third_rows // 8
    tail = lax.broadcasted_iota(jnp.int32, (third_rows, 128), 1) >= 3 * LZ
    even = place_of(fast)[0] == 0
    for pair in range(LX // per // 2):
        terms = []
        for number in (2 * pair, 2 * pair + 1):
            rows = []
            for line in range(number * per, (number + 1) * per):
                at = slice(line * pitch, line * pitch + ny)
                rows += [part_0[at] + xdone[0, at], part_1[at] + xdone[1, at]]
            terms.append(jnp.concatenate(rows, axis=0))
        both = dot(hat_y, thrice(jnp.concatenate(terms, axis=1), 0, True))
        for k in range(2):
            done = both[:, 128 * k : 128 * (k + 1)]
            tops = done[3 * third_rows :]
            dense = []
            for q in range(3):
                moved = pltpu.roll(tops, 3 * LZ - q * LZ, 1)
                dense.append(jnp.where(tail, moved, done[q * third_rows : (q + 1) * third_rows]))
            dense = jnp.concatenate(dense, axis=0)
            number = 2 * pair + k
            d, t = number // pieces, number % pieces
            for g in range(4):
                first = dense[g * size : (g + 1) * size]
                second = dense[(g + 4) * size : (g + 5) * size]
                keep_ref[d, g // 2, g % 2, t] = jnp.where(even, first, second)
                send_ref[d, g // 2, g % 2, t] = jnp.where(even, second, first)
    for copy in copies:
        copy.wait()


def core_kernel(keep_ref, got_ref, keep_y, send_y, keep_x, send_x):
    _, x, y, _ = place_of(True)
    keep_y[...] = keep_ref[:, y, 0] + got_ref[:, y, 0]
    send_y[...] = keep_ref[:, 1 - y, 0] + got_ref[:, 1 - y, 0]
    keep_x[...] = keep_ref[:, :, 1, x] + got_ref[:, :, 1, x]
    send_x[...] = keep_ref[:, :, 1, 1 - x] + got_ref[:, :, 1, 1 - x]


def plane_kernel(keep_y, got_y, keep_x, got_x, keep_0, send_0, keep_1, send_1):
    _, x, y, _ = place_of(True)
    keep_0[...] = keep_y[:, x] + got_y[:, x]
    send_0[...] = keep_y[:, 1 - x] + got_y[:, 1 - x]
    keep_1[...] = keep_x[:, y] + got_x[:, y]
    send_1[...] = keep_x[:, 1 - y] + got_x[:, 1 - y]


def line_kernel(keep_0, got_0, keep_1, got_1, *outs):
    z = place_of(True)[3]
    count = len(outs)
    for k, out in enumerate(outs):
        at = lax.rem(z + k, count)
        out[0] = keep_0[at] + got_0[at]
        out[1] = keep_1[at] + got_1[at]


def sum_kernel(scale, *refs):
    total = refs[0][...]
    for ref in refs[1:-1]:
        total = total + ref[...]
    refs[-1][...] = total * scale


def unpack_kernel(fast, per, own, got_c, got_x, got_xc, out_ref, lines):
    core, x, _, _ = place_of(fast)
    parts, count, size, _ = own.shape
    runs = size // per
    given = ((own, core, x), (got_c, 1 - core, x), (got_x, core, 1 - x), (got_xc, 1 - core, 1 - x))
    for ref, c, u in given:
        for p in range(parts):
            for t in range(count):
                for k in range(runs):
                    at = ((c * parts + p) * 2 + u) * runs + k
                    lines[at, t * per : (t + 1) * per] = ref[p, t, k * per : (k + 1) * per]
    rows = count * per
    lane = lax.broadcasted_iota(jnp.int32, (rows, 128), 1)
    front = lane < 2 * LZ
    even = (lane // LZ) % 2 == 0
    tiles = LY // 4
    groups = lines.shape[0] // 4
    per_c = groups // 3
    for g in range(groups):
        v = [lines[4 * g + k] for k in range(4)]
        a = [jnp.where(front, v[k], pltpu.roll(v[k + 2], 2 * LZ, 1)) for k in range(2)]
        b = [jnp.where(front, pltpu.roll(v[k], 2 * LZ, 1), v[k + 2]) for k in range(2)]
        turned = []
        for p, q in (a, b):
            turned.append(jnp.where(even, p, pltpu.roll(q, LZ, 1)))
            turned.append(jnp.where(even, pltpu.roll(p, 128 - LZ, 1), q))
        for c in range(3):
            at = (c * tiles + g) * 128
            out_ref[:, at : at + 128] = turned[c]
        at = (g // per_c * tiles + groups + g % per_c) * 128
        out_ref[:, at : at + 128] = turned[3]


def on_device(groups, devs, seed, stiff, lengths, low, up, coord_x, coord_y, coord_z):
    slots, nx, ny, nz = stiff.shape
    faces = 2 * slots
    chunk = PLANES * ny // devs
    rows = faces * chunk
    mine = LX // devs
    per = 4 if mine % 4 == 0 else mine
    pieces = mine // per
    size = 3 * LY // 4 // 8 * per
    fast = groups == 4 and devs % 2 == 0 and size % 8 == 0
    shape = lambda *dims: jax.ShapeDtypeStruct(dims, F32)

    packed = pl.pallas_call(
        functools.partial(pack_kernel, devs, slots, nx, ny, nz),
        out_shape=shape(devs, rows + 8, nz),
        in_specs=[HBM] * 5,
        out_specs=VMEM,
        scratch_shapes=[
            pltpu.SMEM((slots,), jnp.int32),
            pltpu.SMEM((slots, 3), jnp.int32),
            pltpu.SMEM((slots, 3), jnp.int32),
            pltpu.VMEM((faces, 3, 2, ny, nz), seed.dtype),
            pltpu.VMEM((faces, 3, ny, nz), F32),
            pltpu.VMEM((faces, PLANES * ny, nz), F32),
            pltpu.SemaphoreType.DMA((3, faces)),
        ],
        compiler_params=params(60),
        name="pack",
    )(lengths, low, up, seed, stiff)
    spread = lax.all_to_all(packed, "dev", 0, 0)
    ext = (nx + 2, ny + 16, nz)
    plain = pltpu.VMEM((nx, ny, nz), F32)

    def one_block(b, stiff, *given):
        return pl.pallas_call(
            functools.partial(block_kernel, b),
            out_shape=(
                shape(slots, 3, nx, ny, nz),
                shape(LX * (ny + 1) + 2 * EDGES * ny, 128),
                *([shape(nx, ny, nz)] if b == 0 else []),
            ),
            in_specs=[SMEM, ANY, ANY, VMEM, VMEM] + [HBM] * len(given),
            out_specs=(HBM, VMEM, VMEM) if b == 0 else (HBM, VMEM),
            scratch_shapes=[
                pltpu.VMEM(ext, F32),
                pltpu.VMEM((3, *ext), F32),
                pltpu.VMEM((3, *ext), F32),
                plain,
                plain,
                pltpu.VMEM((3, nx, ny, nz), F32),
                pltpu.VMEM((3, nx, ny, nz), seed.dtype),
                pltpu.VMEM((nx * (ny + 1), 128), F32),
                pltpu.SemaphoreType.DMA((4,)),
            ],
            input_output_aliases={5: 0} if given else {},
            compiler_params=params(12),
            cost_estimate=pl.CostEstimate(
                flops=3 * 10**9, bytes_accessed=10**7, transcendentals=0
            ),
            name=f"block_{b}",
        )(lengths, seed, stiff, coord_x, coord_z, *given)

    early, part_0, stiff_1 = one_block(0, stiff)
    routed = pl.pallas_call(
        route_kernel,
        out_shape=shape(devs, rows, nz),
        in_specs=[VMEM],
        out_specs=VMEM,
        compiler_params=params(4),
        name="route",
    )(spread)
    early, routed = lax.optimization_barrier((early, routed))
    halos = lax.all_to_all(routed, "dev", 0, 0)
    early, part_1 = one_block(1, stiff_1, early)

    half = shape(devs, 2, 2, pieces, size, 128)
    adjoint, keep, send = pl.pallas_call(
        functools.partial(outer_kernel, fast, per),
        out_shape=(shape(slots, 3, nx, ny, nz), half, half),
        in_specs=[SMEM] * 4 + [VMEM] * 5 + [HBM],
        out_specs=(HBM, VMEM, VMEM),
        scratch_shapes=[
            pltpu.VMEM((faces, PLANES, ny, nz), F32),
            pltpu.VMEM((slots, 3, 2 * ENDS, ny, nz), F32),
            pltpu.VMEM((8 * (ny + 1), 128), F32),
            pltpu.VMEM((slots, LX * (ny + 1), 128), F32),
            pltpu.SemaphoreType.DMA((faces, 3)),
        ],
        input_output_aliases={9: 0},
        compiler_params=params(12),
        name="outer",
    )(
        lengths,
        low,
        up,
        coord_x,
        halos,
        part_0,
        part_1,
        coord_y,
        coord_z,
        early,
    )

    scale = math.sqrt(LX * LY * LZ / (groups * devs * slots * nx * ny * nz))

    def small(kernel, outs, args, scratch=()):
        return pl.pallas_call(
            kernel,
            out_shape=outs,
            in_specs=[VMEM] * len(args),
            out_specs=jax.tree.map(lambda _: VMEM, outs),
            scratch_shapes=scratch,
            compiler_params=params(8),
        )(*args)

    piece = (2, pieces, size, 128)
    if fast:
        lines = devs // 2
        body = pieces * size

        def move(value, to):
            links = []
            for g in range(groups):
                for d in range(devs):
                    c2, x2, y2, z2 = to(g % 2, g // 2, d % 2, d // 2)
                    links.append((g * devs + d, (x2 * 2 + c2) * devs + z2 * 2 + y2))
            return lax.ppermute(value, ("group", "dev"), links)

        flip_c = lambda c, x, y, z: (1 - c, x, y, z)
        flip_x = lambda c, x, y, z: (c, 1 - x, y, z)
        flip_y = lambda c, x, y, z: (c, x, 1 - y, z)
        flip_xc = lambda c, x, y, z: (1 - c, 1 - x, y, z)
        got = move(send, flip_c)
        view = (lines, 2, 2, 2, body, 128)
        part = shape(lines, 2, body, 128)
        keep_y, send_y, keep_x, send_x = small(
            core_kernel, (part,) * 4, (keep.reshape(view), got.reshape(view))
        )
        got_y, got_x = move(send_y, flip_y), move(send_x, flip_x)
        part = shape(lines, body, 128)
        keep_0, send_0, keep_1, send_1 = small(
            plane_kernel, (part,) * 4, (keep_y, got_y, keep_x, got_x)
        )
        got_0, got_1 = move(send_0, flip_x), move(send_1, flip_y)
        part = shape(2, body, 128)
        sums = small(line_kernel, (part,) * lines, (keep_0, got_0, keep_1, got_1))
        terms = [sums[0]]
        for k in range(1, lines):
            terms.append(move(sums[k], lambda c, x, y, z, k=k: (c, x, y, (z + k) % lines)))
        own = small(functools.partial(sum_kernel, scale), part, tuple(terms))
        others = [move(own, to) for to in (flip_c, flip_x, flip_xc)]
        quarters = [v.reshape(piece) for v in (own, *others)]
    else:
        whole = jnp.stack([keep, send], axis=1).reshape(devs, -1, 128)
        owned = lax.psum_scatter(whole, "dev", scatter_dimension=0, tiled=True)
        owned = lax.psum(owned, "group") * scale
        owned = owned.reshape(2, 2, 2, pieces, size, 128)
        quarters = [owned[c, :, x] for x in range(2) for c in range(2)]
    lattice = small(
        functools.partial(unpack_kernel, fast, per),
        shape(mine, 3 * LY * LZ),
        tuple(quarters),
        [pltpu.VMEM((3 * LY // 4, mine, 128), F32)],
    )
    return adjoint, lattice


def solution(mesh):
    both = ("group", "dev")
    in_specs = (
        P(both, None, None, None, None),
        P(both, None, None, None),
        P(both),
        P(both, None),
        P(both, None),
        P(both, None),
        P(both, None),
        P(both, None),
    )
    out_specs = (P(both, None, None, None, None), P("dev", None))
    body = functools.partial(on_device, mesh.shape["group"], mesh.shape["dev"])
    return jax.shard_map(
        body, mesh=mesh, in_specs=in_specs, out_specs=out_specs, check_vma=False
    )
```

```python
import functools
import math

import jax
import jax.numpy as jnp
from jax import lax
from jax.experimental import pallas as pl
from jax.experimental.pallas import tpu as pltpu
from jax.sharding import PartitionSpec as P

LX = 96
LY = 64
LZ = 32
DOMINANCE = 1.25
PLANES = 8
STEP = 24
ENDS = 3
EDGES = 20

F32 = jnp.float32
BF16 = jnp.bfloat16
SMEM = pl.BlockSpec(memory_space=pltpu.SMEM)
VMEM = pl.BlockSpec(memory_space=pltpu.VMEM)
ANY = pl.BlockSpec(memory_space=pl.ANY)
HBM = pl.BlockSpec(memory_space=pltpu.HBM)


def place_of(fast):
    if not fast:
        return (jnp.int32(0),) * 4
    group, dev = lax.axis_index("group"), lax.axis_index("dev")
    halve = lambda v: lax.shift_right_logical(v, 1)
    return group & 1, halve(group), dev & 1, halve(dev)


def params(mib):
    return pltpu.CompilerParams(vmem_limit_bytes=mib * 1024 * 1024)


def neighbours(v, axis):
    extent = v.shape[axis]
    place = lax.broadcasted_iota(jnp.int32, v.shape, axis)
    up = jnp.where(place == 0, 0.0, pltpu.roll(v, 1, axis))
    down = jnp.where(place == extent - 1, 0.0, pltpu.roll(v, extent - 1, axis))
    return up + down


def plane_parts(v):
    along_z = neighbours(v, v.ndim - 1)
    first = v + 0.5 * along_z
    second = 0.5 * v + (1.0 / 3.0) * along_z
    beside = first + neighbours(second, v.ndim - 2)
    own = along_z + neighbours(first, v.ndim - 2)
    return beside, own


def padded_stencil(ref, lead, i, count):
    rows = ref.shape[-2] - 16
    planes = pl.ds(i, count + 2)
    v = ref[(*lead, planes, slice(8, 8 + rows))]
    t = ref[(*lead, planes, slice(7, 7 + rows))] + ref[(*lead, planes, slice(9, 9 + rows))]
    t_beside = t[:-2] + t[2:]
    near = t[1:-1] + (v[:-2] + v[2:])
    mixed = v[1:-1] + 0.5 * near + (1.0 / 3.0) * t_beside
    return v[1:-1], near + 0.5 * t_beside + neighbours(mixed, mixed.ndim - 1)


def split(v):
    high = v.astype(BF16)
    return high, (v - high.astype(F32)).astype(BF16)


def thrice(v, axis, data):
    high, low = split(v)
    parts = [high, low, high] if data else [high, high, low]
    return jnp.concatenate(parts, axis=axis)


def dot(a, b, contract_b=0):
    numbers = (((1,), (contract_b,)), ((), ()))
    return lax.dot_general(a, b, numbers, preferred_element_type=F32)


def pack_kernel(devs, slots, nx, ny, nz, len_in, low_in, up_in, seed_in, stiff_in, out_ref, *scratch):
    len_ref, low_ref, up_ref, seed_ref, stiff_ref, packet, sems = scratch
    rows = PLANES * ny
    chunk = rows // devs
    small = []
    for k, (src, dst) in enumerate(((len_in, len_ref), (low_in, low_ref), (up_in, up_ref))):
        small.append(pltpu.make_async_copy(src, dst, sems.at[0, k]))
        small[k].start()
    copies = {}

    base = nx // 2 - 3

    for s in range(slots):
        for side in range(2):
            f = 2 * s + side
            at = pl.ds(0, 3) if side == 0 else pl.ds(base, nx - base)
            to = pl.ds(0, 3 if side == 0 else nx - base)
            copies[f] = (
                pltpu.make_async_copy(stiff_in.at[s, at], stiff_ref.at[f, to], sems.at[1, f]),
                pltpu.make_async_copy(seed_in.at[s, :, at], seed_ref.at[f, :, to], sems.at[2, f]),
            )
            for copy in copies[f]:
                copy.start()
    small[0].wait()
    small[1].wait()
    small[2].wait()
    wanted = []
    for s in range(slots):
        for side, ref in ((0, low_ref), (1, up_ref)):
            number = jnp.maximum(ref[s, 0], 0) * (2 * slots) + ref[s, 1] * 2 + (1 - side)
            wanted.append(number.astype(F32))
    row = lax.broadcasted_iota(jnp.int32, (8, nz), 0)
    note = jnp.zeros((8, nz), F32)
    for f, number in enumerate(wanted):
        note = jnp.where(row == f, number, note)
    for f in (0, 2, 1, 3):
        side = f % 2
        for copy in copies[f]:
            copy.wait()
        at = [k if side == 0 else len_ref[f // 2] - 1 - k - base for k in range(3)]
        stiff = [stiff_ref[f, i] for i in at]
        parts = [plane_parts(v) for v in stiff]
        inner = parts[0][1] + parts[1][0]
        next_near = parts[1][1] + parts[0][0] + parts[2][0]
        scale = 1.0 / (DOMINANCE * next_near)
        planes = [stiff[0], inner]
        planes += [seed_ref[f, c, at[0]].astype(F32) for c in range(3)]
        for c in range(3):
            planes.append(plane_parts(seed_ref[f, c, at[1]].astype(F32) * scale)[0])
        for k, plane in enumerate(planes):
            packet[f, k * ny : (k + 1) * ny] = plane
    for j in range(devs):
        for f in range(2 * slots):
            out_ref[j, f * chunk : (f + 1) * chunk] = packet[f, j * chunk : (j + 1) * chunk]
        out_ref[j, 2 * slots * chunk :] = note


def route_kernel(in_ref, out_ref):
    devs, rows, _ = out_ref.shape
    faces = 4
    chunk = rows // faces
    for e in range(devs):
        for f in range(faces):
            cell = in_ref[e, rows + f : rows + f + 1, 0:1]
            number = cell[0, 0].astype(jnp.int32)
            source = lax.shift_right_logical(number, 2)
            start = (number & 3) * chunk
            if chunk % 8 == 0:
                start = pl.multiple_of(start, 8)
            out_ref[e, f * chunk : (f + 1) * chunk] = in_ref[source, pl.ds(start, chunk)]


def hat_along_z(coord, nz):
    row = lax.broadcasted_iota(jnp.int32, (128, 3 * nz), 0)
    lane = lax.broadcasted_iota(jnp.int32, (128, 3 * nz), 1)
    point = (row % LZ).astype(F32)
    hat = jnp.maximum(0.0, 1.0 - jnp.abs(point - jnp.concatenate([coord] * 3, axis=1)))
    return thrice(jnp.where((row // LZ) == (lane // nz), hat, 0.0), 1, False)


class Planes:
    def __init__(self, ref, start, ny):
        self.ref, self.start, self.ny = ref, start, ny

    def rows(self, key):
        return pl.ds(self.start + (key[0] * EDGES + key[1]) * self.ny, self.ny)

    def __getitem__(self, key):
        return self.ref[self.rows(key)]

    def __setitem__(self, key, value):
        self.ref[self.rows(key)] = value


def block_kernel(b, len_ref, seed_in, stiff_in, cx_ref, cz_ref, *refs):
    s_ext, w_ext, v_ext, fac_ref, mul_ref, adj, seeds, zdone, sems = refs[-9:]
    adj_out, part_ref, edge_out, *passed = refs[:4] if b == 0 else refs[1:4]
    nx, ny, nz = fac_ref.shape
    edge_ref = Planes(edge_out, 0, ny)
    last = 8 + ny
    length = len_ref[b]
    loads = (
        pltpu.make_async_copy(
            stiff_in.at[0] if b == 0 else stiff_in, s_ext.at[pl.ds(1, nx), pl.ds(8, ny)], sems.at[0]
        ),
        pltpu.make_async_copy(seed_in.at[b], seeds, sems.at[1]),
    )
    for copy in loads:
        copy.start()
    if b == 0:
        ahead = pltpu.make_async_copy(stiff_in.at[1], passed[0], sems.at[3])
        ahead.start()
    zeros = jnp.zeros((nx + 2, 8, nz), F32)
    plane = jnp.zeros((ny, nz), F32)
    for ref, lead in ((s_ext, ()), *((r, (c,)) for r in (w_ext, v_ext) for c in range(3))):
        ref[(*lead, slice(None), slice(0, 8))] = zeros
        ref[(*lead, slice(None), slice(last, last + 8))] = zeros
        for i in (0, nx + 1):
            ref[(*lead, i, slice(8, last))] = plane
    hat_z = hat_along_z(cz_ref[b : b + 1, :], nz)
    line = lax.broadcasted_iota(jnp.int32, (LX, 3 * nx), 0).astype(F32)
    lane = lax.broadcasted_iota(jnp.int32, (LX, 3 * nx), 1)
    x = lane % nx
    coord = jnp.concatenate([cx_ref[b : b + 1, :]] * 3, axis=1)
    hat = jnp.maximum(0.0, 1.0 - jnp.abs(line - coord))
    hat = jnp.where(jnp.logical_and(x >= ENDS, x < length - ENDS), hat, 0.0)
    high, low = split(hat)
    hat_x = jnp.where(lane < 2 * nx, high.astype(F32), low.astype(F32)).astype(BF16)
    for copy in loads:
        copy.wait()

    def clear(i, _):
        s_ext[i + 1, 8:last] = plane
        return 0

    lax.fori_loop(length, nx, clear, 0)

    def loop(body):
        def step(k, _):
            body(k * STEP)
            return 0

        lax.fori_loop(0, nx // STEP, step, 0)

    def first(i):
        stiff, near = padded_stencil(s_ext, (), i, STEP)
        active = i + lax.broadcasted_iota(jnp.int32, (STEP, ny, nz), 0) < length
        safe = jnp.where(active, DOMINANCE * stiff * near, 1.0)
        inv = jnp.where(active, 1.0 / safe, 0.0)
        fac = stiff * inv
        fac_ref[pl.ds(i, STEP)] = fac
        mul_ref[pl.ds(i, STEP)] = stiff * fac
        for c in range(3):
            seed = seeds[c, pl.ds(i, STEP)].astype(F32)
            w_ext[c, pl.ds(i + 1, STEP), 8:last] = seed * fac
            adj[c, pl.ds(i, STEP)] = seed * inv

    loop(first)

    at = [[k if side == 0 else length - 1 - k for k in range(4)] for side in range(2)]
    for f in range(2):
        for c in range(3):
            edge_ref[f, 11 + c] = adj[c, at[f][1]]
            edge_ref[f, 14 + c] = adj[c, at[f][2]]

    def second(i):
        mul = mul_ref[pl.ds(i, STEP)]
        for c in range(3):
            here, near = padded_stencil(w_ext, (c,), i, STEP)
            v_ext[c, pl.ds(i + 1, STEP), 8:last] = here + mul * near

    loop(second)

    def third(i):
        fac = fac_ref[pl.ds(i, STEP)]
        for c in range(3):
            _, near = padded_stencil(v_ext, (c,), i, STEP)
            adj[c, pl.ds(i, STEP)] += fac * near

    loop(third)
    store = pltpu.make_async_copy(adj, adj_out.at[b], sems.at[2])
    store.start()

    def parts(ref, *lead):
        v = ref[(*lead, slice(8, last))]
        t = ref[(*lead, slice(7, last - 1))] + ref[(*lead, slice(9, last + 1))]
        own = t + neighbours(v + 0.5 * t, 1)
        return v + 0.5 * t + neighbours(0.5 * v + (1.0 / 3.0) * t, 1), own

    for f in range(2):
        edge_ref[f, 0] = s_ext[at[f][0] + 1, 8:last]
        edge_ref[f, 1] = parts(s_ext, at[f][0] + 1)[1] + parts(s_ext, at[f][1] + 1)[0]
        mul_1, fac_1, fac_2 = mul_ref[at[f][1]], fac_ref[at[f][1]], fac_ref[at[f][2]]
        edge_ref[f, 17], edge_ref[f, 18], edge_ref[f, 19] = mul_1, fac_1, fac_2
        for c in range(3):
            edge_ref[f, 2 + c] = seeds[c, at[f][0]].astype(F32)
            beside, own = parts(w_ext, c, at[f][1] + 1)
            edge_ref[f, 5 + c] = beside
            own = own + parts(w_ext, c, at[f][2] + 1)[0]
            edge_ref[f, 8 + c] = w_ext[c, at[f][1] + 1, 8:last] + mul_1 * own
            beside, own = parts(v_ext, c, at[f][2] + 1)
            edge_ref[f, 11 + c] += fac_1 * beside
            edge_ref[f, 14 + c] += fac_2 * (own + parts(v_ext, c, at[f][3] + 1)[0])

    group = 16
    pitch = ny + 1
    for x in range(0, nx, group):
        rows = [adj[c, x : x + group].reshape(group * ny, nz) for c in range(3)]
        done = dot(thrice(jnp.concatenate(rows, axis=1), 1, True), hat_z, 1)
        for k in range(group):
            zdone[(x + k) * pitch : (x + k) * pitch + ny] = done[k * ny : (k + 1) * ny]
    for y in range(0, ny, 2):
        part = [zdone[pl.ds(y + k, nx, stride=pitch), :] for k in range(2)]
        done = dot(hat_x, thrice(jnp.concatenate(part, axis=1), 0, True))
        for k in range(2):
            part_ref[pl.ds(y + k, LX, stride=pitch), :] = done[:, 128 * k : 128 * (k + 1)]
    store.wait()
    if b == 0:
        ahead.wait()


def ends_kernel(
    len_ref,
    low_ref,
    up_ref,
    cx_ref,
    halo_ref,
    edge_0,
    edge_1,
    cz_ref,
    adj_in,
    adj_out,
    xdone,
    pack,
    ends,
    zdone,
    sems,
):
    del adj_in
    slots = 2
    faces = 2 * slots
    _, _, _, ny, nz = ends.shape
    pitch = ny + 1
    chunk = halo_ref.shape[1] // faces
    zero_plane = jnp.zeros((ny, nz), F32)

    for s in range(slots):
        for side, ref in ((0, low_ref), (1, up_ref)):
            f = 2 * s + side
            wall = ref[s, 0] < 0
            turned = ref[s, 2] == 1

            def place(reverse, f=f):
                for k in range(PLANES):
                    for r in range(ny):
                        at = k * ny + r
                        to = ny - 1 - r if reverse else r
                        j, o = at // chunk, at % chunk
                        pack[f, k, to : to + 1] = halo_ref[j, f * chunk + o : f * chunk + o + 1]

            @pl.when(wall)
            def _(f=f):
                for k in range(PLANES):
                    pack[f, k] = zero_plane

            @pl.when(jnp.logical_and(jnp.logical_not(wall), turned))
            def _(place=place):
                place(True)

            @pl.when(jnp.logical_and(jnp.logical_not(wall), jnp.logical_not(turned)))
            def _(place=place):
                place(False)

    copies = []
    for f in range(faces):
        b, side = f // 2, f % 2
        edge = Planes((edge_0, edge_1)[b], 0, ny)
        stiff, inside = edge[side, 0], edge[side, 1]
        beside = plane_parts(stiff)[0]
        there = 1.0 / (DOMINANCE * (pack[f, 1] + beside))
        inv = 1.0 / (DOMINANCE * stiff * (inside + plane_parts(pack[f, 0])[0]))
        fac = stiff * inv
        mul_1, fac_1, fac_2 = edge[side, 17], edge[side, 18], edge[side, 19]
        for c in range(3):
            seed = edge[side, 2 + c]
            w_n = pack[f, 2 + c] * there
            w_0 = seed * fac
            beside_n, own_n = plane_parts(w_n)
            beside_0, own_0 = plane_parts(w_0)
            v_n = w_n + pack[f, 0] * there * (own_n + pack[f, 5 + c] + beside_0)
            v_0 = w_0 + stiff * fac * (own_0 + edge[side, 5 + c] + beside_n)
            v_1 = edge[side, 8 + c] + mul_1 * beside_0
            beside_n = plane_parts(v_n)[0]
            beside_0, own_0 = plane_parts(v_0)
            beside_1, own_1 = plane_parts(v_1)
            rows = [
                seed * inv + fac * (own_0 + beside_1 + beside_n),
                edge[side, 11 + c] + fac_1 * (own_1 + beside_0),
                edge[side, 14 + c] + fac_2 * beside_1,
            ]
            for k, row in enumerate(rows):
                ends[b, c, k if side == 0 else 2 * ENDS - 1 - k] = row
            start = 0 if side == 0 else len_ref[b] - ENDS
            copy = pltpu.make_async_copy(
                ends.at[b, c, pl.ds(side * ENDS, ENDS)],
                adj_out.at[b, c, pl.ds(start, ENDS)],
                sems.at[f, c],
            )
            copy.start()
            copies.append(copy)

    eight = 8
    line = lax.broadcasted_iota(jnp.int32, (LX, 4 * eight), 0).astype(F32)
    lane = lax.broadcasted_iota(jnp.int32, (LX, 4 * eight), 1)
    for b in range(slots):
        hat_z = hat_along_z(cz_ref[b : b + 1, :], nz)
        rows = [ends[b, c].reshape(2 * ENDS * ny, nz) for c in range(3)]
        done = dot(thrice(jnp.concatenate(rows, axis=1), 1, True), hat_z, 1)
        for k in range(eight):
            rows = done[k * ny : (k + 1) * ny] if k < 2 * ENDS else jnp.zeros((ny, 128), F32)
            zdone[k * pitch : k * pitch + ny] = rows
        coord = jnp.full((LX, 4 * eight), -4.0, F32)
        for k in range(2 * ENDS):
            at = k if k < ENDS else len_ref[b] - 2 * ENDS + k
            coord = jnp.where(lane % eight == k, cx_ref[b, at], coord)
        hat = jnp.maximum(0.0, 1.0 - jnp.abs(line - coord))
        high, low = split(hat)
        hat_x = jnp.where(lane < 2 * eight, high.astype(F32), low.astype(F32)).astype(BF16)
        for y in range(0, ny, 2):
            part = [zdone[pl.ds(y + k, eight, stride=pitch), :] for k in range(2)]
            high, low = split(jnp.concatenate(part, axis=1))
            high, low = high.astype(F32), low.astype(F32)
            stack = jnp.concatenate([high, low, high, jnp.zeros_like(high)], axis=0)
            done = dot(hat_x, stack.astype(BF16))
            for k in range(2):
                xdone[b, pl.ds(y + k, LX, stride=pitch), :] = done[:, 128 * k : 128 * (k + 1)]

    for copy in copies:
        copy.wait()


def close_kernel(fast, per, part_0, part_1, xdone, cy_ref, keep_ref, send_ref):
    slots, ny = cy_ref.shape
    pitch = ny + 1
    depth = per * slots * ny
    row = lax.broadcasted_iota(jnp.int32, (LY * per, depth), 0).astype(F32)
    lane = lax.broadcasted_iota(jnp.int32, (LY * per, depth), 1).astype(F32)
    which = jnp.floor((row + 0.5) * (1.0 / per))
    inside = row - which * per
    owner = jnp.floor((lane + 0.5) * (1.0 / (slots * ny)))
    coord = jnp.concatenate([cy_ref[b : b + 1, :] for b in range(slots)] * per, axis=1)
    hat_y = jnp.maximum(0.0, 1.0 - jnp.abs(which - coord))
    hat_y = thrice(jnp.where(inside == owner, hat_y, 0.0), 1, False)
    third_rows = LY // 4 * per
    pieces = keep_ref.shape[3]
    size = 3 * third_rows // 8
    tail = lax.broadcasted_iota(jnp.int32, (third_rows, 128), 1) >= 3 * LZ
    even = place_of(fast)[0] == 0
    for pair in range(LX // per // 2):
        terms = []
        for number in (2 * pair, 2 * pair + 1):
            rows = []
            for line in range(number * per, (number + 1) * per):
                at = slice(line * pitch, line * pitch + ny)
                rows += [part_0[at] + xdone[0, at], part_1[at] + xdone[1, at]]
            terms.append(jnp.concatenate(rows, axis=0))
        both = dot(hat_y, thrice(jnp.concatenate(terms, axis=1), 0, True))
        for k in range(2):
            done = both[:, 128 * k : 128 * (k + 1)]
            tops = done[3 * third_rows :]
            dense = []
            for q in range(3):
                moved = pltpu.roll(tops, 3 * LZ - q * LZ, 1)
                dense.append(jnp.where(tail, moved, done[q * third_rows : (q + 1) * third_rows]))
            dense = jnp.concatenate(dense, axis=0)
            number = 2 * pair + k
            d, t = number // pieces, number % pieces
            for g in range(4):
                first = dense[g * size : (g + 1) * size]
                second = dense[(g + 4) * size : (g + 5) * size]
                keep_ref[d, g // 2, g % 2, t] = jnp.where(even, first, second)
                send_ref[d, g // 2, g % 2, t] = jnp.where(even, second, first)


def core_kernel(keep_ref, got_ref, keep_y, send_y, keep_x, send_x):
    _, x, y, _ = place_of(True)
    keep_y[...] = keep_ref[:, y, 0] + got_ref[:, y, 0]
    send_y[...] = keep_ref[:, 1 - y, 0] + got_ref[:, 1 - y, 0]
    keep_x[...] = keep_ref[:, :, 1, x] + got_ref[:, :, 1, x]
    send_x[...] = keep_ref[:, :, 1, 1 - x] + got_ref[:, :, 1, 1 - x]


def plane_kernel(keep_y, got_y, keep_x, got_x, keep_0, send_0, keep_1, send_1):
    _, x, y, _ = place_of(True)
    keep_0[...] = keep_y[:, x] + got_y[:, x]
    send_0[...] = keep_y[:, 1 - x] + got_y[:, 1 - x]
    keep_1[...] = keep_x[:, y] + got_x[:, y]
    send_1[...] = keep_x[:, 1 - y] + got_x[:, 1 - y]


def line_kernel(keep_0, got_0, keep_1, got_1, *outs):
    z = place_of(True)[3]
    count = len(outs)
    for k, out in enumerate(outs):
        at = lax.rem(z + k, count)
        out[0] = keep_0[at] + got_0[at]
        out[1] = keep_1[at] + got_1[at]


def sum_kernel(scale, *refs):
    total = refs[0][...]
    for ref in refs[1:-1]:
        total = total + ref[...]
    refs[-1][...] = total * scale


def unpack_kernel(fast, per, own, got_c, got_x, got_xc, out_ref, lines):
    core, x, _, _ = place_of(fast)
    parts, count, size, _ = own.shape
    runs = size // per
    given = ((own, core, x), (got_c, 1 - core, x), (got_x, core, 1 - x), (got_xc, 1 - core, 1 - x))
    for ref, c, u in given:
        for p in range(parts):
            for t in range(count):
                for k in range(runs):
                    at = ((c * parts + p) * 2 + u) * runs + k
                    lines[at, t * per : (t + 1) * per] = ref[p, t, k * per : (k + 1) * per]
    rows = count * per
    lane = lax.broadcasted_iota(jnp.int32, (rows, 128), 1)
    front = lane < 2 * LZ
    even = (lane // LZ) % 2 == 0
    tiles = LY // 4
    groups = lines.shape[0] // 4
    per_c = groups // 3
    for g in range(groups):
        v = [lines[4 * g + k] for k in range(4)]
        a = [jnp.where(front, v[k], pltpu.roll(v[k + 2], 2 * LZ, 1)) for k in range(2)]
        b = [jnp.where(front, pltpu.roll(v[k], 2 * LZ, 1), v[k + 2]) for k in range(2)]
        turned = []
        for p, q in (a, b):
            turned.append(jnp.where(even, p, pltpu.roll(q, LZ, 1)))
            turned.append(jnp.where(even, pltpu.roll(p, 128 - LZ, 1), q))
        for c in range(3):
            at = (c * tiles + g) * 128
            out_ref[:, at : at + 128] = turned[c]
        at = (g // per_c * tiles + groups + g % per_c) * 128
        out_ref[:, at : at + 128] = turned[3]


def on_device(groups, devs, seed, stiff, lengths, low, up, coord_x, coord_y, coord_z):
    slots, nx, ny, nz = stiff.shape
    faces = 2 * slots
    chunk = PLANES * ny // devs
    rows = faces * chunk
    mine = LX // devs
    per = 4 if mine % 4 == 0 else mine
    pieces = mine // per
    size = 3 * LY // 4 // 8 * per
    fast = groups == 4 and devs % 2 == 0 and size % 8 == 0
    shape = lambda *dims: jax.ShapeDtypeStruct(dims, F32)

    packed = pl.pallas_call(
        functools.partial(pack_kernel, devs, slots, nx, ny, nz),
        out_shape=shape(devs, rows + 8, nz),
        in_specs=[HBM] * 5,
        out_specs=VMEM,
        scratch_shapes=[
            pltpu.SMEM((slots,), jnp.int32),
            pltpu.SMEM((slots, 3), jnp.int32),
            pltpu.SMEM((slots, 3), jnp.int32),
            pltpu.VMEM((faces, 3, nx - nx // 2 + 3, ny, nz), seed.dtype),
            pltpu.VMEM((faces, nx - nx // 2 + 3, ny, nz), F32),
            pltpu.VMEM((faces, PLANES * ny, nz), F32),
            pltpu.SemaphoreType.DMA((3, faces)),
        ],
        compiler_params=params(60),
        name="pack",
    )(lengths, low, up, seed, stiff)
    spread = lax.all_to_all(packed, "dev", 0, 0)
    ext = (nx + 2, ny + 16, nz)
    plain = pltpu.VMEM((nx, ny, nz), F32)

    def one_block(b, stiff, *given):
        return pl.pallas_call(
            functools.partial(block_kernel, b),
            out_shape=(
                shape(slots, 3, nx, ny, nz),
                shape(LX * (ny + 1), 128),
                shape(2 * EDGES * ny, 128),
                *([shape(nx, ny, nz)] if b == 0 else []),
            ),
            in_specs=[SMEM, ANY, ANY, VMEM, VMEM] + [HBM] * len(given),
            out_specs=(HBM, VMEM, VMEM, VMEM) if b == 0 else (HBM, VMEM, VMEM),
            scratch_shapes=[
                pltpu.VMEM(ext, F32),
                pltpu.VMEM((3, *ext), F32),
                pltpu.VMEM((3, *ext), F32),
                plain,
                plain,
                pltpu.VMEM((3, nx, ny, nz), F32),
                pltpu.VMEM((3, nx, ny, nz), seed.dtype),
                pltpu.VMEM((nx * (ny + 1), 128), F32),
                pltpu.SemaphoreType.DMA((4,)),
            ],
            input_output_aliases={5: 0} if given else {},
            compiler_params=params(12),
            cost_estimate=pl.CostEstimate(
                flops=3 * 10**9, bytes_accessed=10**7, transcendentals=0
            ),
            name=f"block_{b}",
        )(lengths, seed, stiff, coord_x, coord_z, *given)

    early, part_0, edge_0, stiff_1 = one_block(0, stiff)
    routed = pl.pallas_call(
        route_kernel,
        out_shape=shape(devs, rows, nz),
        in_specs=[VMEM],
        out_specs=VMEM,
        compiler_params=params(4),
        name="route",
    )(spread)
    early, routed = lax.optimization_barrier((early, routed))
    halos = lax.all_to_all(routed, "dev", 0, 0)
    early, part_1, edge_1 = one_block(1, stiff_1, early)

    half = shape(devs, 2, 2, pieces, size, 128)
    pitch = ny + 1
    adjoint, last = pl.pallas_call(
        ends_kernel,
        out_shape=(shape(slots, 3, nx, ny, nz), shape(slots, LX * pitch, 128)),
        in_specs=[SMEM] * 4 + [VMEM] * 4 + [HBM],
        out_specs=(HBM, VMEM),
        scratch_shapes=[
            pltpu.VMEM((faces, PLANES, ny, nz), F32),
            pltpu.VMEM((slots, 3, 2 * ENDS, ny, nz), F32),
            pltpu.VMEM((8 * pitch, 128), F32),
            pltpu.SemaphoreType.DMA((faces, 3)),
        ],
        input_output_aliases={8: 0},
        compiler_params=params(8),
        name="ends",
    )(lengths, low, up, coord_x, halos, edge_0, edge_1, coord_z, early)
    keep, send = pl.pallas_call(
        functools.partial(close_kernel, fast, per),
        out_shape=(half, half),
        in_specs=[VMEM] * 4,
        out_specs=(VMEM, VMEM),
        compiler_params=params(12),
        name="close",
    )(part_0, part_1, last, coord_y)

    scale = math.sqrt(LX * LY * LZ / (groups * devs * slots * nx * ny * nz))

    def small(kernel, outs, args, scratch=()):
        return pl.pallas_call(
            kernel,
            out_shape=outs,
            in_specs=[VMEM] * len(args),
            out_specs=jax.tree.map(lambda _: VMEM, outs),
            scratch_shapes=scratch,
            compiler_params=params(8),
        )(*args)

    piece = (2, pieces, size, 128)
    if fast:
        lines = devs // 2
        body = pieces * size

        def move(value, to):
            links = []
            for g in range(groups):
                for d in range(devs):
                    c2, x2, y2, z2 = to(g % 2, g // 2, d % 2, d // 2)
                    links.append((g * devs + d, (x2 * 2 + c2) * devs + z2 * 2 + y2))
            return lax.ppermute(value, ("group", "dev"), links)

        flip_c = lambda c, x, y, z: (1 - c, x, y, z)
        flip_x = lambda c, x, y, z: (c, 1 - x, y, z)
        flip_y = lambda c, x, y, z: (c, x, 1 - y, z)
        flip_xc = lambda c, x, y, z: (1 - c, 1 - x, y, z)
        got = move(send, flip_c)
        view = (lines, 2, 2, 2, body, 128)
        part = shape(lines, 2, body, 128)
        keep_y, send_y, keep_x, send_x = small(
            core_kernel, (part,) * 4, (keep.reshape(view), got.reshape(view))
        )
        got_y, got_x = move(send_y, flip_y), move(send_x, flip_x)
        part = shape(lines, body, 128)
        keep_0, send_0, keep_1, send_1 = small(
            plane_kernel, (part,) * 4, (keep_y, got_y, keep_x, got_x)
        )
        got_0, got_1 = move(send_0, flip_x), move(send_1, flip_y)
        part = shape(2, body, 128)
        sums = small(line_kernel, (part,) * lines, (keep_0, got_0, keep_1, got_1))
        terms = [sums[0]]
        for k in range(1, lines):
            terms.append(move(sums[k], lambda c, x, y, z, k=k: (c, x, y, (z + k) % lines)))
        own = small(functools.partial(sum_kernel, scale), part, tuple(terms))
        others = [move(own, to) for to in (flip_c, flip_x, flip_xc)]
        quarters = [v.reshape(piece) for v in (own, *others)]
    else:
        whole = jnp.stack([keep, send], axis=1).reshape(devs, -1, 128)
        owned = lax.psum_scatter(whole, "dev", scatter_dimension=0, tiled=True)
        owned = lax.psum(owned, "group") * scale
        owned = owned.reshape(2, 2, 2, pieces, size, 128)
        quarters = [owned[c, :, x] for x in range(2) for c in range(2)]
    lattice = small(
        functools.partial(unpack_kernel, fast, per),
        shape(mine, 3 * LY * LZ),
        tuple(quarters),
        [pltpu.VMEM((3 * LY // 4, mine, 128), F32)],
    )
    return adjoint, lattice


def solution(mesh):
    both = ("group", "dev")
    in_specs = (
        P(both, None, None, None, None),
        P(both, None, None, None),
        P(both),
        P(both, None),
        P(both, None),
        P(both, None),
        P(both, None),
        P(both, None),
    )
    out_specs = (P(both, None, None, None, None), P("dev", None))
    body = functools.partial(on_device, mesh.shape["group"], mesh.shape["dev"])
    return jax.shard_map(
        body, mesh=mesh, in_specs=in_specs, out_specs=out_specs, check_vma=False
    )
```

```python
import functools
import math

import jax
import jax.numpy as jnp
from jax import lax
from jax.experimental import pallas as pl
from jax.experimental.pallas import tpu as pltpu
from jax.sharding import PartitionSpec as P

LX = 96
LY = 64
LZ = 32
DOMINANCE = 1.25
PLANES = 8
STEP = 24
ENDS = 3
EDGES = 20

F32 = jnp.float32
BF16 = jnp.bfloat16
SMEM = pl.BlockSpec(memory_space=pltpu.SMEM)
VMEM = pl.BlockSpec(memory_space=pltpu.VMEM)
ANY = pl.BlockSpec(memory_space=pl.ANY)
HBM = pl.BlockSpec(memory_space=pltpu.HBM)


def place_of(fast):
    if not fast:
        return (jnp.int32(0),) * 4
    group, dev = lax.axis_index("group"), lax.axis_index("dev")
    halve = lambda v: lax.shift_right_logical(v, 1)
    return group & 1, halve(group), dev & 1, halve(dev)


def params(mib):
    return pltpu.CompilerParams(vmem_limit_bytes=mib * 1024 * 1024)


def neighbours(v, axis):
    extent = v.shape[axis]
    place = lax.broadcasted_iota(jnp.int32, v.shape, axis)
    up = jnp.where(place == 0, 0.0, pltpu.roll(v, 1, axis))
    down = jnp.where(place == extent - 1, 0.0, pltpu.roll(v, extent - 1, axis))
    return up + down


def plane_parts(v):
    along_z = neighbours(v, v.ndim - 1)
    first = v + 0.5 * along_z
    second = 0.5 * v + (1.0 / 3.0) * along_z
    beside = first + neighbours(second, v.ndim - 2)
    own = along_z + neighbours(first, v.ndim - 2)
    return beside, own


def padded_stencil(ref, lead, i, count):
    rows = ref.shape[-2] - 16
    planes = pl.ds(i, count + 2)
    v = ref[(*lead, planes, slice(8, 8 + rows))]
    t = ref[(*lead, planes, slice(7, 7 + rows))] + ref[(*lead, planes, slice(9, 9 + rows))]
    t_beside = t[:-2] + t[2:]
    near = t[1:-1] + (v[:-2] + v[2:])
    mixed = v[1:-1] + 0.5 * near + (1.0 / 3.0) * t_beside
    return v[1:-1], near + 0.5 * t_beside + neighbours(mixed, mixed.ndim - 1)


def split(v):
    high = v.astype(BF16)
    return high, (v - high.astype(F32)).astype(BF16)


def thrice(v, axis, data):
    high, low = split(v)
    parts = [high, low, high] if data else [high, high, low]
    return jnp.concatenate(parts, axis=axis)


def dot(a, b, contract_b=0):
    numbers = (((1,), (contract_b,)), ((), ()))
    return lax.dot_general(a, b, numbers, preferred_element_type=F32)


def pack_kernel(devs, slots, nx, ny, nz, len_in, low_in, up_in, seed_in, stiff_in, out_ref, *scratch):
    len_ref, low_ref, up_ref, seed_ref, stiff_ref, packet, sems = scratch
    rows = PLANES * ny
    chunk = rows // devs
    small = []
    for k, (src, dst) in enumerate(((len_in, len_ref), (low_in, low_ref), (up_in, up_ref))):
        small.append(pltpu.make_async_copy(src, dst, sems.at[0, k]))
        small[k].start()
    copies = {}

    base = nx // 2 - 3

    for s in range(slots):
        for side in range(2):
            f = 2 * s + side
            at = pl.ds(0, 3) if side == 0 else pl.ds(base, nx - base)
            to = pl.ds(0, 3 if side == 0 else nx - base)
            copies[f] = (
                pltpu.make_async_copy(stiff_in.at[s, at], stiff_ref.at[f, to], sems.at[1, f]),
                pltpu.make_async_copy(seed_in.at[s, :, at], seed_ref.at[f, :, to], sems.at[2, f]),
            )
            for copy in copies[f]:
                copy.start()
    small[0].wait()
    small[1].wait()
    small[2].wait()
    wanted = []
    for s in range(slots):
        for side, ref in ((0, low_ref), (1, up_ref)):
            number = jnp.maximum(ref[s, 0], 0) * (2 * slots) + ref[s, 1] * 2 + (1 - side)
            wanted.append(number.astype(F32))
    row = lax.broadcasted_iota(jnp.int32, (8, nz), 0)
    note = jnp.zeros((8, nz), F32)
    for f, number in enumerate(wanted):
        note = jnp.where(row == f, number, note)
    for f in (0, 2, 1, 3):
        side = f % 2
        for copy in copies[f]:
            copy.wait()
        at = [k if side == 0 else len_ref[f // 2] - 1 - k - base for k in range(3)]
        stiff = [stiff_ref[f, i] for i in at]
        parts = [plane_parts(v) for v in stiff]
        inner = parts[0][1] + parts[1][0]
        next_near = parts[1][1] + parts[0][0] + parts[2][0]
        scale = 1.0 / (DOMINANCE * next_near)
        planes = [stiff[0], inner]
        planes += [seed_ref[f, c, at[0]].astype(F32) for c in range(3)]
        for c in range(3):
            planes.append(plane_parts(seed_ref[f, c, at[1]].astype(F32) * scale)[0])
        for k, plane in enumerate(planes):
            packet[f, k * ny : (k + 1) * ny] = plane
    for j in range(devs):
        for f in range(2 * slots):
            out_ref[j, f * chunk : (f + 1) * chunk] = packet[f, j * chunk : (j + 1) * chunk]
        out_ref[j, 2 * slots * chunk :] = note


def route_kernel(in_ref, out_ref):
    devs, rows, _ = out_ref.shape
    faces = 4
    chunk = rows // faces
    for e in range(devs):
        for f in range(faces):
            cell = in_ref[e, rows + f : rows + f + 1, 0:1]
            number = cell[0, 0].astype(jnp.int32)
            source = lax.shift_right_logical(number, 2)
            start = (number & 3) * chunk
            if chunk % 8 == 0:
                start = pl.multiple_of(start, 8)
            out_ref[e, f * chunk : (f + 1) * chunk] = in_ref[source, pl.ds(start, chunk)]


def hat_along_z(coord, nz):
    row = lax.broadcasted_iota(jnp.int32, (128, 3 * nz), 0)
    lane = lax.broadcasted_iota(jnp.int32, (128, 3 * nz), 1)
    point = (row % LZ).astype(F32)
    hat = jnp.maximum(0.0, 1.0 - jnp.abs(point - jnp.concatenate([coord] * 3, axis=1)))
    return thrice(jnp.where((row // LZ) == (lane // nz), hat, 0.0), 1, False)


class Planes:
    def __init__(self, ref, start, ny):
        self.ref, self.start, self.ny = ref, start, ny

    def rows(self, key):
        return pl.ds(self.start + (key[0] * EDGES + key[1]) * self.ny, self.ny)

    def __getitem__(self, key):
        return self.ref[self.rows(key)]

    def __setitem__(self, key, value):
        self.ref[self.rows(key)] = value


def block_kernel(b, len_ref, seed_in, stiff_in, cx_ref, cz_ref, *refs):
    s_ext, w_ext, v_ext, fac_ref, mul_ref, adj, seeds, zdone, sems = refs[-9:]
    adj_out, part_ref, edge_out, *passed = refs[:4] if b == 0 else refs[1:4]
    nx, ny, nz = fac_ref.shape
    edge_ref = Planes(edge_out, 0, ny)
    last = 8 + ny
    length = len_ref[b]
    loads = (
        pltpu.make_async_copy(
            stiff_in.at[0] if b == 0 else stiff_in, s_ext.at[pl.ds(1, nx), pl.ds(8, ny)], sems.at[0]
        ),
        pltpu.make_async_copy(seed_in.at[b], seeds, sems.at[1]),
    )
    for copy in loads:
        copy.start()
    if b == 0:
        ahead = pltpu.make_async_copy(stiff_in.at[1], passed[0], sems.at[3])
        ahead.start()
    zeros = jnp.zeros((nx + 2, 8, nz), F32)
    plane = jnp.zeros((ny, nz), F32)
    for ref, lead in ((s_ext, ()), *((r, (c,)) for r in (w_ext, v_ext) for c in range(3))):
        ref[(*lead, slice(None), slice(0, 8))] = zeros
        ref[(*lead, slice(None), slice(last, last + 8))] = zeros
        for i in (0, nx + 1):
            ref[(*lead, i, slice(8, last))] = plane
    hat_z = hat_along_z(cz_ref[b : b + 1, :], nz)
    line = lax.broadcasted_iota(jnp.int32, (LX, 3 * nx), 0).astype(F32)
    lane = lax.broadcasted_iota(jnp.int32, (LX, 3 * nx), 1)
    x = lane % nx
    coord = jnp.concatenate([cx_ref[b : b + 1, :]] * 3, axis=1)
    hat = jnp.maximum(0.0, 1.0 - jnp.abs(line - coord))
    hat = jnp.where(jnp.logical_and(x >= ENDS, x < length - ENDS), hat, 0.0)
    high, low = split(hat)
    hat_x = jnp.where(lane < 2 * nx, high.astype(F32), low.astype(F32)).astype(BF16)
    for copy in loads:
        copy.wait()

    def clear(i, _):
        s_ext[i + 1, 8:last] = plane
        return 0

    lax.fori_loop(length, nx, clear, 0)

    def loop(body):
        def step(k, _):
            body(k * STEP)
            return 0

        lax.fori_loop(0, nx // STEP, step, 0)

    def first(i):
        stiff, near = padded_stencil(s_ext, (), i, STEP)
        active = i + lax.broadcasted_iota(jnp.int32, (STEP, ny, nz), 0) < length
        safe = jnp.where(active, DOMINANCE * stiff * near, 1.0)
        inv = jnp.where(active, 1.0 / safe, 0.0)
        fac = stiff * inv
        fac_ref[pl.ds(i, STEP)] = fac
        mul_ref[pl.ds(i, STEP)] = stiff * fac
        for c in range(3):
            seed = seeds[c, pl.ds(i, STEP)].astype(F32)
            w_ext[c, pl.ds(i + 1, STEP), 8:last] = seed * fac
            adj[c, pl.ds(i, STEP)] = seed * inv

    loop(first)

    at = [[k if side == 0 else length - 1 - k for k in range(4)] for side in range(2)]
    for f in range(2):
        for c in range(3):
            edge_ref[f, 11 + c] = adj[c, at[f][1]]
            edge_ref[f, 14 + c] = adj[c, at[f][2]]

    def second(i):
        mul = mul_ref[pl.ds(i, STEP)]
        for c in range(3):
            here, near = padded_stencil(w_ext, (c,), i, STEP)
            v_ext[c, pl.ds(i + 1, STEP), 8:last] = here + mul * near

    loop(second)

    def third(i):
        fac = fac_ref[pl.ds(i, STEP)]
        for c in range(3):
            _, near = padded_stencil(v_ext, (c,), i, STEP)
            adj[c, pl.ds(i, STEP)] += fac * near

    loop(third)
    store = pltpu.make_async_copy(adj, adj_out.at[b], sems.at[2])
    store.start()

    def parts(ref, *lead):
        v = ref[(*lead, slice(8, last))]
        t = ref[(*lead, slice(7, last - 1))] + ref[(*lead, slice(9, last + 1))]
        own = t + neighbours(v + 0.5 * t, 1)
        return v + 0.5 * t + neighbours(0.5 * v + (1.0 / 3.0) * t, 1), own

    for f in range(2):
        edge_ref[f, 0] = s_ext[at[f][0] + 1, 8:last]
        edge_ref[f, 1] = parts(s_ext, at[f][0] + 1)[1] + parts(s_ext, at[f][1] + 1)[0]
        mul_1, fac_1, fac_2 = mul_ref[at[f][1]], fac_ref[at[f][1]], fac_ref[at[f][2]]
        edge_ref[f, 17], edge_ref[f, 18], edge_ref[f, 19] = mul_1, fac_1, fac_2
        for c in range(3):
            edge_ref[f, 2 + c] = seeds[c, at[f][0]].astype(F32)
            beside, own = parts(w_ext, c, at[f][1] + 1)
            edge_ref[f, 5 + c] = beside
            own = own + parts(w_ext, c, at[f][2] + 1)[0]
            edge_ref[f, 8 + c] = w_ext[c, at[f][1] + 1, 8:last] + mul_1 * own
            beside, own = parts(v_ext, c, at[f][2] + 1)
            edge_ref[f, 11 + c] += fac_1 * beside
            edge_ref[f, 14 + c] += fac_2 * (own + parts(v_ext, c, at[f][3] + 1)[0])

    group = 16
    pitch = ny + 1
    for x in range(0, nx, group):
        rows = [adj[c, x : x + group].reshape(group * ny, nz) for c in range(3)]
        done = dot(thrice(jnp.concatenate(rows, axis=1), 1, True), hat_z, 1)
        for k in range(group):
            zdone[(x + k) * pitch : (x + k) * pitch + ny] = done[k * ny : (k + 1) * ny]
    for y in range(0, ny, 2):
        part = [zdone[pl.ds(y + k, nx, stride=pitch), :] for k in range(2)]
        done = dot(hat_x, thrice(jnp.concatenate(part, axis=1), 0, True))
        for k in range(2):
            part_ref[pl.ds(y + k, LX, stride=pitch), :] = done[:, 128 * k : 128 * (k + 1)]
    store.wait()
    if b == 0:
        ahead.wait()


def ends_kernel(
    len_ref,
    low_ref,
    up_ref,
    cx_ref,
    halo_ref,
    edge_0,
    edge_1,
    cz_ref,
    adj_in,
    adj_out,
    xdone,
    pack,
    ends,
    zdone,
    sems,
):
    del adj_in
    slots = 2
    faces = 2 * slots
    _, _, _, ny, nz = ends.shape
    pitch = ny + 1
    chunk = halo_ref.shape[1] // faces
    zero_plane = jnp.zeros((ny, nz), F32)

    for s in range(slots):
        for side, ref in ((0, low_ref), (1, up_ref)):
            f = 2 * s + side
            wall = ref[s, 0] < 0
            turned = ref[s, 2] == 1

            def place(reverse, f=f):
                for k in range(PLANES):
                    for r in range(ny):
                        at = k * ny + r
                        to = ny - 1 - r if reverse else r
                        j, o = at // chunk, at % chunk
                        pack[f, k, to : to + 1] = halo_ref[j, f * chunk + o : f * chunk + o + 1]

            @pl.when(wall)
            def _(f=f):
                for k in range(PLANES):
                    pack[f, k] = zero_plane

            @pl.when(jnp.logical_and(jnp.logical_not(wall), turned))
            def _(place=place):
                place(True)

            @pl.when(jnp.logical_and(jnp.logical_not(wall), jnp.logical_not(turned)))
            def _(place=place):
                place(False)

    copies = []
    for f in range(faces):
        b, side = f // 2, f % 2
        edge = Planes((edge_0, edge_1)[b], 0, ny)
        stiff, inside = edge[side, 0], edge[side, 1]
        beside = plane_parts(stiff)[0]
        there = 1.0 / (DOMINANCE * (pack[f, 1] + beside))
        inv = 1.0 / (DOMINANCE * stiff * (inside + plane_parts(pack[f, 0])[0]))
        fac = stiff * inv
        mul_1, fac_1, fac_2 = edge[side, 17], edge[side, 18], edge[side, 19]
        for c in range(3):
            seed = edge[side, 2 + c]
            w_n = pack[f, 2 + c] * there
            w_0 = seed * fac
            beside_n, own_n = plane_parts(w_n)
            beside_0, own_0 = plane_parts(w_0)
            v_n = w_n + pack[f, 0] * there * (own_n + pack[f, 5 + c] + beside_0)
            v_0 = w_0 + stiff * fac * (own_0 + edge[side, 5 + c] + beside_n)
            v_1 = edge[side, 8 + c] + mul_1 * beside_0
            beside_n = plane_parts(v_n)[0]
            beside_0, own_0 = plane_parts(v_0)
            beside_1, own_1 = plane_parts(v_1)
            rows = [
                seed * inv + fac * (own_0 + beside_1 + beside_n),
                edge[side, 11 + c] + fac_1 * (own_1 + beside_0),
                edge[side, 14 + c] + fac_2 * beside_1,
            ]
            for k, row in enumerate(rows):
                ends[b, c, k if side == 0 else 2 * ENDS - 1 - k] = row
            start = 0 if side == 0 else len_ref[b] - ENDS
            copy = pltpu.make_async_copy(
                ends.at[b, c, pl.ds(side * ENDS, ENDS)],
                adj_out.at[b, c, pl.ds(start, ENDS)],
                sems.at[f, c],
            )
            copy.start()
            copies.append(copy)

    eight = 8
    line = lax.broadcasted_iota(jnp.int32, (LX, 4 * eight), 0).astype(F32)
    lane = lax.broadcasted_iota(jnp.int32, (LX, 4 * eight), 1)
    for b in range(slots):
        hat_z = hat_along_z(cz_ref[b : b + 1, :], nz)
        rows = [ends[b, c].reshape(2 * ENDS * ny, nz) for c in range(3)]
        done = dot(thrice(jnp.concatenate(rows, axis=1), 1, True), hat_z, 1)
        for k in range(eight):
            rows = done[k * ny : (k + 1) * ny] if k < 2 * ENDS else jnp.zeros((ny, 128), F32)
            zdone[k * pitch : k * pitch + ny] = rows
        coord = jnp.full((LX, 4 * eight), -4.0, F32)
        for k in range(2 * ENDS):
            at = k if k < ENDS else len_ref[b] - 2 * ENDS + k
            coord = jnp.where(lane % eight == k, cx_ref[b, at], coord)
        hat = jnp.maximum(0.0, 1.0 - jnp.abs(line - coord))
        high, low = split(hat)
        hat_x = jnp.where(lane < 2 * eight, high.astype(F32), low.astype(F32)).astype(BF16)
        for y in range(0, ny, 2):
            part = [zdone[pl.ds(y + k, eight, stride=pitch), :] for k in range(2)]
            high, low = split(jnp.concatenate(part, axis=1))
            high, low = high.astype(F32), low.astype(F32)
            stack = jnp.concatenate([high, low, high, jnp.zeros_like(high)], axis=0)
            done = dot(hat_x, stack.astype(BF16))
            for k in range(2):
                xdone[b, pl.ds(y + k, LX, stride=pitch), :] = done[:, 128 * k : 128 * (k + 1)]

    for copy in copies:
        copy.wait()


def close_kernel(fast, per, part_0, part_1, xdone, cy_ref, edge_0, edge_1, keep_ref, send_ref):
    del edge_0, edge_1
    slots, ny = cy_ref.shape
    pitch = ny + 1
    depth = per * slots * ny
    row = lax.broadcasted_iota(jnp.int32, (LY * per, depth), 0).astype(F32)
    lane = lax.broadcasted_iota(jnp.int32, (LY * per, depth), 1).astype(F32)
    which = jnp.floor((row + 0.5) * (1.0 / per))
    inside = row - which * per
    owner = jnp.floor((lane + 0.5) * (1.0 / (slots * ny)))
    coord = jnp.concatenate([cy_ref[b : b + 1, :] for b in range(slots)] * per, axis=1)
    hat_y = jnp.maximum(0.0, 1.0 - jnp.abs(which - coord))
    hat_y = thrice(jnp.where(inside == owner, hat_y, 0.0), 1, False)
    third_rows = LY // 4 * per
    pieces = keep_ref.shape[3]
    size = 3 * third_rows // 8
    tail = lax.broadcasted_iota(jnp.int32, (third_rows, 128), 1) >= 3 * LZ
    even = place_of(fast)[0] == 0
    for pair in range(LX // per // 2):
        terms = []
        for number in (2 * pair, 2 * pair + 1):
            rows = []
            for line in range(number * per, (number + 1) * per):
                at = slice(line * pitch, line * pitch + ny)
                rows += [part_0[at] + xdone[0, at], part_1[at] + xdone[1, at]]
            terms.append(jnp.concatenate(rows, axis=0))
        both = dot(hat_y, thrice(jnp.concatenate(terms, axis=1), 0, True))
        for k in range(2):
            done = both[:, 128 * k : 128 * (k + 1)]
            tops = done[3 * third_rows :]
            dense = []
            for q in range(3):
                moved = pltpu.roll(tops, 3 * LZ - q * LZ, 1)
                dense.append(jnp.where(tail, moved, done[q * third_rows : (q + 1) * third_rows]))
            dense = jnp.concatenate(dense, axis=0)
            number = 2 * pair + k
            d, t = number // pieces, number % pieces
            for g in range(4):
                first = dense[g * size : (g + 1) * size]
                second = dense[(g + 4) * size : (g + 5) * size]
                keep_ref[d, g // 2, g % 2, t] = jnp.where(even, first, second)
                send_ref[d, g // 2, g % 2, t] = jnp.where(even, second, first)


def core_kernel(keep_ref, got_ref, keep_y, send_y, keep_x, send_x):
    _, x, y, _ = place_of(True)
    keep_y[...] = keep_ref[:, y, 0] + got_ref[:, y, 0]
    send_y[...] = keep_ref[:, 1 - y, 0] + got_ref[:, 1 - y, 0]
    keep_x[...] = keep_ref[:, :, 1, x] + got_ref[:, :, 1, x]
    send_x[...] = keep_ref[:, :, 1, 1 - x] + got_ref[:, :, 1, 1 - x]


def plane_kernel(keep_y, got_y, keep_x, got_x, keep_0, send_0, keep_1, send_1):
    _, x, y, _ = place_of(True)
    keep_0[...] = keep_y[:, x] + got_y[:, x]
    send_0[...] = keep_y[:, 1 - x] + got_y[:, 1 - x]
    keep_1[...] = keep_x[:, y] + got_x[:, y]
    send_1[...] = keep_x[:, 1 - y] + got_x[:, 1 - y]


def line_kernel(keep_0, got_0, keep_1, got_1, *outs):
    z = place_of(True)[3]
    count = len(outs)
    for k, out in enumerate(outs):
        at = lax.rem(z + k, count)
        out[0] = keep_0[at] + got_0[at]
        out[1] = keep_1[at] + got_1[at]


def sum_kernel(scale, *refs):
    total = refs[0][...]
    for ref in refs[1:-1]:
        total = total + ref[...]
    refs[-1][...] = total * scale


def unpack_kernel(fast, per, own, got_c, got_x, got_xc, out_ref, lines):
    core, x, _, _ = place_of(fast)
    parts, count, size, _ = own.shape
    runs = size // per
    given = ((own, core, x), (got_c, 1 - core, x), (got_x, core, 1 - x), (got_xc, 1 - core, 1 - x))
    for ref, c, u in given:
        for p in range(parts):
            for t in range(count):
                for k in range(runs):
                    at = ((c * parts + p) * 2 + u) * runs + k
                    lines[at, t * per : (t + 1) * per] = ref[p, t, k * per : (k + 1) * per]
    rows = count * per
    lane = lax.broadcasted_iota(jnp.int32, (rows, 128), 1)
    front = lane < 2 * LZ
    even = (lane // LZ) % 2 == 0
    tiles = LY // 4
    groups = lines.shape[0] // 4
    per_c = groups // 3
    for g in range(groups):
        v = [lines[4 * g + k] for k in range(4)]
        a = [jnp.where(front, v[k], pltpu.roll(v[k + 2], 2 * LZ, 1)) for k in range(2)]
        b = [jnp.where(front, pltpu.roll(v[k], 2 * LZ, 1), v[k + 2]) for k in range(2)]
        turned = []
        for p, q in (a, b):
            turned.append(jnp.where(even, p, pltpu.roll(q, LZ, 1)))
            turned.append(jnp.where(even, pltpu.roll(p, 128 - LZ, 1), q))
        for c in range(3):
            at = (c * tiles + g) * 128
            out_ref[:, at : at + 128] = turned[c]
        at = (g // per_c * tiles + groups + g % per_c) * 128
        out_ref[:, at : at + 128] = turned[3]


def on_device(groups, devs, seed, stiff, lengths, low, up, coord_x, coord_y, coord_z):
    slots, nx, ny, nz = stiff.shape
    faces = 2 * slots
    chunk = PLANES * ny // devs
    rows = faces * chunk
    mine = LX // devs
    per = 4 if mine % 4 == 0 else mine
    pieces = mine // per
    size = 3 * LY // 4 // 8 * per
    fast = groups == 4 and devs % 2 == 0 and size % 8 == 0
    shape = lambda *dims: jax.ShapeDtypeStruct(dims, F32)

    packed = pl.pallas_call(
        functools.partial(pack_kernel, devs, slots, nx, ny, nz),
        out_shape=shape(devs, rows + 8, nz),
        in_specs=[HBM] * 5,
        out_specs=VMEM,
        scratch_shapes=[
            pltpu.SMEM((slots,), jnp.int32),
            pltpu.SMEM((slots, 3), jnp.int32),
            pltpu.SMEM((slots, 3), jnp.int32),
            pltpu.VMEM((faces, 3, nx - nx // 2 + 3, ny, nz), seed.dtype),
            pltpu.VMEM((faces, nx - nx // 2 + 3, ny, nz), F32),
            pltpu.VMEM((faces, PLANES * ny, nz), F32),
            pltpu.SemaphoreType.DMA((3, faces)),
        ],
        compiler_params=params(60),
        name="pack",
    )(lengths, low, up, seed, stiff)
    spread = lax.all_to_all(packed, "dev", 0, 0)
    ext = (nx + 2, ny + 16, nz)
    plain = pltpu.VMEM((nx, ny, nz), F32)

    def one_block(b, stiff, *given):
        return pl.pallas_call(
            functools.partial(block_kernel, b),
            out_shape=(
                shape(slots, 3, nx, ny, nz),
                shape(LX * (ny + 1), 128),
                shape(2 * EDGES * ny, 128),
                *([shape(nx, ny, nz)] if b == 0 else []),
            ),
            in_specs=[SMEM, ANY, ANY, VMEM, VMEM] + [HBM] * len(given),
            out_specs=(HBM, VMEM, VMEM, VMEM) if b == 0 else (HBM, VMEM, VMEM),
            scratch_shapes=[
                pltpu.VMEM(ext, F32),
                pltpu.VMEM((3, *ext), F32),
                pltpu.VMEM((3, *ext), F32),
                plain,
                plain,
                pltpu.VMEM((3, nx, ny, nz), F32),
                pltpu.VMEM((3, nx, ny, nz), seed.dtype),
                pltpu.VMEM((nx * (ny + 1), 128), F32),
                pltpu.SemaphoreType.DMA((4,)),
            ],
            input_output_aliases={5: 0} if given else {},
            compiler_params=params(12),
            cost_estimate=pl.CostEstimate(
                flops=3 * 10**9, bytes_accessed=10**7, transcendentals=0
            ),
            name=f"block_{b}",
        )(lengths, seed, stiff, coord_x, coord_z, *given)

    early, part_0, edge_0, stiff_1 = one_block(0, stiff)
    routed = pl.pallas_call(
        route_kernel,
        out_shape=shape(devs, rows, nz),
        in_specs=[VMEM],
        out_specs=VMEM,
        compiler_params=params(4),
        name="route",
    )(spread)
    early, routed = lax.optimization_barrier((early, routed))
    halos = lax.all_to_all(routed, "dev", 0, 0)
    early, part_1, edge_1 = one_block(1, stiff_1, early)

    half = shape(devs, 2, 2, pieces, size, 128)
    pitch = ny + 1
    adjoint, last = pl.pallas_call(
        ends_kernel,
        out_shape=(shape(slots, 3, nx, ny, nz), shape(slots, LX * pitch, 128)),
        in_specs=[SMEM] * 4 + [VMEM] * 4 + [HBM],
        out_specs=(HBM, VMEM),
        scratch_shapes=[
            pltpu.VMEM((faces, PLANES, ny, nz), F32),
            pltpu.VMEM((slots, 3, 2 * ENDS, ny, nz), F32),
            pltpu.VMEM((8 * pitch, 128), F32),
            pltpu.SemaphoreType.DMA((faces, 3)),
        ],
        input_output_aliases={8: 0},
        compiler_params=params(8),
        name="ends",
    )(lengths, low, up, coord_x, halos, edge_0, edge_1, coord_z, early)
    keep, send = pl.pallas_call(
        functools.partial(close_kernel, fast, per),
        out_shape=(half, half),
        in_specs=[VMEM] * 4 + [ANY] * 2,
        out_specs=(VMEM, VMEM),
        compiler_params=params(12),
        name="close",
    )(part_0, part_1, last, coord_y, edge_0, edge_1)

    scale = math.sqrt(LX * LY * LZ / (groups * devs * slots * nx * ny * nz))

    def small(kernel, outs, args, scratch=()):
        return pl.pallas_call(
            kernel,
            out_shape=outs,
            in_specs=[VMEM] * len(args),
            out_specs=jax.tree.map(lambda _: VMEM, outs),
            scratch_shapes=scratch,
            compiler_params=params(8),
        )(*args)

    piece = (2, pieces, size, 128)
    if fast:
        lines = devs // 2
        body = pieces * size

        def move(value, to):
            links = []
            for g in range(groups):
                for d in range(devs):
                    c2, x2, y2, z2 = to(g % 2, g // 2, d % 2, d // 2)
                    links.append((g * devs + d, (x2 * 2 + c2) * devs + z2 * 2 + y2))
            return lax.ppermute(value, ("group", "dev"), links)

        flip_c = lambda c, x, y, z: (1 - c, x, y, z)
        flip_x = lambda c, x, y, z: (c, 1 - x, y, z)
        flip_y = lambda c, x, y, z: (c, x, 1 - y, z)
        flip_xc = lambda c, x, y, z: (1 - c, 1 - x, y, z)
        got = move(send, flip_c)
        view = (lines, 2, 2, 2, body, 128)
        part = shape(lines, 2, body, 128)
        keep_y, send_y, keep_x, send_x = small(
            core_kernel, (part,) * 4, (keep.reshape(view), got.reshape(view))
        )
        got_y, got_x = move(send_y, flip_y), move(send_x, flip_x)
        part = shape(lines, body, 128)
        keep_0, send_0, keep_1, send_1 = small(
            plane_kernel, (part,) * 4, (keep_y, got_y, keep_x, got_x)
        )
        got_0, got_1 = move(send_0, flip_x), move(send_1, flip_y)
        part = shape(2, body, 128)
        sums = small(line_kernel, (part,) * lines, (keep_0, got_0, keep_1, got_1))
        terms = [sums[0]]
        for k in range(1, lines):
            terms.append(move(sums[k], lambda c, x, y, z, k=k: (c, x, y, (z + k) % lines)))
        own = small(functools.partial(sum_kernel, scale), part, tuple(terms))
        others = [move(own, to) for to in (flip_c, flip_x, flip_xc)]
        quarters = [v.reshape(piece) for v in (own, *others)]
    else:
        whole = jnp.stack([keep, send], axis=1).reshape(devs, -1, 128)
        owned = lax.psum_scatter(whole, "dev", scatter_dimension=0, tiled=True)
        owned = lax.psum(owned, "group") * scale
        owned = owned.reshape(2, 2, 2, pieces, size, 128)
        quarters = [owned[c, :, x] for x in range(2) for c in range(2)]
    lattice = small(
        functools.partial(unpack_kernel, fast, per),
        shape(mine, 3 * LY * LZ),
        tuple(quarters),
        [pltpu.VMEM((3 * LY // 4, mine, 128), F32)],
    )
    return adjoint, lattice


def solution(mesh):
    both = ("group", "dev")
    in_specs = (
        P(both, None, None, None, None),
        P(both, None, None, None),
        P(both),
        P(both, None),
        P(both, None),
        P(both, None),
        P(both, None),
        P(both, None),
    )
    out_specs = (P(both, None, None, None, None), P("dev", None))
    body = functools.partial(on_device, mesh.shape["group"], mesh.shape["dev"])
    return jax.shard_map(
        body, mesh=mesh, in_specs=in_specs, out_specs=out_specs, check_vma=False
    )
```
